128 devices in a mesh: ctx: 16 (over z, x), tp: 8 (over y, core).
Axes of the slice: x: 4, y: 4, z: 4, core: 2. Of those that a mesh axis runs over, the one named last changes fastest.
Arguments:
- projected: bfloat16 [3, 8192, 8192], P(None, 'ctx', 'tp'), may hold values from -6 to 6
- short_filter: float32 [3, 3, 8192], P(None, None, 'tp'), may hold values from -3.5 to 3.5
- long_filter: bfloat16 [128, 8192], P(None, 'tp'), may hold values from -0.5 to 0.5
- skip_gain: float32 [8192], P('tp'), may hold values from -3 to 3
- out_weight: bfloat16 [8192, 8192], P('tp', 'ctx'), may hold values from -0.0625 to 0.0625
- out_grad: bfloat16 [8192, 8192], P('ctx'), may hold values from -6 to 6
- left_source: int32 [16], replicated, may hold values from -1 to 15, as said below
Outputs:
- mixed: bfloat16 [8192, 8192], P(('ctx', 'tp'))
- grad_projected: bfloat16 [3, 8192, 8192], P(None, 'ctx', 'tp')
- grad_long: float32 [128, 8192], P(None, 'tp')
- grad_short: float32 [3, 3, 8192], P(None, None, 'tp')
The draws below stay inside these ranges and needn't reach their ends.
Inputs may be any that keep to these rules, and one draw needn't show every extreme that they name: left_source[b] is -1 where block b begins a contig, else another block; no block is named by two blocks, and following left_source from any block ends at -1 without repeating a block.
All inputs are finite; a program needn't handle non-finite values.
Results may differ from the reference program's by a relative error of at most 0.015.
Values may be sent and summed in bfloat16 or wider, within the bound.
No kernel may reach another device: no remote copies, remote signals or barrier semaphores. Data moves between devices by JAX's collectives and lax.ppermute only.
A program may use at most 128 MiB of HBM per device.

```python
import math
import jax
import jax.numpy as jnp
from jax import lax

D = 8192
FILT = 128
SHORT = 3
TOK_DEV = 512
TOKENS = 8192
N_CTX = 16
N_TP = 8


def draw_left_source(key, part):
    perm_key, link_key = jax.random.split(jax.random.fold_in(key, 7))
    positions = jnp.arange(N_CTX, dtype=jnp.int32)
    placed = jax.random.permutation(perm_key, N_CTX).astype(jnp.int32)
    logical = jnp.zeros((N_CTX,), jnp.int32).at[placed].set(positions)
    last_place = logical[N_CTX - 1]
    swapped = placed.at[N_CTX - 1].set(placed[N_CTX - 2]).at[N_CTX - 2].set(placed[N_CTX - 1])
    placed = jnp.where(last_place == N_CTX - 1, swapped, placed)
    logical = jnp.zeros((N_CTX,), jnp.int32).at[placed].set(positions)
    forced = logical[N_CTX - 1] + 1
    linked = (jax.random.randint(link_key, (N_CTX,), 0, 3) > 0) | (positions == forced)
    linked = linked & (positions > 0)
    previous = jnp.roll(placed, 1)
    values = jnp.where(linked, previous, -1).astype(jnp.int32)
    return jnp.zeros((N_CTX,), jnp.int32).at[placed].set(values)


def steps_of(stream_key, extent, cuts, least, top_value):
    gain, own = 1.0, jax.random.fold_in(stream_key, 6)
    for dim, shards_of in cuts:
        heights = jnp.exp(jax.random.uniform(jax.random.fold_in(own, dim), (shards_of,), jnp.float32, least / len(cuts), top_value / len(cuts)))
        gain = gain * jnp.repeat(heights, extent[dim] // shards_of).reshape([-1 if axis == dim else 1 for axis in range(len(extent))])
    return gain


def normal_values(key, shape, deviation, reach, cuts=(), kind=jnp.bfloat16):
    entries = jax.random.normal(key, shape, jnp.float32) * deviation
    if len(cuts) > 0:
        entries = steps_of(key, shape, cuts, -0.22, 0.18) * entries
    return jnp.clip(entries, min=-reach, max=reach).astype(kind)


def setup_inputs(seed: int = 0) -> dict:
    streams_of = jax.random.split(jax.random.key(seed), 8)
    return {
        "projected": normal_values(streams_of[0], (3, TOKENS, D), 1.0, 6.0, ((1, 16), (2, 8))),
        "short_filter": normal_values(streams_of[1], (3, SHORT, D), SHORT ** -0.5, 3.5, ((2, 8),), jnp.float32),
        "long_filter": normal_values(streams_of[2], (FILT, D), FILT ** -0.5, 0.5, ((1, 8),)),
        "skip_gain": normal_values(streams_of[3], (D,), 0.5, 3.0, ((0, 8),), jnp.float32),
        "out_weight": normal_values(streams_of[4], (D, D), D ** -0.5, 0.0625, ((0, 8), (1, 16))),
        "out_grad": normal_values(streams_of[5], (TOKENS, D), 1.0, 6.0, ((0, 16),)),
        "left_source": draw_left_source(jax.random.fold_in(streams_of[7], 71), 0),
    }


def extend_left(values, edge_rows, source, has_left):
    tail = jnp.take(values[..., values.shape[-2] - edge_rows:, :], source, axis=-3)
    tail = jnp.where(has_left[:, None, None], tail, jnp.zeros_like(tail))
    return jnp.concatenate([tail, values], axis=-2)

def extend_right(values, edge_rows, reader, has_right):
    head = jnp.take(values[..., :edge_rows, :], reader, axis=-3)
    head = jnp.where(has_right[:, None, None], head, jnp.zeros_like(head))
    return jnp.concatenate([values, head], axis=-2)

def toeplitz_ref(filt_taps, block_rows):
    lag_index = jnp.arange(block_rows)[:, None] + FILT - jnp.arange(block_rows + FILT)[None, :]
    inside = (lag_index >= 0) & (lag_index < FILT)
    picked = jnp.take(filt_taps, jnp.clip(lag_index, 0, FILT - 1), axis=0)
    return jnp.where(inside[:, :, None], picked, jnp.zeros_like(picked))

def windows_ref(extended, block_rows):
    shape = extended.shape
    block_count = (shape[1] - FILT) // block_rows
    blocks = extended.reshape(shape[0], shape[1] // block_rows, block_rows, shape[2])
    pieces = [blocks[:, offset:offset + block_count] for offset in range(FILT // block_rows + 1)]
    return jnp.concatenate(pieces, axis=2)

def causal_ref(extended, filt_taps):
    block_rows = FILT // 2
    toeplitz = toeplitz_ref(filt_taps, block_rows)
    windows = windows_ref(extended, block_rows)
    result = jnp.einsum('ijc,brjc->bric', toeplitz, windows, precision=lax.Precision.HIGHEST)
    return result.reshape(extended.shape[0], -1, extended.shape[2])

def lag_ref(grad_conv, extended):
    block_rows = FILT // 2
    windows = windows_ref(extended, block_rows)
    shape = grad_conv.shape
    blocks = grad_conv.reshape(shape[0], shape[1] // block_rows, block_rows, shape[2])
    product = jnp.einsum('bric,brjc->ijc', blocks, windows, precision=lax.Precision.HIGHEST)
    lag_index = jnp.arange(block_rows)[:, None] + FILT - jnp.arange(FILT)[None, :]
    picked = product[jnp.arange(block_rows)[:, None], lag_index]
    return lax.optimization_barrier(jnp.sum(picked, axis=0))

def reference(projected, short_filter, long_filter, skip_gain, out_weight, out_grad, left_source):
    block_total = left_source.shape[0]
    positions = jnp.arange(block_total, dtype=jnp.int32)
    has_left = left_source >= 0
    source = jnp.maximum(left_source, 0).astype(jnp.int32)
    is_reader = left_source[None, :] == positions[:, None]
    has_right = jnp.any(is_reader, axis=1)
    reader = lax.optimization_barrier(jnp.sum(jnp.where(is_reader, positions[None, :], 0), axis=1)).astype(jnp.int32)
    channels = D // N_TP
    edge_rows = SHORT - 1
    grad_scale = 1.0 / math.sqrt(TOKENS)

    def one_group(out_accum, group_index):
        first_chan = group_index * channels
        streams = lax.dynamic_slice_in_dim(projected, first_chan, channels, 2)
        streams = streams.reshape(3, block_total, TOK_DEV, channels).astype(jnp.float32)
        tap_weights = lax.dynamic_slice_in_dim(short_filter, first_chan, channels, 2)
        filt_taps = lax.dynamic_slice_in_dim(long_filter, first_chan, channels, 1).astype(jnp.float32)
        skip_row = lax.dynamic_slice_in_dim(skip_gain, first_chan, channels, 0)
        weight_rows = lax.dynamic_slice_in_dim(out_weight, first_chan, channels, 0)
        streams_ext = extend_left(streams, edge_rows, source, has_left)
        act = jnp.zeros((3, block_total, TOK_DEV, channels), jnp.float32)
        for shift in range(SHORT):
            act = act + tap_weights[:, shift][:, None, None, :] * streams_ext[:, :, edge_rows - shift:edge_rows - shift + TOK_DEV]
        mixin = (act[1] * act[2]).astype(jnp.bfloat16)
        mixin_wide = mixin.astype(jnp.float32)
        mixin_ext = extend_left(mixin_wide, FILT, source, has_left)
        conv = causal_ref(mixin_ext, filt_taps) + skip_row * mixin_wide
        gated = (act[0] * conv).astype(jnp.bfloat16)
        partial_out = jnp.dot(gated.reshape(TOKENS, channels), weight_rows, preferred_element_type=jnp.float32)
        out_accum = out_accum + partial_out
        back_grad = jnp.dot(out_grad, weight_rows.T, preferred_element_type=jnp.float32)
        back_grad = back_grad.reshape(block_total, TOK_DEV, channels)
        grad_conv = (back_grad * act[0]).astype(jnp.bfloat16)
        grad_gate = back_grad * conv
        grad_wide = grad_conv.astype(jnp.float32)
        grad_ext = extend_right(grad_wide, FILT, reader, has_right)
        grad_mixin = jnp.flip(causal_ref(jnp.flip(grad_ext, 1), filt_taps), 1) + skip_row * grad_wide
        grad_act = jnp.stack([grad_gate, grad_mixin * act[2], grad_mixin * act[1]])
        grad_act_ext = extend_right(grad_act, edge_rows, reader, has_right)
        grad_streams = jnp.zeros((3, block_total, TOK_DEV, channels), jnp.float32)
        for shift in range(SHORT):
            grad_streams = grad_streams + tap_weights[:, shift][:, None, None, :] * grad_act_ext[:, :, shift:shift + TOK_DEV]
        short_terms = jnp.stack([lax.optimization_barrier(jnp.sum(grad_act * streams_ext[:, :, edge_rows - shift:edge_rows - shift + TOK_DEV], axis=(1, 2))) for shift in range(SHORT)], axis=1)
        long_terms = lag_ref(grad_wide, mixin_ext)
        grad_streams = grad_streams.reshape(3, TOKENS, channels).astype(jnp.bfloat16)
        return (out_accum, (grad_streams, long_terms * grad_scale, short_terms * grad_scale))
    out_accum, outputs = lax.scan(one_group, jnp.zeros((TOKENS, D), jnp.float32), jnp.arange(N_TP, dtype=jnp.int32))
    grad_streams, long_terms, short_terms = outputs
    grad_projected = jnp.transpose(grad_streams, (1, 2, 0, 3)).reshape(3, TOKENS, D)
    grad_long = jnp.transpose(long_terms, (1, 0, 2)).reshape(FILT, D)
    grad_short = jnp.transpose(short_terms, (1, 2, 0, 3)).reshape(3, SHORT, D)
    return (out_accum.astype(jnp.bfloat16), grad_projected, grad_long, grad_short)
```

```python
import math

import jax
import jax.numpy as jnp
import numpy as np
from jax import lax
from jax.experimental import pallas as pl
from jax.experimental.pallas import tpu as pltpu
from jax.sharding import PartitionSpec as P


f32, bf16 = jnp.float32, jnp.bfloat16
BLK = 128
SIDE = 4
PAD = 8


def split_hi_lo(matrix):
    hi = matrix.astype(np.float32).astype(bf16)
    lo = (matrix - hi.astype(np.float64)).astype(np.float32).astype(bf16)
    return hi, lo


def angles(times):
    freqs = np.concatenate([np.arange(0, BLK, 2), np.arange(1, BLK, 2)]) + 0.5
    return 2.0 * np.pi * freqs[:, None] * times[None, :] / (2 * BLK)


def forward_matrix():
    th = angles(np.arange(BLK, dtype=np.float64))
    hi, lo = split_hi_lo(np.concatenate([np.cos(th), -np.sin(th)], 0))
    return np.concatenate([hi, lo], 1)


def inverse_matrix(start):
    th = angles(np.arange(start, start + BLK, dtype=np.float64)).T / 1.0
    hi, lo = split_hi_lo(np.concatenate([np.cos(th), -np.sin(th)], 1) / BLK)
    return np.concatenate([hi, lo], 0)


def spectrum(fwd, rows):
    return jnp.dot(fwd, jnp.concatenate([rows, rows], 0), preferred_element_type=f32)


def delay(v):
    h = BLK // 2
    re, im = v[:BLK], v[BLK:]
    return jnp.concatenate([im[:h], -im[h:], -re[:h], re[h:]], 0)


def product(a, b):
    ar, ai, br, bi = a[:BLK], a[BLK:], b[:BLK], b[BLK:]
    return jnp.concatenate([ar * br - ai * bi, ar * bi + ai * br], 0)


def product_conj(a, b):
    ar, ai, br, bi = a[:BLK], a[BLK:], b[:BLK], b[BLK:]
    return jnp.concatenate([ar * br + ai * bi, ai * br - ar * bi], 0)


def invert(inv, y):
    hi = y.astype(bf16)
    lo = (y - hi.astype(f32)).astype(bf16)
    both = jnp.dot(inv, hi, preferred_element_type=f32)
    return both[:BLK] + both[BLK:] + jnp.dot(inv[:BLK], lo, preferred_element_type=f32)


def forward_kernel(order, proj, halo, sf, lf, skip, fwd, inv, gated, conv, act, mspec, fspec, ext):
    rows = proj.shape[1]
    fmat, imat = fwd[...], inv[...]
    for m in range(3):
        ext[PAD : PAD + rows] = proj[m].astype(f32)
        edge = halo[BLK : BLK + PAD].astype(f32)
        ext[PAD - 2 : PAD] = edge[2 * m : 2 * m + 2]
        total = sf[m, 0:1] * ext[PAD : PAD + rows]
        for s in (1, 2):
            total = total + sf[m, s : s + 1] * ext[PAD - s : PAD - s + rows]
        act[m] = total
    filt = spectrum(fmat, lf[...])
    fspec[...] = filt
    before = spectrum(fmat, halo[:BLK])
    for b in range(rows // BLK):
        span = slice(b * BLK, (b + 1) * BLK)
        mixin = (act[1, span] * act[2, span]).astype(bf16)
        here = spectrum(fmat, mixin)
        window = before + delay(here)
        before = here
        mspec[b] = window
        out = invert(imat, product(filt, window)) + skip[...] * mixin.astype(f32)
        conv[span] = out
        gate = (act[0, span] * out).astype(bf16)
        for half in range(2):
            start = pl.multiple_of(order[2 * b + half], BLK // 2)
            gated[pl.ds(start, BLK // 2)] = gate[half * (BLK // 2) : (half + 1) * (BLK // 2)]


def backward_kernel(bg, act0, act12, convh, mspec, fspec, skip, fwd, inv, invlag, pay, longt, gmix):
    rows = bg.shape[0]
    nb = rows // BLK
    fmat, imat = fwd[...], inv[...]
    filt = fspec[...]
    grads, specs = [], []
    lag = jnp.zeros(filt.shape, f32)
    for b in range(nb):
        span = slice(b * BLK, (b + 1) * BLK)
        g = (bg[span] * act0[0, span]).astype(bf16)
        if b == 0:
            pay[:BLK] = g
        here = spectrum(fmat, g)
        lag = lag + product_conj(here, mspec[b])
        grads.append(g)
        specs.append(here)
    longt[...] = invert(invlag[...], lag).astype(bf16)
    for b in range(nb):
        span = slice(b * BLK, (b + 1) * BLK)
        window = specs[b] + delay(specs[b + 1]) if b + 1 < nb else specs[b]
        gm = invert(imat, product_conj(window, filt)) + skip[...] * grads[b].astype(f32)
        gmix[span] = gm
        if b == 0:
            head = gm[:PAD]
            ga0 = bg[:PAD] * convh[...]
            ga1 = head * act12[1]
            ga2 = head * act12[0]
            pay[BLK:] = jnp.concatenate(
                [ga0[:2], ga1[:2], ga2[:2], jnp.zeros((2, gm.shape[1]), f32)], 0
            ).astype(bf16)


def finish_body(bg, conv, gmix, act, proj, sf, extra, gp, ext):
    rows = bg.shape[0]
    sums = []
    for m in range(3):
        if m == 0:
            ga = bg[...] * conv[...]
        else:
            ga = gmix[...] * act[2 - m]
        ext[:rows] = ga
        ext[rows : rows + PAD] = extra[m]
        x = proj[m].astype(f32)
        total = sf[m, 0:1] * ga
        sums.append(jnp.sum(x * ga, axis=0, keepdims=True))
        for s in (1, 2):
            moved = ext[s : s + rows]
            total = total + sf[m, s : s + 1] * moved
            sums.append(jnp.sum(x * moved, axis=0, keepdims=True))
        gp[m] = total.astype(bf16)
    return jnp.concatenate(sums + [jnp.zeros((7, bg.shape[1]), f32)], 0)


def top_kernel(bg, conv, gmix, act, bgn, convn, gmixn, actn, proj, sf, gp, short, ext):
    extra = [bgn[...] * convn[...], gmixn[...] * actn[1], gmixn[...] * actn[0]]
    short[...] = finish_body(bg, conv, gmix, act, proj, sf, extra, gp, ext)


def bottom_kernel(
    bg, conv, gmix, act, halo, proj, sf, fspec, fwd, inv, short_in, gp_in, gp, short, ext, gfull
):
    del gp_in
    rows = bg.shape[0]
    late = delay(spectrum(fwd[...], halo[:BLK]))
    gfull[...] = gmix[...]
    gfull[rows - BLK :] = gfull[rows - BLK :] + invert(inv[...], product_conj(late, fspec[...]))
    edge = halo[BLK : BLK + PAD].astype(f32)
    zeros = jnp.zeros((PAD - 2, edge.shape[1]), f32)
    extra = [jnp.concatenate([edge[2 * m : 2 * m + 2], zeros], 0) for m in range(3)]
    short[...] = short_in[...] + finish_body(bg, conv, gfull, act, proj, sf, extra, gp, ext)


def pieces_kernel(counts, first, cols, *refs):
    del cols
    nw = len(counts)
    weights = refs[:nw]
    if first:
        gated, og, mine, other, acc = refs[nw:]
    else:
        gated, og, acc_in, mine, other, acc = refs[nw:]
    step = pl.program_id(0)

    @pl.when(step == 0)
    def _():
        acc[...] = jnp.zeros_like(acc) if first else acc_in[...]

    begin = 0
    for ref, count in zip(weights, counts):

        @pl.when((step >= begin) & (step < begin + count))
        def _(ref=ref):
            w = ref[...]
            half = gated.shape[0] // 2
            out = jnp.dot(gated[...], w, preferred_element_type=f32).astype(bf16)
            mine[...] = out[:half]
            other[...] = out[half:]
            acc[...] += lax.dot_general(
                og[...], w, (((1,), (1,)), ((), ())), preferred_element_type=f32
            )

        begin += count


def multiply_pieces(weights, cols, gated, out_grad, acc):
    rows, chans = gated.shape
    width = weights[0].shape[1]
    counts = tuple(w.shape[0] // chans for w in weights)
    total = sum(counts)
    first = acc is None
    in_specs, begin = [], 0
    for count in counts:
        in_specs.append(
            pl.BlockSpec(
                (chans, width),
                lambda i, c, begin=begin, count=count: (jnp.clip(i - begin, 0, count - 1), 0),
            )
        )
        begin += count
    in_specs += [
        pl.BlockSpec((rows, chans), lambda i, c: (0, 0), pipeline_mode=pl.Buffered(1)),
        pl.BlockSpec((rows, width), lambda i, c: (0, c[i])),
    ]
    whole = pl.BlockSpec((rows, chans), lambda i, c: (0, 0), pipeline_mode=pl.Buffered(1))
    operands = [*weights, gated, out_grad]
    if not first:
        in_specs.append(whole)
        operands.append(acc)
    half_shape = jax.ShapeDtypeStruct((rows // 2, total * width), bf16)
    half_spec = pl.BlockSpec((rows // 2, width), lambda i, c: (0, i))

    def kernel(cols_ref, *refs):
        pieces_kernel(counts, first, cols_ref, *refs)

    return pl.pallas_call(
        kernel,
        grid_spec=pltpu.PrefetchScalarGridSpec(
            num_scalar_prefetch=1,
            grid=(total,),
            in_specs=in_specs,
            out_specs=[half_spec, half_spec, whole],
        ),
        out_shape=[half_shape, half_shape, jax.ShapeDtypeStruct((rows, chans), f32)],
        cost_estimate=pl.CostEstimate(
            flops=4 * rows * chans * width * total,
            bytes_accessed=total * (2 * chans * width + 4 * rows * width) + 10 * rows * chans,
            transcendentals=0,
        ),
        name="pieces",
    )(cols, *operands)


def collect_kernel(counts, cols, *refs):
    mixed = refs[-1]
    width = mixed.shape[1] // sum(counts)
    begin = 0
    for i, count in enumerate(counts):
        parts = refs[4 * i : 4 * i + 4]
        for p in range(count):
            lanes = slice(p * width, (p + 1) * width)
            vals = [r[:, lanes].astype(f32) for r in parts]
            start = pl.multiple_of(cols[begin + p] * width, width)
            mixed[:, pl.ds(start, width)] = (
                (vals[0] + vals[1]) + (vals[2] + vals[3])
            ).astype(bf16)
        begin += count


def on_device(projected, short_filter, long_filter, skip_gain, out_weight, out_grad, left_source):
    rows, chans = projected.shape[1:]
    width = out_weight.shape[1] // 2
    ctx_count, tp_count = lax.axis_size("ctx"), lax.axis_size("tp")
    me, tp = lax.axis_index("ctx"), lax.axis_index("tp")
    zi, xi, yi, ci = me // SIDE, me % SIDE, tp // 2, tp % 2

    def ring(value, axis, step):
        if axis == "x":
            pairs = [(d, d // SIDE * SIDE + (d + step) % SIDE) for d in range(ctx_count)]
        else:
            pairs = [(d, (d + SIDE * step) % ctx_count) for d in range(ctx_count)]
        return lax.ppermute(value, "ctx", pairs)

    def swap(value, axis, k):
        shift = {"x": k, "z": k * SIDE, "core": k, "y": 2 * k}[axis]
        name = "ctx" if axis in "xz" else "tp"
        return lax.ppermute(value, name, [(d, d ^ shift) for d in range(lax.axis_size(name))])

    def gather(piece, first, second):
        h = piece.shape[0] // 2
        p, q = ring(piece, first, 1), ring(piece, first, -1)
        t, b = ring(p[:h], first, 1), ring(q[h:], first, -1)
        line = jnp.concatenate([piece, p, q, t, b], 0)
        lp, lq = ring(line, second, 1), ring(line, second, -1)
        far_t, far_b = ring(lp[: 4 * h], second, 1), ring(lq[4 * h :], second, -1)
        return line, lp, lq, far_t, far_b

    def blocks(half, near, far_steps):
        out = []
        for f in far_steps:
            for n in near:
                z, x = (f, n) if half == 0 else (n, f)
                out.append(2 * ((zi + z) % SIDE * SIDE + (xi + x) % SIDE) + half)
        return out

    order4 = (0, -1, 1, 2)
    cols1 = jnp.stack(blocks(0, order4, (0,)) + blocks(1, order4, (0,)))
    cols2 = jnp.stack(blocks(0, order4, (-1, 1)) + blocks(1, order4, (-1, 1)))
    cols3 = jnp.stack(blocks(0, order4, (2,)) + blocks(1, order4, (2,)))

    line_a, lp_a, lq_a, ft_a, fb_a = gather(out_weight[:, :width], "x", "z")
    line_b, lp_b, lq_b, ft_b, fb_b = gather(out_weight[:, width:], "z", "x")

    positions = jnp.arange(ctx_count, dtype=jnp.int32)
    matches = left_source[None, :] == positions[:, None]
    readers = jnp.where(
        jnp.any(matches, 1), jnp.sum(jnp.where(matches, positions[None, :], 0), 1), -1
    )

    def pick(options, index):
        low = jnp.where(index == 1, options[1], options[0])
        high = jnp.where(index == 3, options[3], options[2])
        return jnp.where(index >= 2, high, low)

    def at(table, index):
        return lax.dynamic_index_in_dim(table, index, 0, keepdims=False)

    def along_x(payloads):
        return [payloads[0]] + [swap(payloads[k], "x", k) for k in (1, 2, 3)]

    def chosen(got, table):
        out = []
        for k in range(SIDE):
            source = jnp.maximum(at(table, (zi ^ k) * SIDE + xi), 0)
            out.append(pick(got, (source % SIDE) ^ xi))
        return out

    def landed(got, table):
        source = at(table, me)
        value = pick(got, (jnp.maximum(source, 0) // SIDE) ^ zi)
        return jnp.where(source >= 0, value, jnp.zeros_like(value))

    near = projected[1:, rows - BLK - PAD :].astype(f32)
    tail = jnp.zeros((2, BLK, chans), f32)
    for s in range(3):
        tail = tail + short_filter[1:, s][:, None] * near[:, PAD - s : PAD - s + BLK]
    raw = projected[:, rows - 2 :].reshape(6, chans)
    sent = jnp.concatenate(
        [(tail[0] * tail[1]).astype(bf16), raw, jnp.zeros((2, chans), bf16)], 0
    )
    got = along_x([sent] * SIDE)
    to_z = chosen(got, left_source)
    left = landed([to_z[0]] + [swap(to_z[k], "z", k) for k in (1, 2, 3)], left_source)

    fwd = jnp.asarray(forward_matrix())
    inv_late, inv_now, inv_lag = (jnp.asarray(inverse_matrix(s)) for s in (BLK, 0, -BLK))
    skip_row = skip_gain[None, :]
    share = rows // tp_count
    order = jnp.stack(
        [
            (((t % 2) ^ ci) * SIDE + ((t // 2) ^ yi)) * share
            for t in range(tp_count)
        ]
    ).astype(jnp.int32)
    tile = 256
    grid = (chans // tile,)
    nb = rows // BLK

    def col(*lead):
        return pl.BlockSpec((*lead, tile), lambda i, *_: (*([0] * len(lead)), i))

    const = pl.BlockSpec((2 * BLK, 2 * BLK), lambda i, *_: (0, 0))
    gated, conv, act, mspec, fspec = pl.pallas_call(
        forward_kernel,
        grid_spec=pltpu.PrefetchScalarGridSpec(
            num_scalar_prefetch=1,
            grid=grid,
            in_specs=[
                col(3, rows), col(BLK + PAD), col(3, 3), col(BLK), col(1), const, const,
            ],
            out_specs=[col(rows), col(rows), col(3, rows), col(nb, 2 * BLK), col(2 * BLK)],
            scratch_shapes=[pltpu.VMEM((rows + PAD, tile), f32)],
        ),
        out_shape=[
            jax.ShapeDtypeStruct((rows, chans), bf16),
            jax.ShapeDtypeStruct((rows, chans), f32),
            jax.ShapeDtypeStruct((3, rows, chans), f32),
            jax.ShapeDtypeStruct((nb, 2 * BLK, chans), f32),
            jax.ShapeDtypeStruct((2 * BLK, chans), f32),
        ],
        cost_estimate=pl.CostEstimate(
            flops=12_000_000_000, bytes_accessed=20 << 20, transcendentals=0
        ),
        name="forward",
    )(order, projected, left, short_filter, long_filter, skip_row, fwd, inv_late)

    def scatter(mine, other):
        total = (mine.astype(f32) + swap(other, "core", 1).astype(f32)).astype(bf16)
        parts = [total[k * share : (k + 1) * share] for k in range(SIDE)]
        return [parts[0]] + [swap(parts[k], "y", k) for k in (1, 2, 3)]

    mine1, other1, acc = multiply_pieces([line_a, line_b], cols1, gated, out_grad, None)
    out1 = scatter(mine1, other1)
    mine2, other2, acc = multiply_pieces([lp_a, lq_a, lp_b, lq_b], cols2, gated, out_grad, acc)
    out2 = scatter(mine2, other2)
    mine3, other3, acc = multiply_pieces([ft_a, fb_a, ft_b, fb_b], cols3, gated, out_grad, acc)
    out3 = scatter(mine3, other3)

    pay, long_terms, gmix = pl.pallas_call(
        backward_kernel,
        grid=grid,
        in_specs=[
            col(rows),
            pl.BlockSpec((1, rows, tile), lambda i: (0, 0, i)),
            col(2, PAD),
            col(PAD),
            col(nb, 2 * BLK),
            col(2 * BLK),
            col(1),
            const,
            const,
            const,
        ],
        out_specs=[col(BLK + PAD), col(BLK), col(rows)],
        out_shape=[
            jax.ShapeDtypeStruct((BLK + PAD, chans), bf16),
            jax.ShapeDtypeStruct((BLK, chans), bf16),
            jax.ShapeDtypeStruct((rows, chans), f32),
        ],
        cost_estimate=pl.CostEstimate(
            flops=12_000_000_000, bytes_accessed=12 << 20, transcendentals=0
        ),
        name="backward",
    )(acc, act, act[1:, :PAD], conv, mspec, fspec, skip_row, fwd, inv_now, inv_lag)

    quarter = BLK // SIDE

    def part(k):
        return lax.dynamic_slice_in_dim(long_terms, (xi ^ k) * quarter, quarter, 0)

    got = along_x([jnp.concatenate([pay, part(k)], 0) for k in range(SIDE)])
    sums = [g[BLK + PAD :].astype(f32) for g in got]
    quarter_sum = ((sums[0] + sums[1]) + (sums[2] + sums[3])).astype(bf16)
    to_z = chosen([g[: BLK + PAD] for g in got], readers)
    got = [jnp.concatenate([v, quarter_sum], 0) for v in to_z]
    got = [got[0]] + [swap(got[k], "z", k) for k in (1, 2, 3)]
    right = landed([g[: BLK + PAD] for g in got], readers)
    sums = [g[BLK + PAD :].astype(f32) for g in got]
    my_quarter = (sums[0] + sums[1]) + (sums[2] + sums[3])

    half = rows // 2

    def rows_at(block, n, *lead):
        return pl.BlockSpec(
            (*lead, n, tile), lambda i: (*([0] * len(lead)), block, i)
        )

    act12_spec = lambda block, n: pl.BlockSpec(
        (pl.Element(2), pl.Element(n), pl.Element(tile)), lambda i: (1, block * n, i * tile)
    )
    gp_shape = jax.ShapeDtypeStruct((3, rows, chans), bf16)
    short_shape = jax.ShapeDtypeStruct((16, chans), f32)
    gp, short = pl.pallas_call(
        top_kernel,
        grid=grid,
        in_specs=[
            rows_at(0, half), rows_at(0, half), rows_at(0, half), act12_spec(0, half),
            rows_at(half // PAD, PAD), rows_at(half // PAD, PAD), rows_at(half // PAD, PAD),
            act12_spec(half // PAD, PAD), rows_at(0, half, 3), col(3, 3),
        ],
        out_specs=[rows_at(0, half, 3), col(16)],
        out_shape=[gp_shape, short_shape],
        scratch_shapes=[pltpu.VMEM((half + PAD, tile), f32)],
        cost_estimate=pl.CostEstimate(
            flops=200_000_000, bytes_accessed=8 << 20, transcendentals=0
        ),
        name="top",
    )(acc, conv, gmix, act, acc, conv, gmix, act, projected, short_filter)
    gp, short = pl.pallas_call(
        bottom_kernel,
        grid=grid,
        in_specs=[
            rows_at(1, half), rows_at(1, half), rows_at(1, half), act12_spec(1, half),
            col(BLK + PAD), rows_at(1, half, 3), col(3, 3), col(2 * BLK), const, const, col(16),
            pl.BlockSpec(memory_space=pl.ANY),
        ],
        out_specs=[rows_at(1, half, 3), col(16)],
        out_shape=[gp_shape, short_shape],
        scratch_shapes=[pltpu.VMEM((half + PAD, tile), f32), pltpu.VMEM((half, tile), f32)],
        input_output_aliases={11: 0},
        cost_estimate=pl.CostEstimate(
            flops=2_000_000_000, bytes_accessed=9 << 20, transcendentals=0
        ),
        name="bottom",
    )(acc, conv, gmix, act, right, projected, short_filter, fspec, fwd, inv_now, short, gp)

    message = jnp.concatenate([my_quarter, short], 0)
    got = along_x([message] * SIDE)
    quarters = [g[:quarter] for g in got]
    long_total = jnp.concatenate([pick(quarters, xi ^ q) for q in range(SIDE)], 0)
    sums = [g[quarter:] for g in got]
    sums = (sums[0] + sums[1]) + (sums[2] + sums[3])
    sums = [sums] + [swap(sums, "z", k) for k in (1, 2, 3)]
    short_total = ((sums[0] + sums[1]) + (sums[2] + sums[3]))[:9].reshape(3, 3, chans)

    counts = tuple(o[0].shape[1] // width for o in (out1, out2, out3))
    mixed = pl.pallas_call(
        lambda cols, *refs: collect_kernel(counts, cols, *refs),
        grid_spec=pltpu.PrefetchScalarGridSpec(
            num_scalar_prefetch=1,
            grid=(1,),
            in_specs=[
                pl.BlockSpec(o[0].shape, lambda i, c: (0, 0))
                for o in (out1, out2, out3)
                for _ in range(SIDE)
            ],
            out_specs=pl.BlockSpec((share, 2 * width * ctx_count), lambda i, c: (0, 0)),
        ),
        out_shape=jax.ShapeDtypeStruct((share, 2 * width * ctx_count), bf16),
        cost_estimate=pl.CostEstimate(flops=10_000_000, bytes_accessed=5 << 20, transcendentals=0),
        name="collect",
    )(jnp.concatenate([cols1, cols2, cols3]), *out1, *out2, *out3)

    scale = 1.0 / math.sqrt(rows * ctx_count)
    return mixed, gp, long_total * scale, short_total * scale


def solution(mesh):
    placed = (
        P(None, "ctx", "tp"),
        P(None, None, "tp"),
        P(None, "tp"),
        P("tp"),
        P("tp", "ctx"),
        P("ctx", None),
        P(),
    )
    return jax.shard_map(
        on_device,
        mesh=mesh,
        in_specs=placed,
        out_specs=(
            P(("ctx", "tp"), None),
            P(None, "ctx", "tp"),
            P(None, "tp"),
            P(None, None, "tp"),
        ),
        check_vma=False,
    )
```

```python
import math

import jax
import jax.numpy as jnp
import numpy as np
from jax import lax
from jax.experimental import pallas as pl
from jax.experimental.pallas import tpu as pltpu
from jax.sharding import PartitionSpec as P


f32, bf16 = jnp.float32, jnp.bfloat16
BLK = 128
SIDE = 4
PAD = 8


def split_hi_lo(matrix):
    hi = matrix.astype(np.float32).astype(bf16)
    lo = (matrix - hi.astype(np.float64)).astype(np.float32).astype(bf16)
    return hi, lo


def angles(times):
    freqs = np.concatenate([np.arange(0, BLK, 2), np.arange(1, BLK, 2)]) + 0.5
    return 2.0 * np.pi * freqs[:, None] * times[None, :] / (2 * BLK)


def forward_matrix():
    th = angles(np.arange(BLK, dtype=np.float64))
    hi, lo = split_hi_lo(np.concatenate([np.cos(th), -np.sin(th)], 0))
    return np.concatenate([hi, lo], 1)


def inverse_matrix(start):
    th = angles(np.arange(start, start + BLK, dtype=np.float64)).T / 1.0
    hi, lo = split_hi_lo(np.concatenate([np.cos(th), -np.sin(th)], 1) / BLK)
    return np.concatenate([hi, lo], 0)


def spectrum(fwd, rows):
    return jnp.dot(fwd, jnp.concatenate([rows, rows], 0), preferred_element_type=f32)


def delay(v):
    h = BLK // 2
    re, im = v[:BLK], v[BLK:]
    return jnp.concatenate([im[:h], -im[h:], -re[:h], re[h:]], 0)


def product(a, b):
    ar, ai, br, bi = a[:BLK], a[BLK:], b[:BLK], b[BLK:]
    return jnp.concatenate([ar * br - ai * bi, ar * bi + ai * br], 0)


def product_conj(a, b):
    ar, ai, br, bi = a[:BLK], a[BLK:], b[:BLK], b[BLK:]
    return jnp.concatenate([ar * br + ai * bi, ai * br - ar * bi], 0)


def invert(inv, y):
    hi = y.astype(bf16)
    lo = (y - hi.astype(f32)).astype(bf16)
    both = jnp.dot(inv, hi, preferred_element_type=f32)
    return both[:BLK] + both[BLK:] + jnp.dot(inv[:BLK], lo, preferred_element_type=f32)


def forward_kernel(order, proj, halo, sf, lf, skip, fwd, inv, gated, conv, act, mspec, fspec, ext):
    rows = proj.shape[1]
    fmat, imat = fwd[...], inv[...]
    for m in range(3):
        ext[PAD : PAD + rows] = proj[m].astype(f32)
        edge = halo[BLK : BLK + PAD].astype(f32)
        ext[PAD - 2 : PAD] = edge[2 * m : 2 * m + 2]
        total = sf[m, 0:1] * ext[PAD : PAD + rows]
        for s in (1, 2):
            total = total + sf[m, s : s + 1] * ext[PAD - s : PAD - s + rows]
        act[m] = total
    filt = spectrum(fmat, lf[...])
    fspec[...] = filt
    before = spectrum(fmat, halo[:BLK])
    for b in range(rows // BLK):
        span = slice(b * BLK, (b + 1) * BLK)
        mixin = (act[1, span] * act[2, span]).astype(bf16)
        here = spectrum(fmat, mixin)
        window = before + delay(here)
        before = here
        mspec[b] = window
        out = invert(imat, product(filt, window)) + skip[...] * mixin.astype(f32)
        conv[span] = out
        gate = (act[0, span] * out).astype(bf16)
        for half in range(2):
            start = pl.multiple_of(order[2 * b + half], BLK // 2)
            gated[pl.ds(start, BLK // 2)] = gate[half * (BLK // 2) : (half + 1) * (BLK // 2)]


def backward_kernel(place, acc, act0, act12, convh, mspec, fspec, skip, fwd, inv, invlag, *refs):
    og, refs = refs[: 2 * SIDE], refs[2 * SIDE :]
    weights, (bg, pay0, pay1, pay2, pay3, gmix, lagbuf) = refs[:6], refs[6:]
    rows = bg.shape[0]
    nb = rows // BLK
    fmat, imat = fwd[...], inv[...]
    filt = fspec[...]
    blocks = []
    for first, second, third in (weights[:3], weights[3:]):
        blocks += [first[0], first[1], second[...], third[...]]
    bg[...] = acc[...] + lax.dot_general(
        jnp.concatenate([o[...] for o in og], 1),
        jnp.concatenate(blocks, 1),
        (((1,), (1,)), ((), ())),
        preferred_element_type=f32,
    )
    grads, specs = [], []
    lag = jnp.zeros(filt.shape, f32)
    for b in range(nb):
        span = slice(b * BLK, (b + 1) * BLK)
        g = (bg[span] * act0[0, span]).astype(bf16)
        here = spectrum(fmat, g)
        lag = lag + product_conj(here, mspec[b])
        grads.append(g)
        specs.append(here)
    lagbuf[...] = invert(invlag[...], lag)
    for b in range(nb):
        span = slice(b * BLK, (b + 1) * BLK)
        window = specs[b] + delay(specs[b + 1]) if b + 1 < nb else specs[b]
        gm = invert(imat, product_conj(window, filt)) + skip[...] * grads[b].astype(f32)
        gmix[span] = gm
        if b == 0:
            head = gm[:PAD]
            ga0 = bg[:PAD] * convh[...]
            ga1 = head * act12[1]
            ga2 = head * act12[0]
            edge = jnp.concatenate(
                [ga0[:2], ga1[:2], ga2[:2], jnp.zeros((2, gm.shape[1]), f32)], 0
            ).astype(bf16)
    quarter = BLK // SIDE
    for k, pay in enumerate((pay0, pay1, pay2, pay3)):
        pay[:BLK] = grads[0]
        pay[BLK : BLK + PAD] = edge
        start = pl.multiple_of((place[0] ^ k) * quarter, quarter)
        pay[BLK + PAD :] = lagbuf[pl.ds(start, quarter)].astype(bf16)


def finish_body(bg, conv, gmix, act, proj, sf, extra, gp, ext):
    rows = bg.shape[0]
    sums = []
    for m in range(3):
        if m == 0:
            ga = bg[...] * conv[...]
        else:
            ga = gmix[...] * act[2 - m]
        ext[:rows] = ga
        ext[rows : rows + PAD] = extra[m]
        x = proj[m].astype(f32)
        total = sf[m, 0:1] * ga
        sums.append(jnp.sum(x * ga, axis=0, keepdims=True))
        for s in (1, 2):
            moved = ext[s : s + rows]
            total = total + sf[m, s : s + 1] * moved
            sums.append(jnp.sum(x * moved, axis=0, keepdims=True))
        gp[m] = total.astype(bf16)
    return jnp.concatenate(sums + [jnp.zeros((7, bg.shape[1]), f32)], 0)


def top_kernel(bg, conv, gmix, act, bgn, convn, gmixn, actn, proj, sf, gp, short, ext):
    extra = [bgn[...] * convn[...], gmixn[...] * actn[1], gmixn[...] * actn[0]]
    short[...] = finish_body(bg, conv, gmix, act, proj, sf, extra, gp, ext)


def bottom_kernel(
    bg, conv, gmix, act, halo, proj, sf, fspec, fwd, inv, short_in, gp_in, gp, short, ext, gfull
):
    del gp_in
    rows = bg.shape[0]
    late = delay(spectrum(fwd[...], halo[:BLK]))
    gfull[: rows - BLK] = gmix[: rows - BLK]
    gfull[rows - BLK :] = gmix[rows - BLK :] + invert(inv[...], product_conj(late, fspec[...]))
    edge = halo[BLK : BLK + PAD].astype(f32)
    zeros = jnp.zeros((PAD - 2, edge.shape[1]), f32)
    extra = [jnp.concatenate([edge[2 * m : 2 * m + 2], zeros], 0) for m in range(3)]
    short[...] = short_in[...] + finish_body(bg, conv, gfull, act, proj, sf, extra, gp, ext)


def pieces_kernel(layout, first, back, *refs):
    nw = sum(len(counts) for counts in layout)
    weights, refs = refs[:nw], refs[nw:]
    gated, refs = refs[0], refs[1:]
    if back:
        og, refs = refs[:SIDE], refs[SIDE:]
        if not first:
            acc_in, refs = refs[0], refs[1:]
        mine, other, acc, buf = refs
    else:
        mine, other, buf = refs
    step = pl.program_id(0)
    if back:

        @pl.when(step == 0)
        def _():
            acc[...] = jnp.zeros_like(acc) if first else acc_in[...]

    chans = gated.shape[1]
    half = gated.shape[0] // 2
    begin = 0
    for i, counts in enumerate(layout):
        part = weights[begin : begin + len(counts)]
        begin += len(counts)

        @pl.when(step == i)
        def _(part=part, counts=counts):
            at = 0
            for r, c in zip(part, counts):
                for n in range(c):
                    buf[:, at : at + r.shape[1]] = r[n * chans : (n + 1) * chans]
                    at += r.shape[1]

    out = jnp.dot(gated[...], buf[...], preferred_element_type=f32).astype(bf16)
    mine[...] = out[:half]
    other[...] = out[half:]
    if back:
        acc[...] += lax.dot_general(
            jnp.concatenate([o[...] for o in og], 1),
            buf[...],
            (((1,), (1,)), ((), ())),
            preferred_element_type=f32,
        )


def multiply_pieces(groups, cols, gated, out_grad, acc, back=True):
    rows, chans = gated.shape
    width = groups[0][0].shape[1]
    layout = [tuple(w.shape[0] // chans for w in group) for group in groups]
    steps = len(groups)
    first = acc is None
    one = pl.Buffered(1)
    weights = [w for group in groups for w in group]
    in_specs = [pl.BlockSpec(w.shape, lambda i, c: (0, 0), pipeline_mode=one) for w in weights]
    whole = pl.BlockSpec((rows, chans), lambda i, c: (0, 0), pipeline_mode=one)
    in_specs.append(whole)
    operands = [*weights, gated]
    if back:
        in_specs += [
            pl.BlockSpec((rows, width), lambda i, c, j=j: (0, c[SIDE * i + j])) for j in range(SIDE)
        ]
        operands += [out_grad] * SIDE
        if not first:
            in_specs.append(whole)
            operands.append(acc)
    half_shape = jax.ShapeDtypeStruct((rows // 2, steps * SIDE * width), bf16)
    half_spec = pl.BlockSpec((rows // 2, SIDE * width), lambda i, c: (0, i))

    def kernel(cols_ref, *refs):
        del cols_ref
        pieces_kernel(layout, first, back, *refs)

    return pl.pallas_call(
        kernel,
        grid_spec=pltpu.PrefetchScalarGridSpec(
            num_scalar_prefetch=1,
            grid=(steps,),
            in_specs=in_specs,
            out_specs=[half_spec, half_spec] + [whole] * back,
            scratch_shapes=[pltpu.VMEM((chans, SIDE * width), bf16)],
        ),
        out_shape=[half_shape, half_shape] + [jax.ShapeDtypeStruct((rows, chans), f32)] * back,
        cost_estimate=pl.CostEstimate(
            flops=(2 + 2 * back) * rows * chans * width * SIDE * steps,
            bytes_accessed=SIDE * steps * (2 * chans * width + 4 * rows * width) + 10 * rows * chans,
            transcendentals=0,
        ),
        name="pieces",
    )(cols, *operands)


def collect_kernel(counts, cols, *refs):
    mixed = refs[-1]
    width = mixed.shape[1] // sum(counts)
    begin = 0
    for i, count in enumerate(counts):
        parts = refs[4 * i : 4 * i + 4]

        @pl.loop(0, count)
        def _(p, parts=parts, begin=begin):
            lanes = pl.ds(pl.multiple_of(p * width, width), width)
            vals = [r[:, lanes].astype(f32) for r in parts]
            start = pl.multiple_of(cols[begin + p] * width, width)
            mixed[:, pl.ds(start, width)] = (
                (vals[0] + vals[1]) + (vals[2] + vals[3])
            ).astype(bf16)

        begin += count


def on_device(projected, short_filter, long_filter, skip_gain, out_weight, out_grad, left_source):
    rows, chans = projected.shape[1:]
    width = out_weight.shape[1] // 2
    ctx_count, tp_count = lax.axis_size("ctx"), lax.axis_size("tp")
    me, tp = lax.axis_index("ctx"), lax.axis_index("tp")
    zi, xi, yi, ci = me // SIDE, me % SIDE, tp // 2, tp % 2

    def ring(value, axis, step):
        if axis == "x":
            pairs = [(d, d // SIDE * SIDE + (d + step) % SIDE) for d in range(ctx_count)]
        else:
            pairs = [(d, (d + SIDE * step) % ctx_count) for d in range(ctx_count)]
        return lax.ppermute(value, "ctx", pairs)

    def swap(value, axis, k):
        shift = {"x": k, "z": k * SIDE, "core": k, "y": 2 * k}[axis]
        name = "ctx" if axis in "xz" else "tp"
        return lax.ppermute(value, name, [(d, d ^ shift) for d in range(lax.axis_size(name))])

    def gather(piece, first, second):
        h = piece.shape[0] // 2
        p, q = ring(piece, first, 1), ring(piece, first, -1)
        t, b = ring(p[:h], first, 1), ring(q[h:], first, -1)
        line = jnp.concatenate([piece, p, q], 0)
        lp, lq = ring(line, second, 1), ring(line, second, -1)
        far = jnp.concatenate([t, b], 0)
        fp, fq = ring(far, second, 1), ring(far, second, -1)
        ft, fb = ring(lp[: 4 * h], second, 1), ring(lq[4 * h :], second, -1)
        ff = ring(fq, second, -1)
        return [line, far], [[lp, fp], [lq, fq]], [ft, fb, ff]

    def blocks(half, near, far_steps):
        out = []
        for f in far_steps:
            for n in near:
                z, x = (f, n) if half == 0 else (n, f)
                out.append(2 * ((zi + z) % SIDE * SIDE + (xi + x) % SIDE) + half)
        return out

    order4 = (0, -1, 1, 2)
    cols1 = jnp.stack(blocks(0, order4, (0,)) + blocks(1, order4, (0,)))
    cols2 = jnp.stack(blocks(0, order4, (-1, 1)) + blocks(1, order4, (-1, 1)))
    cols3 = jnp.stack(blocks(0, order4, (2,)) + blocks(1, order4, (2,)))

    positions = jnp.arange(ctx_count, dtype=jnp.int32)
    matches = left_source[None, :] == positions[:, None]
    readers = jnp.where(
        jnp.any(matches, 1), jnp.sum(jnp.where(matches, positions[None, :], 0), 1), -1
    )

    def pick(options, index):
        low = jnp.where(index == 1, options[1], options[0])
        high = jnp.where(index == 3, options[3], options[2])
        return jnp.where(index >= 2, high, low)

    def at(table, index):
        return lax.dynamic_index_in_dim(table, index, 0, keepdims=False)

    def along_x(payloads):
        return [payloads[0]] + [swap(payloads[k], "x", k) for k in (1, 2, 3)]

    def along_z(payloads):
        return [payloads[0]] + [swap(payloads[k], "z", k) for k in (1, 2, 3)]

    def chosen(got, table):
        out = []
        for k in range(SIDE):
            source = jnp.maximum(at(table, (zi ^ k) * SIDE + xi), 0)
            out.append(pick(got, (source % SIDE) ^ xi))
        return out

    def landed(got, table):
        source = at(table, me)
        value = pick(got, (jnp.maximum(source, 0) // SIDE) ^ zi)
        return jnp.where(source >= 0, value, jnp.zeros_like(value))

    near = projected[1:, rows - BLK - PAD :].astype(f32)
    tail = jnp.zeros((2, BLK, chans), f32)
    for s in range(3):
        tail = tail + short_filter[1:, s][:, None] * near[:, PAD - s : PAD - s + BLK]
    raw = projected[:, rows - 2 :].reshape(6, chans)
    sent = jnp.concatenate(
        [(tail[0] * tail[1]).astype(bf16), raw, jnp.zeros((2, chans), bf16)], 0
    )
    got = along_x([sent] * SIDE)
    to_z = chosen(got, left_source)
    got = along_z(to_z)
    left = landed(got, left_source)

    wa, wb, _ = lax.optimization_barrier((out_weight[:, :width], out_weight[:, width:], sent))
    near_a, mid_a, far_a = gather(wa, "x", "z")
    near_b, mid_b, far_b = gather(wb, "z", "x")

    fwd = jnp.asarray(forward_matrix())
    inv_late, inv_now, inv_lag = (jnp.asarray(inverse_matrix(s)) for s in (BLK, 0, -BLK))
    skip_row = skip_gain[None, :]
    share = rows // tp_count
    order = jnp.stack(
        [
            (((t % 2) ^ ci) * SIDE + ((t // 2) ^ yi)) * share
            for t in range(tp_count)
        ]
    ).astype(jnp.int32)
    tile = 256
    grid = (chans // tile,)
    nb = rows // BLK

    def col(*lead):
        return pl.BlockSpec((*lead, tile), lambda i, *_: (*([0] * len(lead)), i))

    const = pl.BlockSpec((2 * BLK, 2 * BLK), lambda i, *_: (0, 0))
    forward = pl.pallas_call(
        forward_kernel,
        grid_spec=pltpu.PrefetchScalarGridSpec(
            num_scalar_prefetch=1,
            grid=grid,
            in_specs=[
                col(3, rows), col(BLK + PAD), col(3, 3), col(BLK), col(1), const, const,
            ],
            out_specs=[col(rows), col(rows), col(3, rows), col(nb, 2 * BLK), col(2 * BLK)],
            scratch_shapes=[pltpu.VMEM((rows + PAD, tile), f32)],
        ),
        out_shape=[
            jax.ShapeDtypeStruct((rows, chans), bf16),
            jax.ShapeDtypeStruct((rows, chans), f32),
            jax.ShapeDtypeStruct((3, rows, chans), f32),
            jax.ShapeDtypeStruct((nb, 2 * BLK, chans), f32),
            jax.ShapeDtypeStruct((2 * BLK, chans), f32),
        ],
        cost_estimate=pl.CostEstimate(
            flops=12_000_000_000, bytes_accessed=20 << 20, transcendentals=0
        ),
        name="forward",
    )
    gated, conv, act, mspec, fspec = forward(
        order, projected, left, short_filter, long_filter, skip_row, fwd, inv_late
    )

    def scatter(mine, other):
        got = swap(other, "core", 1)
        total = (mine.astype(f32) + got.astype(f32)).astype(bf16)
        parts = [total[k * share : (k + 1) * share] for k in range(SIDE)]
        return [parts[0]] + [swap(parts[k], "y", k) for k in (1, 2, 3)]

    mine1, other1, acc = multiply_pieces([near_a, near_b], cols1, gated, out_grad, None)
    out1 = scatter(mine1, other1)
    mine2, other2, acc = multiply_pieces(mid_a + mid_b, cols2, gated, out_grad, acc)
    out2 = scatter(mine2, other2)

    quarter = BLK // SIDE
    place = jnp.concatenate([jnp.reshape(xi, (1,)), cols3]).astype(jnp.int32)

    def third(w):
        count = w.shape[0] // chans
        if count == 1:
            return w, pl.BlockSpec((tile, width), lambda i, c: (i, 0))
        return w.reshape(count, chans, width), pl.BlockSpec(
            (count, tile, width), lambda i, c: (0, i, 0)
        )

    lasts, last_specs = zip(*[third(w) for w in far_a + far_b])
    pay_shape = jax.ShapeDtypeStruct((BLK + PAD + quarter, chans), bf16)
    pay_spec = col(BLK + PAD + quarter)
    backward = pl.pallas_call(
        backward_kernel,
        grid_spec=pltpu.PrefetchScalarGridSpec(
            num_scalar_prefetch=1,
            grid=grid,
            in_specs=[
                col(rows),
                pl.BlockSpec((1, rows, tile), lambda i, c: (0, 0, i)),
                pl.BlockSpec(
                    (pl.Element(2), pl.Element(PAD), pl.Element(tile)),
                    lambda i, c: (1, 0, i * tile),
                ),
                col(PAD),
                col(nb, 2 * BLK),
                col(2 * BLK),
                col(1),
                const,
                const,
                const,
                *[
                    pl.BlockSpec((rows, width), lambda i, c, j=j: (0, c[1 + j]))
                    for j in range(2 * SIDE)
                ],
                *last_specs,
            ],
            out_specs=[col(rows), pay_spec, pay_spec, pay_spec, pay_spec, col(rows)],
            scratch_shapes=[pltpu.VMEM((BLK, tile), f32)],
        ),
        out_shape=[
            jax.ShapeDtypeStruct((rows, chans), f32),
            pay_shape, pay_shape, pay_shape, pay_shape,
            jax.ShapeDtypeStruct((rows, chans), f32),
        ],
        cost_estimate=pl.CostEstimate(
            flops=8_000_000_000, bytes_accessed=20 << 20, transcendentals=0
        ),
        name="backward",
    )
    bg, pay0, pay1, pay2, pay3, gmix = backward(
        place, acc, act, act, conv, mspec, fspec, skip_row, fwd, inv_now, inv_lag,
        *[out_grad] * (2 * SIDE), *lasts,
    )

    got = along_x([pay0, pay1, pay2, pay3])
    sums = [g[BLK + PAD :].astype(f32) for g in got]
    quarter_sum = ((sums[0] + sums[1]) + (sums[2] + sums[3])).astype(bf16)
    to_z = chosen([g[: BLK + PAD] for g in got], readers)
    got = along_z([jnp.concatenate([v, quarter_sum], 0) for v in to_z])
    right = landed([g[: BLK + PAD] for g in got], readers)
    sums = [g[BLK + PAD :].astype(f32) for g in got]
    my_quarter = (sums[0] + sums[1]) + (sums[2] + sums[3])

    mine3, other3 = multiply_pieces([far_a, far_b], cols3, gated, None, None, back=False)
    out3 = scatter(mine3, other3)

    low = rows - BLK - PAD

    def rows_at(start, n, *lead):
        zeros = [0] * len(lead)
        dims = [pl.Element(d) for d in (*lead, n, tile)]
        return pl.BlockSpec(tuple(dims), lambda i: (*zeros, start, i * tile))

    def acts_at(start, n):
        return pl.BlockSpec(
            (pl.Element(2), pl.Element(n), pl.Element(tile)), lambda i: (1, start, i * tile)
        )

    gp_shape = jax.ShapeDtypeStruct((3, rows, chans), bf16)
    short_shape = jax.ShapeDtypeStruct((16, chans), f32)
    top = pl.pallas_call(
        top_kernel,
        grid=grid,
        in_specs=[
            rows_at(0, low), rows_at(0, low), rows_at(0, low), acts_at(0, low),
            rows_at(low, PAD), rows_at(low, PAD), rows_at(low, PAD), acts_at(low, PAD),
            rows_at(0, low, 3), col(3, 3),
        ],
        out_specs=[rows_at(0, low, 3), col(16)],
        out_shape=[gp_shape, short_shape],
        scratch_shapes=[pltpu.VMEM((low + PAD, tile), f32)],
        cost_estimate=pl.CostEstimate(
            flops=200_000_000, bytes_accessed=10 << 20, transcendentals=0
        ),
        name="top",
    )
    gp, short = top(bg, conv, gmix, act, bg, conv, gmix, act, projected, short_filter)
    rest = rows - low
    bottom = pl.pallas_call(
        bottom_kernel,
        grid=grid,
        in_specs=[
            rows_at(low, rest), rows_at(low, rest), rows_at(low, rest), acts_at(low, rest),
            col(BLK + PAD), rows_at(low, rest, 3), col(3, 3), col(2 * BLK), const, const, col(16),
            pl.BlockSpec(memory_space=pl.ANY),
        ],
        out_specs=[rows_at(low, rest, 3), col(16)],
        out_shape=[gp_shape, short_shape],
        scratch_shapes=[pltpu.VMEM((rest + PAD, tile), f32), pltpu.VMEM((rest, tile), f32)],
        input_output_aliases={11: 0},
        cost_estimate=pl.CostEstimate(
            flops=2_000_000_000, bytes_accessed=5 << 20, transcendentals=0
        ),
        name="bottom",
    )
    gp, short = bottom(
        bg, conv, gmix, act, right, projected, short_filter, fspec, fwd, inv_now, short, gp
    )

    got = along_x([my_quarter] * SIDE)
    long_total = jnp.concatenate([pick(got, xi ^ q) for q in range(SIDE)], 0)
    sums = along_x([short] * SIDE)
    sums = (sums[0] + sums[1]) + (sums[2] + sums[3])
    sums = along_z([sums] * SIDE)
    short_total = ((sums[0] + sums[1]) + (sums[2] + sums[3]))[:9].reshape(3, 3, chans)

    counts = tuple(o[0].shape[1] // width for o in (out1, out2, out3))
    mixed = pl.pallas_call(
        lambda cols, *refs: collect_kernel(counts, cols, *refs),
        grid_spec=pltpu.PrefetchScalarGridSpec(
            num_scalar_prefetch=1,
            grid=(1,),
            in_specs=[
                pl.BlockSpec(o[0].shape, lambda i, c: (0, 0))
                for o in (out1, out2, out3)
                for _ in range(SIDE)
            ],
            out_specs=pl.BlockSpec((share, 2 * width * ctx_count), lambda i, c: (0, 0)),
        ),
        out_shape=jax.ShapeDtypeStruct((share, 2 * width * ctx_count), bf16),
        cost_estimate=pl.CostEstimate(flops=10_000_000, bytes_accessed=5 << 20, transcendentals=0),
        name="collect",
    )(jnp.concatenate([cols1, cols2, cols3]), *out1, *out2, *out3)

    scale = 1.0 / math.sqrt(rows * ctx_count)
    return mixed, gp, long_total * scale, short_total * scale


def solution(mesh):
    placed = (
        P(None, "ctx", "tp"),
        P(None, None, "tp"),
        P(None, "tp"),
        P("tp"),
        P("tp", "ctx"),
        P("ctx", None),
        P(),
    )
    return jax.shard_map(
        on_device,
        mesh=mesh,
        in_specs=placed,
        out_specs=(
            P(("ctx", "tp"), None),
            P(None, "ctx", "tp"),
            P(None, "tp"),
            P(None, None, "tp"),
        ),
        check_vma=False,
    )
```

```python
import math

import jax
import jax.numpy as jnp
import numpy as np
from jax import lax
from jax.experimental import pallas as pl
from jax.experimental.pallas import tpu as pltpu
from jax.sharding import PartitionSpec as P


f32, bf16 = jnp.float32, jnp.bfloat16
BLK = 128
SIDE = 4
PAD = 8


def split_hi_lo(matrix):
    hi = matrix.astype(np.float32).astype(bf16)
    lo = (matrix - hi.astype(np.float64)).astype(np.float32).astype(bf16)
    return hi, lo


def angles(times):
    freqs = np.concatenate([np.arange(0, BLK, 2), np.arange(1, BLK, 2)]) + 0.5
    return 2.0 * np.pi * freqs[:, None] * times[None, :] / (2 * BLK)


def forward_matrix():
    th = angles(np.arange(BLK, dtype=np.float64))
    hi, lo = split_hi_lo(np.concatenate([np.cos(th), -np.sin(th)], 0))
    return np.concatenate([hi, lo], 1)


def inverse_matrix(start):
    th = angles(np.arange(start, start + BLK, dtype=np.float64)).T / 1.0
    hi, lo = split_hi_lo(np.concatenate([np.cos(th), -np.sin(th)], 1) / BLK)
    return np.concatenate([hi, lo], 0)


def spectrum(fwd, rows):
    return jnp.dot(fwd, jnp.concatenate([rows, rows], 0), preferred_element_type=f32)


def delay(v):
    h = BLK // 2
    re, im = v[:BLK], v[BLK:]
    return jnp.concatenate([im[:h], -im[h:], -re[:h], re[h:]], 0)


def product(a, b):
    ar, ai, br, bi = a[:BLK], a[BLK:], b[:BLK], b[BLK:]
    return jnp.concatenate([ar * br - ai * bi, ar * bi + ai * br], 0)


def product_conj(a, b):
    ar, ai, br, bi = a[:BLK], a[BLK:], b[:BLK], b[BLK:]
    return jnp.concatenate([ar * br + ai * bi, ai * br - ar * bi], 0)


def invert(inv, y):
    hi = y.astype(bf16)
    lo = (y - hi.astype(f32)).astype(bf16)
    both = jnp.dot(inv, hi, preferred_element_type=f32)
    return both[:BLK] + both[BLK:] + jnp.dot(inv[:BLK], lo, preferred_element_type=f32)


def forward_kernel(order, proj, halo, sf, lf, skip, fwd, inv, gated, conv, act, mspec, fspec, ext):
    rows = proj.shape[1]
    fmat, imat = fwd[...], inv[...]
    for m in range(3):
        ext[PAD : PAD + rows] = proj[m].astype(f32)
        edge = halo[BLK : BLK + PAD].astype(f32)
        ext[PAD - 2 : PAD] = edge[2 * m : 2 * m + 2]
        total = sf[m, 0:1] * ext[PAD : PAD + rows]
        for s in (1, 2):
            total = total + sf[m, s : s + 1] * ext[PAD - s : PAD - s + rows]
        act[m] = total
    filt = spectrum(fmat, lf[...])
    fspec[...] = filt
    nb, wide = rows // BLK, filt.shape[1]
    mixins = [
        (act[1, b * BLK : (b + 1) * BLK] * act[2, b * BLK : (b + 1) * BLK]).astype(bf16)
        for b in range(nb)
    ]
    spec = spectrum(fmat, jnp.concatenate([halo[:BLK]] + mixins, 1))
    window = spec[:, : nb * wide] + delay(spec[:, wide:])
    out = invert(imat, product(window, jnp.concatenate([filt] * nb, 1)))
    for b in range(nb):
        span = slice(b * BLK, (b + 1) * BLK)
        lanes = slice(b * wide, (b + 1) * wide)
        mspec[b] = window[:, lanes]
        full = out[:, lanes] + skip[...] * mixins[b].astype(f32)
        conv[span] = full
        gate = (act[0, span] * full).astype(bf16)
        for half in range(2):
            start = pl.multiple_of(order[2 * b + half], BLK // 2)
            gated[pl.ds(start, BLK // 2)] = gate[half * (BLK // 2) : (half + 1) * (BLK // 2)]


def backward_kernel(place, acc, act0, act12, convh, mspec, fspec, skip, fwd, inv, invlag, *refs):
    og, refs = refs[: 2 * SIDE], refs[2 * SIDE :]
    weights, (bg, pay0, pay1, pay2, pay3, gmix, lagbuf) = refs[:4], refs[4:]
    rows = bg.shape[0]
    nb = rows // BLK
    fmat, imat = fwd[...], inv[...]
    filt = fspec[...]
    blocks = [w[n] for w in weights for n in range(2)]
    bg[...] = acc[...] + lax.dot_general(
        jnp.concatenate([o[...] for o in og], 1),
        jnp.concatenate(blocks, 1),
        (((1,), (1,)), ((), ())),
        preferred_element_type=f32,
    )
    wide = filt.shape[1]
    grads = [
        (bg[b * BLK : (b + 1) * BLK] * act0[0, b * BLK : (b + 1) * BLK]).astype(bf16)
        for b in range(nb)
    ]
    spec = spectrum(fmat, jnp.concatenate(grads, 1))
    lag = product_conj(spec[:, :wide], mspec[0])
    for b in range(1, nb):
        lag = lag + product_conj(spec[:, b * wide : (b + 1) * wide], mspec[b])
    lagbuf[...] = invert(invlag[...], lag)
    following = jnp.concatenate([spec[:, wide:], jnp.zeros(filt.shape, f32)], 1)
    window = spec + delay(following)
    out = invert(imat, product_conj(window, jnp.concatenate([filt] * nb, 1)))
    for b in range(nb):
        gm = out[:, b * wide : (b + 1) * wide] + skip[...] * grads[b].astype(f32)
        gmix[b * BLK : (b + 1) * BLK] = gm
        if b == 0:
            head = gm[:PAD]
            ga0 = bg[:PAD] * convh[...]
            ga1 = head * act12[1]
            ga2 = head * act12[0]
            edge = jnp.concatenate(
                [ga0[:2], ga1[:2], ga2[:2], jnp.zeros((2, gm.shape[1]), f32)], 0
            ).astype(bf16)
    quarter = BLK // SIDE
    for k, pay in enumerate((pay0, pay1, pay2, pay3)):
        pay[:BLK] = grads[0]
        pay[BLK : BLK + PAD] = edge
        start = pl.multiple_of((place[0] ^ k) * quarter, quarter)
        pay[BLK + PAD :] = lagbuf[pl.ds(start, quarter)].astype(bf16)


def finish_body(bg, conv, gmix, act, proj, sf, extra, gp, ext):
    rows = bg.shape[0]
    sums = []
    for m in range(3):
        if m == 0:
            ga = bg[...] * conv[...]
        else:
            ga = gmix[...] * act[2 - m]
        ext[:rows] = ga
        ext[rows : rows + PAD] = extra[m]
        x = proj[m].astype(f32)
        total = sf[m, 0:1] * ga
        sums.append(jnp.sum(x * ga, axis=0, keepdims=True))
        for s in (1, 2):
            moved = ext[s : s + rows]
            total = total + sf[m, s : s + 1] * moved
            sums.append(jnp.sum(x * moved, axis=0, keepdims=True))
        gp[m] = total.astype(bf16)
    return jnp.concatenate(sums + [jnp.zeros((7, bg.shape[1]), f32)], 0)


def top_kernel(bg, conv, gmix, act, bgn, convn, gmixn, actn, proj, sf, gp, short, ext):
    extra = [bgn[...] * convn[...], gmixn[...] * actn[1], gmixn[...] * actn[0]]
    short[...] = finish_body(bg, conv, gmix, act, proj, sf, extra, gp, ext)


def bottom_kernel(
    bg, conv, gmix, act, halo, proj, sf, fspec, fwd, inv, short_in, gp_in, gp, short, ext, gfull
):
    del gp_in
    rows = bg.shape[0]
    late = delay(spectrum(fwd[...], halo[:BLK]))
    gfull[: rows - BLK] = gmix[: rows - BLK]
    gfull[rows - BLK :] = gmix[rows - BLK :] + invert(inv[...], product_conj(late, fspec[...]))
    edge = halo[BLK : BLK + PAD].astype(f32)
    zeros = jnp.zeros((PAD - 2, edge.shape[1]), f32)
    extra = [jnp.concatenate([edge[2 * m : 2 * m + 2], zeros], 0) for m in range(3)]
    short[...] = short_in[...] + finish_body(bg, conv, gfull, act, proj, sf, extra, gp, ext)


def pieces_kernel(steps, back, *refs):
    weights, refs = refs[: 2 * steps], refs[2 * steps :]
    if back:
        gated, og, (mine, other, acc, buf, sems) = refs[0], refs[1 : 1 + SIDE], refs[1 + SIDE :]
    else:
        gated, mine, other, buf, sems = refs
    step = pl.program_id(0)
    chans, half = gated.shape[1], gated.shape[0] // 2
    width = buf.shape[2] // SIDE

    def copies(i):
        return [
            pltpu.make_async_copy(
                weights[2 * i + j // 2].at[pl.ds((j % 2) * chans, chans)],
                buf.at[i % 2, :, pl.ds(j * width, width)],
                sems.at[i % 2, j],
            )
            for j in range(SIDE)
        ]

    @pl.when(step == 0)
    def _():
        for c in copies(0):
            c.start()
        if back:
            acc[...] = jnp.zeros_like(acc)

    for i in range(steps):

        @pl.when(step == i)
        def _(i=i):
            if i + 1 < steps:
                for c in copies(i + 1):
                    c.start()
            for c in copies(i):
                c.wait()

    w = buf[step % 2]
    out = jnp.dot(gated[...], w, preferred_element_type=f32).astype(bf16)
    mine[...] = out[:half]
    other[...] = out[half:]
    if back:
        acc[...] += lax.dot_general(
            jnp.concatenate([o[...] for o in og], 1),
            w,
            (((1,), (1,)), ((), ())),
            preferred_element_type=f32,
        )


def multiply_pieces(weights, cols, gated, out_grad, back):
    rows, chans = gated.shape
    width = weights[0].shape[1]
    steps = len(weights) // 2
    whole = pl.BlockSpec((rows, chans), lambda i, c: (0, 0), pipeline_mode=pl.Buffered(1))
    in_specs = [pl.BlockSpec(memory_space=pl.ANY)] * len(weights) + [whole]
    operands = [*weights, gated]
    if back:
        in_specs += [
            pl.BlockSpec((rows, width), lambda i, c, j=j: (0, c[SIDE * i + j])) for j in range(SIDE)
        ]
        operands += [out_grad] * SIDE
    half_shape = jax.ShapeDtypeStruct((rows // 2, steps * SIDE * width), bf16)
    half_spec = pl.BlockSpec((rows // 2, SIDE * width), lambda i, c: (0, i))

    def kernel(cols_ref, *refs):
        del cols_ref
        pieces_kernel(steps, back, *refs)

    return pl.pallas_call(
        kernel,
        grid_spec=pltpu.PrefetchScalarGridSpec(
            num_scalar_prefetch=1,
            grid=(steps,),
            in_specs=in_specs,
            out_specs=[half_spec, half_spec] + [whole] * back,
            scratch_shapes=[
                pltpu.VMEM((2, chans, SIDE * width), bf16),
                pltpu.SemaphoreType.DMA((2, SIDE)),
            ],
        ),
        out_shape=[half_shape, half_shape] + [jax.ShapeDtypeStruct((rows, chans), f32)] * back,
        cost_estimate=pl.CostEstimate(
            flops=(2 + 2 * back) * rows * chans * width * SIDE * steps,
            bytes_accessed=SIDE * steps * (2 * chans * width + 4 * rows * width) + 6 * rows * chans,
            transcendentals=0,
        ),
        name="pieces",
    )(cols, *operands)


def collect_kernel(counts, cols, *refs):
    mixed = refs[-1]
    width = mixed.shape[1] // sum(counts)
    begin = 0
    for i, count in enumerate(counts):
        parts = refs[4 * i : 4 * i + 4]

        @pl.loop(0, count)
        def _(p, parts=parts, begin=begin):
            lanes = pl.ds(pl.multiple_of(p * width, width), width)
            vals = [r[:, lanes].astype(f32) for r in parts]
            start = pl.multiple_of(cols[begin + p] * width, width)
            mixed[:, pl.ds(start, width)] = (
                (vals[0] + vals[1]) + (vals[2] + vals[3])
            ).astype(bf16)

        begin += count


def on_device(projected, short_filter, long_filter, skip_gain, out_weight, out_grad, left_source):
    rows, chans = projected.shape[1:]
    width = out_weight.shape[1] // 2
    ctx_count, tp_count = lax.axis_size("ctx"), lax.axis_size("tp")
    me, tp = lax.axis_index("ctx"), lax.axis_index("tp")
    zi, xi, yi, ci = me // SIDE, me % SIDE, tp // 2, tp % 2

    def ring(value, axis, step):
        if axis == "x":
            pairs = [(d, d // SIDE * SIDE + (d + step) % SIDE) for d in range(ctx_count)]
        else:
            pairs = [(d, (d + SIDE * step) % ctx_count) for d in range(ctx_count)]
        return lax.ppermute(value, "ctx", pairs)

    def swap(value, axis, k):
        shift = {"x": k, "z": k * SIDE, "core": k, "y": 2 * k}[axis]
        name = "ctx" if axis in "xz" else "tp"
        return lax.ppermute(value, name, [(d, d ^ shift) for d in range(lax.axis_size(name))])

    def gather(piece, first, second, turn):
        p, q = ring(piece, first, 1), ring(piece, first, -1)
        r = ring(p if turn > 0 else q, first, turn)
        one, two = jnp.concatenate([piece, p], 0), jnp.concatenate([q, r], 0)
        op, oq = ring(one, second, 1), ring(one, second, -1)
        tp_, tq = ring(two, second, 1), ring(two, second, -1)
        far_one = ring(op, second, 1)
        far_two = ring(tq, second, -1)
        return [one, two], [op, tp_, oq, tq], [far_one, far_two]

    def blocks(half, near, far_steps):
        out = []
        for f in far_steps:
            for n in near:
                z, x = (f, n) if half == 0 else (n, f)
                out.append(2 * ((zi + z) % SIDE * SIDE + (xi + x) % SIDE) + half)
        return out

    order4 = (0, -1, 1, 2)
    cols1 = jnp.stack(
        blocks(0, order4, (0,)) + blocks(1, order4, (0,))
        + blocks(0, order4, (-1, 1)) + blocks(1, order4, (-1, 1))
    )
    cols3 = jnp.stack(blocks(0, order4, (2,)) + blocks(1, order4, (2,)))

    positions = jnp.arange(ctx_count, dtype=jnp.int32)
    matches = left_source[None, :] == positions[:, None]
    readers = jnp.where(
        jnp.any(matches, 1), jnp.sum(jnp.where(matches, positions[None, :], 0), 1), -1
    )

    def pick(options, index):
        low = jnp.where(index == 1, options[1], options[0])
        high = jnp.where(index == 3, options[3], options[2])
        return jnp.where(index >= 2, high, low)

    def at(table, index):
        return lax.dynamic_index_in_dim(table, index, 0, keepdims=False)

    def along_x(payloads):
        return [payloads[0]] + [swap(payloads[k], "x", k) for k in (1, 2, 3)]

    def along_z(payloads):
        return [payloads[0]] + [swap(payloads[k], "z", k) for k in (1, 2, 3)]

    def chosen(got, table):
        out = []
        for k in range(SIDE):
            source = jnp.maximum(at(table, (zi ^ k) * SIDE + xi), 0)
            out.append(pick(got, (source % SIDE) ^ xi))
        return out

    def landed(got, table):
        source = at(table, me)
        value = pick(got, (jnp.maximum(source, 0) // SIDE) ^ zi)
        return jnp.where(source >= 0, value, jnp.zeros_like(value))

    near = projected[1:, rows - BLK - PAD :].astype(f32)
    tail = jnp.zeros((2, BLK, chans), f32)
    for s in range(3):
        tail = tail + short_filter[1:, s][:, None] * near[:, PAD - s : PAD - s + BLK]
    raw = projected[:, rows - 2 :].reshape(6, chans)
    sent = jnp.concatenate(
        [(tail[0] * tail[1]).astype(bf16), raw, jnp.zeros((2, chans), bf16)], 0
    )
    got = along_x([sent] * SIDE)
    to_z = chosen(got, left_source)
    got = along_z(to_z)
    left = landed(got, left_source)

    wa, wb, _ = lax.optimization_barrier((out_weight[:, :width], out_weight[:, width:], sent))
    near_a, mid_a, far_a = gather(wa, "x", "z", 1)
    near_b, mid_b, far_b = gather(wb, "z", "x", -1)

    fwd = jnp.asarray(forward_matrix())
    inv_late, inv_now, inv_lag = (jnp.asarray(inverse_matrix(s)) for s in (BLK, 0, -BLK))
    skip_row = skip_gain[None, :]
    share = rows // tp_count
    order = jnp.stack(
        [
            (((t % 2) ^ ci) * SIDE + ((t // 2) ^ yi)) * share
            for t in range(tp_count)
        ]
    ).astype(jnp.int32)
    tile = 256
    grid = (chans // tile,)
    nb = rows // BLK

    def col(*lead):
        return pl.BlockSpec((*lead, tile), lambda i, *_: (*([0] * len(lead)), i))

    const = pl.BlockSpec((2 * BLK, 2 * BLK), lambda i, *_: (0, 0))
    forward = pl.pallas_call(
        forward_kernel,
        grid_spec=pltpu.PrefetchScalarGridSpec(
            num_scalar_prefetch=1,
            grid=grid,
            in_specs=[
                col(3, rows), col(BLK + PAD), col(3, 3), col(BLK), col(1), const, const,
            ],
            out_specs=[col(rows), col(rows), col(3, rows), col(nb, 2 * BLK), col(2 * BLK)],
            scratch_shapes=[pltpu.VMEM((rows + PAD, tile), f32)],
        ),
        out_shape=[
            jax.ShapeDtypeStruct((rows, chans), bf16),
            jax.ShapeDtypeStruct((rows, chans), f32),
            jax.ShapeDtypeStruct((3, rows, chans), f32),
            jax.ShapeDtypeStruct((nb, 2 * BLK, chans), f32),
            jax.ShapeDtypeStruct((2 * BLK, chans), f32),
        ],
        cost_estimate=pl.CostEstimate(
            flops=12_000_000_000, bytes_accessed=20 << 20, transcendentals=0
        ),
        name="forward",
    )
    gated, conv, act, mspec, fspec = forward(
        order, projected, left, short_filter, long_filter, skip_row, fwd, inv_late
    )

    def scatter(mine, other):
        got = swap(other, "core", 1)
        total = (mine.astype(f32) + got.astype(f32)).astype(bf16)
        parts = [total[k * share : (k + 1) * share] for k in range(SIDE)]
        return [parts[0]] + [swap(parts[k], "y", k) for k in (1, 2, 3)]

    mine1, other1, acc = multiply_pieces(
        near_a + near_b + mid_a + mid_b, cols1, gated, out_grad, True
    )
    out1 = scatter(mine1, other1)

    quarter = BLK // SIDE
    place = jnp.concatenate([jnp.reshape(xi, (1,)), cols3]).astype(jnp.int32)

    def third(w):
        count = w.shape[0] // chans
        return w.reshape(count, chans, width), pl.BlockSpec(
            (count, tile, width), lambda i, c: (0, i, 0)
        )

    lasts, last_specs = zip(*[third(w) for w in far_a + far_b])
    pay_shape = jax.ShapeDtypeStruct((BLK + PAD + quarter, chans), bf16)
    pay_spec = col(BLK + PAD + quarter)
    backward = pl.pallas_call(
        backward_kernel,
        grid_spec=pltpu.PrefetchScalarGridSpec(
            num_scalar_prefetch=1,
            grid=grid,
            in_specs=[
                col(rows),
                pl.BlockSpec((1, rows, tile), lambda i, c: (0, 0, i)),
                pl.BlockSpec(
                    (pl.Element(2), pl.Element(PAD), pl.Element(tile)),
                    lambda i, c: (1, 0, i * tile),
                ),
                col(PAD),
                col(nb, 2 * BLK),
                col(2 * BLK),
                col(1),
                const,
                const,
                const,
                *[
                    pl.BlockSpec((rows, width), lambda i, c, j=j: (0, c[1 + j]))
                    for j in range(2 * SIDE)
                ],
                *last_specs,
            ],
            out_specs=[col(rows), pay_spec, pay_spec, pay_spec, pay_spec, col(rows)],
            scratch_shapes=[pltpu.VMEM((BLK, tile), f32)],
        ),
        out_shape=[
            jax.ShapeDtypeStruct((rows, chans), f32),
            pay_shape, pay_shape, pay_shape, pay_shape,
            jax.ShapeDtypeStruct((rows, chans), f32),
        ],
        cost_estimate=pl.CostEstimate(
            flops=8_000_000_000, bytes_accessed=20 << 20, transcendentals=0
        ),
        name="backward",
    )
    bg, pay0, pay1, pay2, pay3, gmix = backward(
        place, acc, act, act, conv, mspec, fspec, skip_row, fwd, inv_now, inv_lag,
        *[out_grad] * (2 * SIDE), *lasts,
    )

    got = along_x([pay0, pay1, pay2, pay3])
    sums = [g[BLK + PAD :].astype(f32) for g in got]
    quarter_sum = ((sums[0] + sums[1]) + (sums[2] + sums[3])).astype(bf16)
    to_z = chosen([g[: BLK + PAD] for g in got], readers)
    got = along_z([jnp.concatenate([v, quarter_sum], 0) for v in to_z])
    right = landed([g[: BLK + PAD] for g in got], readers)
    sums = [g[BLK + PAD :].astype(f32) for g in got]
    my_quarter = (sums[0] + sums[1]) + (sums[2] + sums[3])

    mine3, other3 = multiply_pieces(far_a + far_b, cols3, gated, None, False)
    out3 = scatter(mine3, other3)

    low = rows - BLK - PAD

    def rows_at(start, n, *lead):
        zeros = [0] * len(lead)
        dims = [pl.Element(d) for d in (*lead, n, tile)]
        return pl.BlockSpec(tuple(dims), lambda i: (*zeros, start, i * tile))

    def acts_at(start, n):
        return pl.BlockSpec(
            (pl.Element(2), pl.Element(n), pl.Element(tile)), lambda i: (1, start, i * tile)
        )

    gp_shape = jax.ShapeDtypeStruct((3, rows, chans), bf16)
    short_shape = jax.ShapeDtypeStruct((16, chans), f32)
    top = pl.pallas_call(
        top_kernel,
        grid=grid,
        in_specs=[
            rows_at(0, low), rows_at(0, low), rows_at(0, low), acts_at(0, low),
            rows_at(low, PAD), rows_at(low, PAD), rows_at(low, PAD), acts_at(low, PAD),
            rows_at(0, low, 3), col(3, 3),
        ],
        out_specs=[rows_at(0, low, 3), col(16)],
        out_shape=[gp_shape, short_shape],
        scratch_shapes=[pltpu.VMEM((low + PAD, tile), f32)],
        cost_estimate=pl.CostEstimate(
            flops=200_000_000, bytes_accessed=10 << 20, transcendentals=0
        ),
        name="top",
    )
    gp, short = top(bg, conv, gmix, act, bg, conv, gmix, act, projected, short_filter)
    rest = rows - low
    bottom = pl.pallas_call(
        bottom_kernel,
        grid=grid,
        in_specs=[
            rows_at(low, rest), rows_at(low, rest), rows_at(low, rest), acts_at(low, rest),
            col(BLK + PAD), rows_at(low, rest, 3), col(3, 3), col(2 * BLK), const, const, col(16),
            pl.BlockSpec(memory_space=pl.ANY),
        ],
        out_specs=[rows_at(low, rest, 3), col(16)],
        out_shape=[gp_shape, short_shape],
        scratch_shapes=[pltpu.VMEM((rest + PAD, tile), f32), pltpu.VMEM((rest, tile), f32)],
        input_output_aliases={11: 0},
        cost_estimate=pl.CostEstimate(
            flops=2_000_000_000, bytes_accessed=5 << 20, transcendentals=0
        ),
        name="bottom",
    )
    gp, short = bottom(
        bg, conv, gmix, act, right, projected, short_filter, fspec, fwd, inv_now, short, gp
    )

    got = along_x([jnp.concatenate([my_quarter, short], 0).astype(bf16)] * SIDE)
    long_total = jnp.concatenate([pick(got, xi ^ q)[:quarter] for q in range(SIDE)], 0)
    sums = [g[quarter:].astype(f32) for g in got]
    sums = (sums[0] + sums[1]) + (sums[2] + sums[3])
    sums = along_z([sums] * SIDE)
    short_total = ((sums[0] + sums[1]) + (sums[2] + sums[3]))[:9].reshape(3, 3, chans)

    counts = tuple(o[0].shape[1] // width for o in (out1, out3))
    collect = pl.pallas_call(
        lambda cols, *refs: collect_kernel(counts, cols, *refs),
        grid_spec=pltpu.PrefetchScalarGridSpec(
            num_scalar_prefetch=1,
            grid=(1,),
            in_specs=[
                pl.BlockSpec(o[0].shape, lambda i, c: (0, 0))
                for o in (out1, out3)
                for _ in range(SIDE)
            ],
            out_specs=pl.BlockSpec((share, 2 * width * ctx_count), lambda i, c: (0, 0)),
        ),
        out_shape=jax.ShapeDtypeStruct((share, 2 * width * ctx_count), bf16),
        cost_estimate=pl.CostEstimate(flops=10_000_000, bytes_accessed=5 << 20, transcendentals=0),
        name="collect",
    )
    mixed = collect(jnp.concatenate([cols1, cols3]), *out1, *out3)

    scale = 1.0 / math.sqrt(rows * ctx_count)
    return mixed, gp, long_total.astype(f32) * scale, short_total * scale


def solution(mesh):
    placed = (
        P(None, "ctx", "tp"),
        P(None, None, "tp"),
        P(None, "tp"),
        P("tp"),
        P("tp", "ctx"),
        P("ctx", None),
        P(),
    )
    return jax.shard_map(
        on_device,
        mesh=mesh,
        in_specs=placed,
        out_specs=(
            P(("ctx", "tp"), None),
            P(None, "ctx", "tp"),
            P(None, "tp"),
            P(None, None, "tp"),
        ),
        check_vma=False,
    )
```

```python
import math

import jax
import jax.numpy as jnp
import numpy as np
from jax import lax
from jax.experimental import pallas as pl
from jax.experimental.pallas import tpu as pltpu
from jax.sharding import PartitionSpec as P


f32, bf16 = jnp.float32, jnp.bfloat16
BLK = 128
SIDE = 4
PAD = 8


def split_hi_lo(matrix):
    hi = matrix.astype(np.float32).astype(bf16)
    lo = (matrix - hi.astype(np.float64)).astype(np.float32).astype(bf16)
    return hi, lo


def angles(times):
    freqs = np.concatenate([np.arange(0, BLK, 2), np.arange(1, BLK, 2)]) + 0.5
    return 2.0 * np.pi * freqs[:, None] * times[None, :] / (2 * BLK)


def forward_matrix():
    th = angles(np.arange(BLK, dtype=np.float64))
    hi, lo = split_hi_lo(np.concatenate([np.cos(th), -np.sin(th)], 0))
    return np.concatenate([hi, lo], 1)


def inverse_matrix(start):
    th = angles(np.arange(start, start + BLK, dtype=np.float64)).T / 1.0
    hi, lo = split_hi_lo(np.concatenate([np.cos(th), -np.sin(th)], 1) / BLK)
    return np.concatenate([hi, lo], 0)


def spectrum(fwd, rows):
    return jnp.dot(fwd, jnp.concatenate([rows, rows], 0), preferred_element_type=f32)


def delay(v):
    h = BLK // 2
    re, im = v[:BLK], v[BLK:]
    return jnp.concatenate([im[:h], -im[h:], -re[:h], re[h:]], 0)


def product(a, b):
    ar, ai, br, bi = a[:BLK], a[BLK:], b[:BLK], b[BLK:]
    return jnp.concatenate([ar * br - ai * bi, ar * bi + ai * br], 0)


def product_conj(a, b):
    ar, ai, br, bi = a[:BLK], a[BLK:], b[:BLK], b[BLK:]
    return jnp.concatenate([ar * br + ai * bi, ai * br - ar * bi], 0)


def invert(inv, y):
    hi = y.astype(bf16)
    lo = (y - hi.astype(f32)).astype(bf16)
    both = jnp.dot(inv, hi, preferred_element_type=f32)
    return both[:BLK] + both[BLK:] + jnp.dot(inv[:BLK], lo, preferred_element_type=f32)


def forward_kernel(order, proj, halo, sf, lf, skip, fwd, inv, gated, conv, act, mspec, fspec, ext):
    rows = proj.shape[1]
    fmat, imat = fwd[...], inv[...]
    for m in range(3):
        ext[PAD : PAD + rows] = proj[m].astype(f32)
        edge = halo[BLK : BLK + PAD].astype(f32)
        ext[PAD - 2 : PAD] = edge[2 * m : 2 * m + 2]
        total = sf[m, 0:1] * ext[PAD : PAD + rows]
        for s in (1, 2):
            total = total + sf[m, s : s + 1] * ext[PAD - s : PAD - s + rows]
        act[m] = total
    filt = spectrum(fmat, lf[...])
    fspec[...] = filt
    nb, wide = rows // BLK, filt.shape[1]
    mixins = [
        (act[1, b * BLK : (b + 1) * BLK] * act[2, b * BLK : (b + 1) * BLK]).astype(bf16)
        for b in range(nb)
    ]
    spec = spectrum(fmat, jnp.concatenate([halo[:BLK]] + mixins, 1))
    window = spec[:, : nb * wide] + delay(spec[:, wide:])
    out = invert(imat, product(window, jnp.concatenate([filt] * nb, 1)))
    for b in range(nb):
        span = slice(b * BLK, (b + 1) * BLK)
        lanes = slice(b * wide, (b + 1) * wide)
        mspec[b] = window[:, lanes]
        full = out[:, lanes] + skip[...] * mixins[b].astype(f32)
        conv[span] = full
        gate = (act[0, span] * full).astype(bf16)
        for half in range(2):
            start = pl.multiple_of(order[2 * b + half], BLK // 2)
            gated[pl.ds(start, BLK // 2)] = gate[half * (BLK // 2) : (half + 1) * (BLK // 2)]


def backward_kernel(place, acc, act0, mspec, fspec, skip, fwd, inv, invlag, *refs):
    og, refs = refs[: 2 * SIDE], refs[2 * SIDE :]
    weights, (bg, long0, long1, long2, long3, gmix, lagbuf) = refs[:4], refs[4:]
    rows = bg.shape[0]
    nb = rows // BLK
    fmat, imat = fwd[...], inv[...]
    filt = fspec[...]
    blocks = [w[n] for w in weights for n in range(2)]
    bg[...] = acc[...] + lax.dot_general(
        jnp.concatenate([o[...] for o in og], 1),
        jnp.concatenate(blocks, 1),
        (((1,), (1,)), ((), ())),
        preferred_element_type=f32,
    )
    wide = filt.shape[1]
    grads = [
        (bg[b * BLK : (b + 1) * BLK] * act0[0, b * BLK : (b + 1) * BLK]).astype(bf16)
        for b in range(nb)
    ]
    spec = spectrum(fmat, jnp.concatenate(grads, 1))
    lag = product_conj(spec[:, :wide], mspec[0])
    for b in range(1, nb):
        lag = lag + product_conj(spec[:, b * wide : (b + 1) * wide], mspec[b])
    lagbuf[...] = invert(invlag[...], lag)
    following = jnp.concatenate([spec[:, wide:], jnp.zeros(filt.shape, f32)], 1)
    window = spec + delay(following)
    out = invert(imat, product_conj(window, jnp.concatenate([filt] * nb, 1)))
    for b in range(nb):
        gm = out[:, b * wide : (b + 1) * wide] + skip[...] * grads[b].astype(f32)
        gmix[b * BLK : (b + 1) * BLK] = gm
    quarter = BLK // SIDE
    for k, part in enumerate((long0, long1, long2, long3)):
        start = pl.multiple_of((place[0] ^ k) * quarter, quarter)
        part[...] = lagbuf[pl.ds(start, quarter)].astype(bf16)


def head_kernel(place, acc, act0, act12, convh, lf, skip, *refs):
    del place
    og, refs = refs[: 2 * SIDE], refs[2 * SIDE :]
    weights, (pay, ext) = refs[:4], refs[4:]
    bg = acc[...] + lax.dot_general(
        jnp.concatenate([o[...] for o in og], 1),
        jnp.concatenate([w[n] for w in weights for n in range(2)], 1),
        (((1,), (1,)), ((), ())),
        preferred_element_type=f32,
    )
    g = (bg * act0[0]).astype(bf16)
    ext[...] = g.astype(f32)
    taps = lf[...].astype(f32)
    gm0 = jnp.sum(taps * ext[:BLK], axis=0, keepdims=True) + skip[...] * ext[0:1]
    gm1 = jnp.sum(taps * ext[1 : BLK + 1], axis=0, keepdims=True) + skip[...] * ext[1:2]
    gm = jnp.concatenate([gm0, gm1], 0)
    edge = [bg[:2] * convh[:2], gm * act12[1, :2], gm * act12[0, :2], jnp.zeros_like(gm)]
    pay[:BLK] = g[:BLK]
    pay[BLK:] = jnp.concatenate(edge, 0).astype(bf16)


def finish_body(bg, conv, gmix, act, proj, sf, extra, gp, ext):
    rows = bg.shape[0]
    sums = []
    for m in range(3):
        if m == 0:
            ga = bg[...] * conv[...]
        else:
            ga = gmix[...] * act[2 - m]
        ext[:rows] = ga
        ext[rows : rows + PAD] = extra[m]
        x = proj[m].astype(f32)
        total = sf[m, 0:1] * ga
        sums.append(jnp.sum(x * ga, axis=0, keepdims=True))
        for s in (1, 2):
            moved = ext[s : s + rows]
            total = total + sf[m, s : s + 1] * moved
            sums.append(jnp.sum(x * moved, axis=0, keepdims=True))
        gp[m] = total.astype(bf16)
    return jnp.concatenate(sums + [jnp.zeros((7, bg.shape[1]), f32)], 0)


def top_kernel(bg, conv, gmix, act, bgn, convn, gmixn, actn, proj, sf, gp, short, ext):
    extra = [bgn[...] * convn[...], gmixn[...] * actn[1], gmixn[...] * actn[0]]
    short[...] = finish_body(bg, conv, gmix, act, proj, sf, extra, gp, ext)


def bottom_kernel(
    bg, conv, gmix, act, halo, proj, sf, fspec, fwd, inv, short_in, gp_in, gp, short, ext, gfull
):
    del gp_in
    rows = bg.shape[0]
    late = delay(spectrum(fwd[...], halo[:BLK]))
    gfull[: rows - BLK] = gmix[: rows - BLK]
    gfull[rows - BLK :] = gmix[rows - BLK :] + invert(inv[...], product_conj(late, fspec[...]))
    edge = halo[BLK : BLK + PAD].astype(f32)
    zeros = jnp.zeros((PAD - 2, edge.shape[1]), f32)
    extra = [jnp.concatenate([edge[2 * m : 2 * m + 2], zeros], 0) for m in range(3)]
    short[...] = short_in[...] + finish_body(bg, conv, gfull, act, proj, sf, extra, gp, ext)


def pieces_kernel(steps, back, more, *refs):
    weights, refs = refs[: 2 * steps], refs[2 * steps :]
    if back:
        gated, og, refs = refs[0], refs[1 : 1 + SIDE], refs[1 + SIDE :]
        if more:
            acc_in, refs = refs[0], refs[3:]
        mine, other, acc, buf, sems = refs
    else:
        gated, mine, other, buf, sems = refs
    step = pl.program_id(0)
    chans, half = gated.shape[1], gated.shape[0] // 2
    width = buf.shape[2] // SIDE

    def copies(i):
        return [
            pltpu.make_async_copy(
                weights[2 * i + j // 2].at[pl.ds((j % 2) * chans, chans)],
                buf.at[i % 2, :, pl.ds(j * width, width)],
                sems.at[i % 2, j],
            )
            for j in range(SIDE)
        ]

    @pl.when(step == 0)
    def _():
        for c in copies(0):
            c.start()
        if back:
            acc[...] = acc_in[...] if more else jnp.zeros_like(acc)

    for i in range(steps):

        @pl.when(step == i)
        def _(i=i):
            if i + 1 < steps:
                for c in copies(i + 1):
                    c.start()
            for c in copies(i):
                c.wait()

    w = buf[step % 2]
    out = jnp.dot(gated[...], w, preferred_element_type=f32).astype(bf16)
    mine[...] = out[:half]
    other[...] = out[half:]
    if back:
        acc[...] += lax.dot_general(
            jnp.concatenate([o[...] for o in og], 1),
            w,
            (((1,), (1,)), ((), ())),
            preferred_element_type=f32,
        )


def multiply_pieces(weights, cols, gated, out_grad=None, total=None, before=None):
    rows, chans = gated.shape
    width = weights[0].shape[1]
    steps = len(weights) // 2
    back, more = out_grad is not None, before is not None
    total = total or steps
    offset = before[0] if more else 0
    whole = pl.BlockSpec((rows, chans), lambda i, c: (0, 0), pipeline_mode=pl.Buffered(1))
    in_specs = [pl.BlockSpec(memory_space=pl.ANY)] * len(weights) + [whole]
    operands = [*weights, gated]
    aliases = {}
    if back:
        in_specs += [
            pl.BlockSpec((rows, width), lambda i, c, j=j: (0, c[SIDE * i + j])) for j in range(SIDE)
        ]
        operands += [out_grad] * SIDE
        if more:
            in_specs += [whole] + [pl.BlockSpec(memory_space=pl.ANY)] * 2
            operands += [before[3], before[1], before[2]]
            aliases = {len(operands) - 1: 0, len(operands): 1}
    half_shape = jax.ShapeDtypeStruct((rows // 2, total * SIDE * width), bf16)
    half_spec = pl.BlockSpec((rows // 2, SIDE * width), lambda i, c: (0, i + offset))

    def kernel(cols_ref, *refs):
        del cols_ref
        pieces_kernel(steps, back, more, *refs)

    return pl.pallas_call(
        kernel,
        grid_spec=pltpu.PrefetchScalarGridSpec(
            num_scalar_prefetch=1,
            grid=(steps,),
            in_specs=in_specs,
            out_specs=[half_spec, half_spec] + [whole] * back,
            scratch_shapes=[
                pltpu.VMEM((2, chans, SIDE * width), bf16),
                pltpu.SemaphoreType.DMA((2, SIDE)),
            ],
        ),
        out_shape=[half_shape, half_shape] + [jax.ShapeDtypeStruct((rows, chans), f32)] * back,
        input_output_aliases=aliases,
        cost_estimate=pl.CostEstimate(
            flops=(2 + 2 * back) * rows * chans * width * SIDE * steps,
            bytes_accessed=SIDE * steps * (2 * chans * width + 4 * rows * width) + 6 * rows * chans,
            transcendentals=0,
        ),
        name="pieces",
    )(cols, *operands)


def collect_kernel(counts, cols, *refs):
    mixed = refs[-1]
    width = mixed.shape[1] // sum(counts)
    begin = 0
    for i, count in enumerate(counts):
        parts = refs[4 * i : 4 * i + 4]

        @pl.loop(0, count)
        def _(p, parts=parts, begin=begin):
            lanes = pl.ds(pl.multiple_of(p * width, width), width)
            vals = [r[:, lanes].astype(f32) for r in parts]
            start = pl.multiple_of(cols[begin + p] * width, width)
            mixed[:, pl.ds(start, width)] = (
                (vals[0] + vals[1]) + (vals[2] + vals[3])
            ).astype(bf16)

        begin += count


def on_device(projected, short_filter, long_filter, skip_gain, out_weight, out_grad, left_source):
    rows, chans = projected.shape[1:]
    width = out_weight.shape[1] // 2
    ctx_count, tp_count = lax.axis_size("ctx"), lax.axis_size("tp")
    me, tp = lax.axis_index("ctx"), lax.axis_index("tp")
    zi, xi, yi, ci = me // SIDE, me % SIDE, tp // 2, tp % 2

    def ring(value, axis, step):
        if axis == "x":
            pairs = [(d, d // SIDE * SIDE + (d + step) % SIDE) for d in range(ctx_count)]
        else:
            pairs = [(d, (d + SIDE * step) % ctx_count) for d in range(ctx_count)]
        return lax.ppermute(value, "ctx", pairs)

    def swap(value, axis, k):
        shift = {"x": k, "z": k * SIDE, "core": k, "y": 2 * k}[axis]
        name = "ctx" if axis in "xz" else "tp"
        return lax.ppermute(value, name, [(d, d ^ shift) for d in range(lax.axis_size(name))])

    def gather(piece, first, second):
        h = piece.shape[0] // 2
        p, q = ring(piece, first, 1), ring(piece, first, -1)
        t, b = ring(p[:h], first, 1), ring(q[h:], first, -1)
        one, two = jnp.concatenate([piece, p], 0), jnp.concatenate([q, t, b], 0)
        op, oq = ring(one, second, 1), ring(one, second, -1)
        tp_, tq = ring(two, second, 1), ring(two, second, -1)
        far_one = ring(op, second, 1)
        far_two = ring(tq, second, -1)
        return [one, two], [op, tp_, oq, tq], [far_one, far_two]

    def blocks(half, near, far_steps):
        out = []
        for f in far_steps:
            for n in near:
                z, x = (f, n) if half == 0 else (n, f)
                out.append(2 * ((zi + z) % SIDE * SIDE + (xi + x) % SIDE) + half)
        return out

    order4 = (0, -1, 1, 2)
    cols1 = jnp.stack(blocks(0, order4, (0,)) + blocks(1, order4, (0,)))
    cols2 = jnp.stack(blocks(0, order4, (-1, 1)) + blocks(1, order4, (-1, 1)))
    cols3 = jnp.stack(blocks(0, order4, (2,)) + blocks(1, order4, (2,)))

    positions = jnp.arange(ctx_count, dtype=jnp.int32)
    matches = left_source[None, :] == positions[:, None]
    readers = jnp.where(
        jnp.any(matches, 1), jnp.sum(jnp.where(matches, positions[None, :], 0), 1), -1
    )

    def pick(options, index):
        low = jnp.where(index == 1, options[1], options[0])
        high = jnp.where(index == 3, options[3], options[2])
        return jnp.where(index >= 2, high, low)

    def at(table, index):
        return lax.dynamic_index_in_dim(table, index, 0, keepdims=False)

    def along_x(payloads):
        return [payloads[0]] + [swap(payloads[k], "x", k) for k in (1, 2, 3)]

    def along_z(payloads):
        return [payloads[0]] + [swap(payloads[k], "z", k) for k in (1, 2, 3)]

    def chosen(got, table):
        out = []
        for k in range(SIDE):
            source = jnp.maximum(at(table, (zi ^ k) * SIDE + xi), 0)
            out.append(pick(got, (source % SIDE) ^ xi))
        return out

    def landed(got, table):
        source = at(table, me)
        value = pick(got, (jnp.maximum(source, 0) // SIDE) ^ zi)
        return jnp.where(source >= 0, value, jnp.zeros_like(value))

    near = projected[1:, rows - BLK - PAD :].astype(f32)
    tail = jnp.zeros((2, BLK, chans), f32)
    for s in range(3):
        tail = tail + short_filter[1:, s][:, None] * near[:, PAD - s : PAD - s + BLK]
    raw = projected[:, rows - 2 :].reshape(6, chans)
    sent = jnp.concatenate(
        [(tail[0] * tail[1]).astype(bf16), raw, jnp.zeros((2, chans), bf16)], 0
    )
    got = along_x([sent] * SIDE)
    to_z = chosen(got, left_source)
    got = along_z(to_z)
    left = landed(got, left_source)

    near_a, mid_a, far_a = gather(out_weight[:, :width], "x", "z")
    near_b, mid_b, far_b = gather(out_weight[:, width:], "z", "x")

    fwd = jnp.asarray(forward_matrix())
    inv_late, inv_now, inv_lag = (jnp.asarray(inverse_matrix(s)) for s in (BLK, 0, -BLK))
    skip_row = skip_gain[None, :]
    share = rows // tp_count
    order = jnp.stack(
        [
            (((t % 2) ^ ci) * SIDE + ((t // 2) ^ yi)) * share
            for t in range(tp_count)
        ]
    ).astype(jnp.int32)
    tile = 256
    grid = (chans // tile,)
    nb = rows // BLK

    def col(*lead):
        return pl.BlockSpec((*lead, tile), lambda i, *_: (*([0] * len(lead)), i))

    const = pl.BlockSpec((2 * BLK, 2 * BLK), lambda i, *_: (0, 0))
    forward = pl.pallas_call(
        forward_kernel,
        grid_spec=pltpu.PrefetchScalarGridSpec(
            num_scalar_prefetch=1,
            grid=grid,
            in_specs=[
                col(3, rows), col(BLK + PAD), col(3, 3), col(BLK), col(1), const, const,
            ],
            out_specs=[col(rows), col(rows), col(3, rows), col(nb, 2 * BLK), col(2 * BLK)],
            scratch_shapes=[pltpu.VMEM((rows + PAD, tile), f32)],
        ),
        out_shape=[
            jax.ShapeDtypeStruct((rows, chans), bf16),
            jax.ShapeDtypeStruct((rows, chans), f32),
            jax.ShapeDtypeStruct((3, rows, chans), f32),
            jax.ShapeDtypeStruct((nb, 2 * BLK, chans), f32),
            jax.ShapeDtypeStruct((2 * BLK, chans), f32),
        ],
        cost_estimate=pl.CostEstimate(
            flops=12_000_000_000, bytes_accessed=20 << 20, transcendentals=0
        ),
        name="forward",
    )
    gated, conv, act, mspec, fspec = forward(
        order, projected, left, short_filter, long_filter, skip_row, fwd, inv_late
    )

    def scatter(mine, other):
        got = swap(other, "core", 1)
        parts = [
            (mine[k * share : (k + 1) * share].astype(f32) + got[k * share : (k + 1) * share].astype(f32)).astype(bf16)
            for k in range(SIDE)
        ]
        return [parts[0]] + [swap(parts[k], "y", k) for k in (1, 2, 3)]

    early = multiply_pieces(near_a + near_b, cols1, gated, out_grad, 6)
    mine1, other1, acc = multiply_pieces(
        mid_a + mid_b, cols2, gated, out_grad, 6, (2, *early)
    )
    out1 = scatter(mine1, other1)

    quarter = BLK // SIDE
    place = jnp.concatenate([jnp.reshape(zi, (1,)), cols3]).astype(jnp.int32)
    lasts = [w.reshape(2, chans, width) for w in far_a + far_b]
    last_spec = pl.BlockSpec((2, tile, width), lambda i, c: (0, i, 0))

    def out_grad_rows(n):
        return [pl.BlockSpec((n, width), lambda i, c, j=j: (0, c[1 + j])) for j in range(2 * SIDE)]

    def first_rows(n, *lead):
        zeros = [0] * len(lead)
        return pl.BlockSpec((*lead, n, tile), lambda i, c: (*zeros, 0, i))

    head = pl.pallas_call(
        head_kernel,
        grid_spec=pltpu.PrefetchScalarGridSpec(
            num_scalar_prefetch=1,
            grid=grid,
            in_specs=[
                first_rows(BLK + PAD),
                first_rows(BLK + PAD, 1),
                pl.BlockSpec(
                    (pl.Element(2), pl.Element(PAD), pl.Element(tile)),
                    lambda i, c: (1, 0, i * tile),
                ),
                first_rows(PAD),
                col(BLK),
                col(1),
                *out_grad_rows(BLK + PAD),
                *[last_spec] * 4,
            ],
            out_specs=col(BLK + PAD),
            scratch_shapes=[pltpu.VMEM((BLK + PAD, tile), f32)],
        ),
        out_shape=jax.ShapeDtypeStruct((BLK + PAD, chans), bf16),
        cost_estimate=pl.CostEstimate(
            flops=600_000_000, bytes_accessed=6 << 20, transcendentals=0
        ),
        name="head",
    )
    pay = head(place, acc, act, act, conv, long_filter, skip_row, *[out_grad] * (2 * SIDE), *lasts)
    got = along_x([pay] * SIDE)

    long_shape = jax.ShapeDtypeStruct((quarter, chans), bf16)
    backward = pl.pallas_call(
        backward_kernel,
        grid_spec=pltpu.PrefetchScalarGridSpec(
            num_scalar_prefetch=1,
            grid=grid,
            in_specs=[
                col(rows),
                first_rows(rows, 1),
                col(nb, 2 * BLK),
                col(2 * BLK),
                col(1),
                const,
                const,
                const,
                *out_grad_rows(rows),
                *[last_spec] * 4,
            ],
            out_specs=[col(rows)] + [col(quarter)] * 4 + [col(rows)],
            scratch_shapes=[pltpu.VMEM((BLK, tile), f32)],
        ),
        out_shape=[jax.ShapeDtypeStruct((rows, chans), f32)]
        + [long_shape] * 4
        + [jax.ShapeDtypeStruct((rows, chans), f32)],
        cost_estimate=pl.CostEstimate(
            flops=8_000_000_000, bytes_accessed=20 << 20, transcendentals=0
        ),
        name="backward",
    )
    bg, *longs, gmix = backward(
        place, acc, act, mspec, fspec, skip_row, fwd, inv_now, inv_lag,
        *[out_grad] * (2 * SIDE), *lasts,
    )

    to_z = chosen(got, readers)
    got = along_z([jnp.concatenate([v, part], 0) for v, part in zip(to_z, longs)])
    right = landed([g[: BLK + PAD] for g in got], readers)
    sums = [g[BLK + PAD :].astype(f32) for g in got]
    my_quarter = (sums[0] + sums[1]) + (sums[2] + sums[3])

    mine3, other3 = multiply_pieces(far_a + far_b, cols3, gated)
    out3 = scatter(mine3, other3)

    low = rows - BLK - PAD

    def rows_at(start, n, *lead):
        zeros = [0] * len(lead)
        dims = [pl.Element(d) for d in (*lead, n, tile)]
        return pl.BlockSpec(tuple(dims), lambda i: (*zeros, start, i * tile))

    def acts_at(start, n):
        return pl.BlockSpec(
            (pl.Element(2), pl.Element(n), pl.Element(tile)), lambda i: (1, start, i * tile)
        )

    gp_shape = jax.ShapeDtypeStruct((3, rows, chans), bf16)
    short_shape = jax.ShapeDtypeStruct((16, chans), f32)
    top = pl.pallas_call(
        top_kernel,
        grid=grid,
        in_specs=[
            rows_at(0, low), rows_at(0, low), rows_at(0, low), acts_at(0, low),
            rows_at(low, PAD), rows_at(low, PAD), rows_at(low, PAD), acts_at(low, PAD),
            rows_at(0, low, 3), col(3, 3),
        ],
        out_specs=[rows_at(0, low, 3), col(16)],
        out_shape=[gp_shape, short_shape],
        scratch_shapes=[pltpu.VMEM((low + PAD, tile), f32)],
        cost_estimate=pl.CostEstimate(
            flops=200_000_000, bytes_accessed=10 << 20, transcendentals=0
        ),
        name="top",
    )
    gp, short = top(bg, conv, gmix, act, bg, conv, gmix, act, projected, short_filter)
    rest = rows - low
    bottom = pl.pallas_call(
        bottom_kernel,
        grid=grid,
        in_specs=[
            rows_at(low, rest), rows_at(low, rest), rows_at(low, rest), acts_at(low, rest),
            col(BLK + PAD), rows_at(low, rest, 3), col(3, 3), col(2 * BLK), const, const, col(16),
            pl.BlockSpec(memory_space=pl.ANY),
        ],
        out_specs=[rows_at(low, rest, 3), col(16)],
        out_shape=[gp_shape, short_shape],
        scratch_shapes=[pltpu.VMEM((rest + PAD, tile), f32), pltpu.VMEM((rest, tile), f32)],
        input_output_aliases={11: 0},
        cost_estimate=pl.CostEstimate(
            flops=2_000_000_000, bytes_accessed=5 << 20, transcendentals=0
        ),
        name="bottom",
    )
    gp, short = bottom(
        bg, conv, gmix, act, right, projected, short_filter, fspec, fwd, inv_now, short, gp
    )

    message = jnp.concatenate([my_quarter, short], 0)
    for along in (along_x, along_z):
        got = along([message.astype(bf16)] * SIDE)
        wide = [g.astype(f32) for g in got]
        message = (wide[0] + wide[1]) + (wide[2] + wide[3])
    long_total = jnp.concatenate([pick(got, zi ^ q)[:quarter] for q in range(SIDE)], 0)
    short_total = message[quarter : quarter + 9].reshape(3, 3, chans)

    counts = tuple(o[0].shape[1] // width for o in (out1, out3))
    collect = pl.pallas_call(
        lambda cols, *refs: collect_kernel(counts, cols, *refs),
        grid_spec=pltpu.PrefetchScalarGridSpec(
            num_scalar_prefetch=1,
            grid=(1,),
            in_specs=[
                pl.BlockSpec(o[0].shape, lambda i, c: (0, 0))
                for o in (out1, out3)
                for _ in range(SIDE)
            ],
            out_specs=pl.BlockSpec((share, 2 * width * ctx_count), lambda i, c: (0, 0)),
        ),
        out_shape=jax.ShapeDtypeStruct((share, 2 * width * ctx_count), bf16),
        cost_estimate=pl.CostEstimate(flops=10_000_000, bytes_accessed=5 << 20, transcendentals=0),
        name="collect",
    )
    mixed = collect(jnp.concatenate([cols1, cols2, cols3]), *out1, *out3)

    scale = 1.0 / math.sqrt(rows * ctx_count)
    return mixed, gp, long_total.astype(f32) * scale, short_total * scale


def solution(mesh):
    placed = (
        P(None, "ctx", "tp"),
        P(None, None, "tp"),
        P(None, "tp"),
        P("tp"),
        P("tp", "ctx"),
        P("ctx", None),
        P(),
    )
    return jax.shard_map(
        on_device,
        mesh=mesh,
        in_specs=placed,
        out_specs=(
            P(("ctx", "tp"), None),
            P(None, "ctx", "tp"),
            P(None, "tp"),
            P(None, None, "tp"),
        ),
        check_vma=False,
    )
```

```python
import math

import jax
import jax.numpy as jnp
import numpy as np
from jax import lax
from jax.experimental import pallas as pl
from jax.experimental.pallas import tpu as pltpu
from jax.sharding import PartitionSpec as P


f32, bf16 = jnp.float32, jnp.bfloat16
BLK = 128
SIDE = 4
PAD = 8


def split_hi_lo(matrix):
    hi = matrix.astype(np.float32).astype(bf16)
    lo = (matrix - hi.astype(np.float64)).astype(np.float32).astype(bf16)
    return hi, lo


def angles(times):
    freqs = np.concatenate([np.arange(0, BLK, 2), np.arange(1, BLK, 2)]) + 0.5
    return 2.0 * np.pi * freqs[:, None] * times[None, :] / (2 * BLK)


def forward_matrix():
    th = angles(np.arange(BLK, dtype=np.float64))
    hi, lo = split_hi_lo(np.concatenate([np.cos(th), -np.sin(th)], 0))
    return np.concatenate([hi, lo], 1)


def inverse_matrix(start):
    th = angles(np.arange(start, start + BLK, dtype=np.float64)).T
    hi, lo = split_hi_lo(np.concatenate([np.cos(th), -np.sin(th)], 1) / BLK)
    return np.concatenate([hi, lo], 1)


def spectrum(fwd, rows):
    return jnp.dot(fwd, jnp.concatenate([rows, rows], 0), preferred_element_type=f32)


def delay(v):
    h = BLK // 2
    re, im = v[:BLK], v[BLK:]
    return jnp.concatenate([im[:h], -im[h:], -re[:h], re[h:]], 0)


def product_conj(a, b):
    ar, ai, br, bi = a[:BLK], a[BLK:], b[:BLK], b[BLK:]
    return jnp.concatenate([ar * br + ai * bi, ai * br - ar * bi], 0)


def two_parts(y):
    hi = y.astype(bf16)
    return hi, (y - hi.astype(f32)).astype(bf16)


def from_parts(inv, parts):
    matrix = jnp.concatenate([inv[...], inv[:, : 2 * BLK]], 1)
    return jnp.dot(matrix, parts, preferred_element_type=f32)


def invert(inv, y):
    hi, lo = two_parts(y)
    return from_parts(inv, jnp.concatenate([hi, hi, lo], 0))


def put_spectrum(buf, row, lanes, y):
    hi, lo = two_parts(y)
    n = y.shape[0]
    buf[row : row + n, lanes] = hi
    buf[2 * BLK + row : 2 * BLK + row + n, lanes] = hi
    buf[4 * BLK + row : 4 * BLK + row + n, lanes] = lo


def chunks(total, size):
    return [(r, min(size, total - r)) for r in range(0, total, size)]


ROWS = 32
FREQS = 16


def window_rows(spec, c, here, after):
    sr, si = slice(c, c + FREQS), slice(BLK + c, BLK + c + FREQS)
    wr, wi = spec[sr, here], spec[si, here]
    if after is None:
        return wr, wi
    ar, ai = spec[sr, after], spec[si, after]
    if c < BLK // 2:
        return wr + ai, wi - ar
    return wr - ai, wi + ar


def forward_kernel(
    proj, halo, sf, lf, skip, fwd, inv, gated, conv, act, mspec, fspec, ext, mix, spec, ybuf, out
):
    rows = proj.shape[1]
    nb, wide = rows // BLK, proj.shape[2]
    fmat = fwd[...]
    edge = halo[BLK : BLK + PAD].astype(f32)
    for m in range(3):
        ext[m, PAD - 2 : PAD] = edge[2 * m : 2 * m + 2]
        for r, n in chunks(rows, ROWS):
            ext[m, PAD + r : PAD + r + n] = proj[m, r : r + n].astype(f32)
    for h in range(2):
        mix[h * BLK : (h + 1) * BLK, :wide] = halo[:BLK]
    for r, n in chunks(rows, ROWS):
        acts = []
        for m in range(3):
            total = sf[m, 0:1] * ext[m, PAD + r : PAD + r + n]
            for s in (1, 2):
                total = total + sf[m, s : s + 1] * ext[m, PAD - s + r : PAD - s + r + n]
            act[m, r : r + n] = total
            acts.append(total)
        mixin = (acts[1] * acts[2]).astype(bf16)
        at, lane = r % BLK, (r // BLK + 1) * wide
        for h in range(2):
            mix[h * BLK + at : h * BLK + at + n, lane : lane + wide] = mixin
    filt = spectrum(fmat, lf[...])
    fspec[...] = filt
    spec[...] = jnp.dot(fmat, mix[...], preferred_element_type=f32)
    for c in range(0, BLK, FREQS):
        fr, fi = fspec[c : c + FREQS], fspec[BLK + c : BLK + c + FREQS]
        for b in range(nb):
            lanes = slice(b * wide, (b + 1) * wide)
            wr, wi = window_rows(spec, c, lanes, slice((b + 1) * wide, (b + 2) * wide))
            mspec[b, c : c + FREQS] = wr
            mspec[b, BLK + c : BLK + c + FREQS] = wi
            put_spectrum(ybuf, c, lanes, fr * wr - fi * wi)
            put_spectrum(ybuf, BLK + c, lanes, fr * wi + fi * wr)
    out[...] = from_parts(inv, ybuf[...])
    for r, n in chunks(rows, ROWS):
        at, lane = r % BLK, r // BLK * wide
        mixin = mix[at : at + n, lane + wide : lane + 2 * wide].astype(f32)
        full = out[at : at + n, lane : lane + wide] + skip[...] * mixin
        conv[r : r + n] = full
        gated[r : r + n] = (act[0, r : r + n] * full).astype(bf16)


def backward_kernel(place, acc, act0, mspec, fspec, skip, fwd, inv, invlag, *refs):
    og, refs = refs[: 2 * SIDE], refs[2 * SIDE :]
    weights, refs = refs[:4], refs[4:]
    bg, long0, long1, long2, long3, gmix, lagbuf, gbuf, spec, ybuf, lagy, out = refs
    rows, wide = bg.shape
    nb = rows // BLK
    bg[...] = acc[...] + lax.dot_general(
        jnp.concatenate([o[...] for o in og], 1),
        jnp.concatenate([w[n] for w in weights for n in range(2)], 1),
        (((1,), (1,)), ((), ())),
        preferred_element_type=f32,
    )
    for r, n in chunks(rows, ROWS):
        g = (bg[r : r + n] * act0[0, r : r + n]).astype(bf16)
        at, lane = r % BLK, r // BLK * wide
        for h in range(2):
            gbuf[h * BLK + at : h * BLK + at + n, lane : lane + wide] = g
    spec[...] = jnp.dot(fwd[...], gbuf[...], preferred_element_type=f32)
    whole = slice(0, wide)
    for c in range(0, BLK, FREQS):
        sr, si = slice(c, c + FREQS), slice(BLK + c, BLK + c + FREQS)
        fr, fi = fspec[sr], fspec[si]
        lag_r = lag_i = None
        for b in range(nb):
            lanes = slice(b * wide, (b + 1) * wide)
            after = slice((b + 1) * wide, (b + 2) * wide) if b + 1 < nb else None
            gr, gi, mr, mi = spec[sr, lanes], spec[si, lanes], mspec[b, sr], mspec[b, si]
            pr, pi = gr * mr + gi * mi, gi * mr - gr * mi
            lag_r, lag_i = (pr, pi) if b == 0 else (lag_r + pr, lag_i + pi)
            wr, wi = window_rows(spec, c, lanes, after)
            put_spectrum(ybuf, c, lanes, wr * fr + wi * fi)
            put_spectrum(ybuf, BLK + c, lanes, wi * fr - wr * fi)
        put_spectrum(lagy, c, whole, lag_r)
        put_spectrum(lagy, BLK + c, whole, lag_i)
    lagbuf[...] = from_parts(invlag, lagy[...])
    quarter = BLK // SIDE
    for k, part in enumerate((long0, long1, long2, long3)):
        start = pl.multiple_of((place[0] ^ k) * quarter, quarter)
        part[...] = lagbuf[pl.ds(start, quarter)].astype(bf16)
    out[...] = from_parts(inv, ybuf[...])
    for r, n in chunks(rows, ROWS):
        at, lane = r % BLK, r // BLK * wide
        g = gbuf[at : at + n, lane : lane + wide].astype(f32)
        gmix[r : r + n] = out[at : at + n, lane : lane + wide] + skip[...] * g


def head_kernel(place, acc, act0, act12, convh, lf, skip, *refs):
    del place
    og, refs = refs[: 2 * SIDE], refs[2 * SIDE :]
    weights, (pay, ext) = refs[:4], refs[4:]
    bg = acc[...] + lax.dot_general(
        jnp.concatenate([o[...] for o in og], 1),
        jnp.concatenate([w[n] for w in weights for n in range(2)], 1),
        (((1,), (1,)), ((), ())),
        preferred_element_type=f32,
    )
    g = (bg * act0[0]).astype(bf16)
    ext[...] = g.astype(f32)
    taps = lf[...].astype(f32)
    gm0 = jnp.sum(taps * ext[:BLK], axis=0, keepdims=True) + skip[...] * ext[0:1]
    gm1 = jnp.sum(taps * ext[1 : BLK + 1], axis=0, keepdims=True) + skip[...] * ext[1:2]
    gm = jnp.concatenate([gm0, gm1], 0)
    edge = [bg[:2] * convh[:2], gm * act12[1, :2], gm * act12[0, :2], jnp.zeros_like(gm)]
    pay[:BLK] = g[:BLK]
    pay[BLK:] = jnp.concatenate(edge, 0).astype(bf16)


def finish_body(bg, conv, gmix, act, proj, sf, extra, gp, ext):
    rows, wide = bg.shape
    sums = []
    for m in range(3):
        for r, n in chunks(rows, ROWS):
            if m == 0:
                ext[m, r : r + n] = bg[r : r + n] * conv[r : r + n]
            else:
                ext[m, r : r + n] = gmix[r : r + n] * act[2 - m, r : r + n]
        ext[m, rows : rows + PAD] = extra[m]
        parts = [jnp.zeros((8, wide), f32)] * 3
        for r, n in chunks(rows, ROWS):
            x = proj[m, r : r + n].astype(f32)
            total = None
            for s in range(3):
                moved = ext[m, r + s : r + s + n]
                term = sf[m, s : s + 1] * moved
                total = term if s == 0 else total + term
                parts[s] = parts[s] + jnp.sum((x * moved).reshape(n // 8, 8, wide), axis=0)
            gp[m, r : r + n] = total.astype(bf16)
        sums += [jnp.sum(p, axis=0, keepdims=True) for p in parts]
    return jnp.concatenate(sums + [jnp.zeros((7, wide), f32)], 0)


def top_kernel(bg, conv, gmix, act, bgn, convn, gmixn, actn, proj, sf, gp, short, ext):
    extra = [bgn[...] * convn[...], gmixn[...] * actn[1], gmixn[...] * actn[0]]
    short[...] = finish_body(bg, conv, gmix, act, proj, sf, extra, gp, ext)


def bottom_kernel(
    bg, conv, gmix, act, halo, proj, sf, fspec, fwd, inv, short_in, gp_in, gp, short, ext, gfull
):
    del gp_in
    rows = bg.shape[0]
    late = delay(spectrum(fwd[...], halo[:BLK]))
    gfull[: rows - BLK] = gmix[: rows - BLK]
    gfull[rows - BLK :] = gmix[rows - BLK :] + invert(inv, product_conj(late, fspec[...]))
    edge = halo[BLK : BLK + PAD].astype(f32)
    zeros = jnp.zeros((PAD - 2, edge.shape[1]), f32)
    extra = [jnp.concatenate([edge[2 * m : 2 * m + 2], zeros], 0) for m in range(3)]
    short[...] = short_in[...] + finish_body(bg, conv, gfull, act, proj, sf, extra, gp, ext)


def pieces_kernel(steps, back, more, *refs):
    weights, refs = refs[: 2 * steps], refs[2 * steps :]
    if back:
        gated, og, refs = refs[0], refs[1 : 1 + SIDE], refs[1 + SIDE :]
        if more:
            acc_in, refs = refs[0], refs[2:]
        result, acc, buf, sems = refs
    else:
        gated, result, buf, sems = refs
    step = pl.program_id(0)
    chans = gated.shape[1]
    width = buf.shape[2] // SIDE

    def copies(i):
        return [
            pltpu.make_async_copy(
                weights[2 * i + j // 2].at[pl.ds((j % 2) * chans, chans)],
                buf.at[i % 2, :, pl.ds(j * width, width)],
                sems.at[i % 2, j],
            )
            for j in range(SIDE)
        ]

    @pl.when(step == 0)
    def _():
        for c in copies(0):
            c.start()
        if back:
            acc[...] = acc_in[...] if more else jnp.zeros_like(acc)

    for i in range(steps):

        @pl.when(step == i)
        def _(i=i):
            if i + 1 < steps:
                for c in copies(i + 1):
                    c.start()
            for c in copies(i):
                c.wait()

    w = buf[step % 2]
    result[...] = jnp.dot(gated[...], w, preferred_element_type=f32).astype(bf16)
    if back:
        acc[...] += lax.dot_general(
            jnp.concatenate([o[...] for o in og], 1),
            w,
            (((1,), (1,)), ((), ())),
            preferred_element_type=f32,
        )


def multiply_pieces(weights, cols, gated, out_grad=None, total=None, before=None):
    rows, chans = gated.shape
    width = weights[0].shape[1]
    steps = len(weights) // 2
    back, more = out_grad is not None, before is not None
    total = total or steps
    offset = before[0] if more else 0
    whole = pl.BlockSpec((rows, chans), lambda i, c: (0, 0), pipeline_mode=pl.Buffered(1))
    in_specs = [pl.BlockSpec(memory_space=pl.ANY)] * len(weights) + [whole]
    operands = [*weights, gated]
    aliases = {}
    if back:
        in_specs += [
            pl.BlockSpec((rows, width), lambda i, c, j=j: (0, c[SIDE * i + j])) for j in range(SIDE)
        ]
        operands += [out_grad] * SIDE
        if more:
            in_specs += [whole, pl.BlockSpec(memory_space=pl.ANY)]
            operands += [before[2], before[1]]
            aliases = {len(operands): 0}
    result_shape = jax.ShapeDtypeStruct((rows, total * SIDE * width), bf16)
    result_spec = pl.BlockSpec((rows, SIDE * width), lambda i, c: (0, i + offset))

    def kernel(cols_ref, *refs):
        del cols_ref
        pieces_kernel(steps, back, more, *refs)

    return pl.pallas_call(
        kernel,
        grid_spec=pltpu.PrefetchScalarGridSpec(
            num_scalar_prefetch=1,
            grid=(steps,),
            in_specs=in_specs,
            out_specs=[result_spec] + [whole] * back,
            scratch_shapes=[
                pltpu.VMEM((2, chans, SIDE * width), bf16),
                pltpu.SemaphoreType.DMA((2, SIDE)),
            ],
        ),
        out_shape=[result_shape] + [jax.ShapeDtypeStruct((rows, chans), f32)] * back,
        input_output_aliases=aliases,
        cost_estimate=pl.CostEstimate(
            flops=(2 + 2 * back) * rows * chans * width * SIDE * steps,
            bytes_accessed=SIDE * steps * (2 * chans * width + 4 * rows * width) + 6 * rows * chans,
            transcendentals=0,
        ),
        name="pieces",
    )(cols, *operands)


def collect_kernel(counts, cols, *refs):
    mixed = refs[-1]
    width = mixed.shape[1] // sum(counts)
    begin = 0
    for ref, count in zip(refs, counts):

        @pl.loop(0, count)
        def _(p, ref=ref, begin=begin):
            lanes = pl.ds(pl.multiple_of(p * width, width), width)
            start = pl.multiple_of(cols[begin + p] * width, width)
            mixed[:, pl.ds(start, width)] = ref[:, lanes]

        begin += count


def on_device(projected, short_filter, long_filter, skip_gain, out_weight, out_grad, left_source):
    rows, chans = projected.shape[1:]
    width = out_weight.shape[1] // 2
    ctx_count, tp_count = lax.axis_size("ctx"), lax.axis_size("tp")
    me = lax.axis_index("ctx")
    zi, xi = me // SIDE, me % SIDE

    def ring(value, axis, step):
        if axis == "x":
            pairs = [(d, d // SIDE * SIDE + (d + step) % SIDE) for d in range(ctx_count)]
        else:
            pairs = [(d, (d + SIDE * step) % ctx_count) for d in range(ctx_count)]
        return lax.ppermute(value, "ctx", pairs)

    def swap(value, axis, k):
        shift = {"x": k, "z": k * SIDE}[axis]
        return lax.ppermute(value, "ctx", [(d, d ^ shift) for d in range(ctx_count)])

    def gather(piece, first, second):
        h = piece.shape[0] // 2
        p, q = ring(piece, first, 1), ring(piece, first, -1)
        t, b = ring(p[:h], first, 1), ring(q[h:], first, -1)
        one, two = jnp.concatenate([piece, p], 0), jnp.concatenate([q, t, b], 0)
        op, oq = ring(one, second, 1), ring(one, second, -1)
        tp_, tq = ring(two, second, 1), ring(two, second, -1)
        far_one = ring(op, second, 1)
        far_two = ring(tq, second, -1)
        return [one, two], [op, tp_, oq, tq], [far_one, far_two]

    def blocks(half, near, far_steps):
        out = []
        for f in far_steps:
            for n in near:
                z, x = (f, n) if half == 0 else (n, f)
                out.append(2 * ((zi + z) % SIDE * SIDE + (xi + x) % SIDE) + half)
        return out

    order4 = (0, -1, 1, 2)
    cols1 = jnp.stack(blocks(0, order4, (0,)) + blocks(1, order4, (0,)))
    cols2 = jnp.stack(blocks(0, order4, (-1, 1)) + blocks(1, order4, (-1, 1)))
    cols3 = jnp.stack(blocks(0, order4, (2,)) + blocks(1, order4, (2,)))

    positions = jnp.arange(ctx_count, dtype=jnp.int32)
    matches = left_source[None, :] == positions[:, None]
    readers = jnp.where(
        jnp.any(matches, 1), jnp.sum(jnp.where(matches, positions[None, :], 0), 1), -1
    )

    def pick(options, index):
        low = jnp.where(index == 1, options[1], options[0])
        high = jnp.where(index == 3, options[3], options[2])
        return jnp.where(index >= 2, high, low)

    def at(table, index):
        return lax.dynamic_index_in_dim(table, index, 0, keepdims=False)

    def along_x(payloads):
        return [payloads[0]] + [swap(payloads[k], "x", k) for k in (1, 2, 3)]

    def along_z(payloads):
        return [payloads[0]] + [swap(payloads[k], "z", k) for k in (1, 2, 3)]

    def chosen(got, table):
        out = []
        for k in range(SIDE):
            source = jnp.maximum(at(table, (zi ^ k) * SIDE + xi), 0)
            out.append(pick(got, (source % SIDE) ^ xi))
        return out

    def landed(got, table):
        source = at(table, me)
        value = pick(got, (jnp.maximum(source, 0) // SIDE) ^ zi)
        return jnp.where(source >= 0, value, jnp.zeros_like(value))

    near = projected[1:, rows - BLK - PAD :].astype(f32)
    tail = jnp.zeros((2, BLK, chans), f32)
    for s in range(3):
        tail = tail + short_filter[1:, s][:, None] * near[:, PAD - s : PAD - s + BLK]
    raw = projected[:, rows - 2 :].reshape(6, chans)
    sent = jnp.concatenate(
        [(tail[0] * tail[1]).astype(bf16), raw, jnp.zeros((2, chans), bf16)], 0
    )
    got = along_x([sent] * SIDE)
    to_z = chosen(got, left_source)
    got = along_z(to_z)
    left = landed(got, left_source)

    near_a, mid_a, far_a = gather(out_weight[:, :width], "x", "z")
    near_b, mid_b, far_b = gather(out_weight[:, width:], "z", "x")

    fwd = jnp.asarray(forward_matrix())
    inv_late, inv_now, inv_lag = (jnp.asarray(inverse_matrix(s)) for s in (BLK, 0, -BLK))
    skip_row = skip_gain[None, :]
    tile = 256
    grid = (chans // tile,)
    nb = rows // BLK

    def col(*lead):
        return pl.BlockSpec((*lead, tile), lambda i, *_: (*([0] * len(lead)), i))

    const = pl.BlockSpec((2 * BLK, 2 * BLK), lambda i, *_: (0, 0))
    const_inv = pl.BlockSpec((BLK, 4 * BLK), lambda i, *_: (0, 0))
    forward = pl.pallas_call(
        forward_kernel,
        grid=grid,
        in_specs=[
            col(3, rows), col(BLK + PAD), col(3, 3), col(BLK), col(1), const, const_inv,
        ],
        out_specs=[col(rows), col(rows), col(3, rows), col(nb, 2 * BLK), col(2 * BLK)],
        scratch_shapes=[
            pltpu.VMEM((3, rows + PAD, tile), f32),
            pltpu.VMEM((2 * BLK, (nb + 1) * tile), bf16),
            pltpu.VMEM((2 * BLK, (nb + 1) * tile), f32),
            pltpu.VMEM((6 * BLK, nb * tile), bf16),
            pltpu.VMEM((BLK, nb * tile), f32),
        ],
        out_shape=[
            jax.ShapeDtypeStruct((rows, chans), bf16),
            jax.ShapeDtypeStruct((rows, chans), f32),
            jax.ShapeDtypeStruct((3, rows, chans), f32),
            jax.ShapeDtypeStruct((nb, 2 * BLK, chans), f32),
            jax.ShapeDtypeStruct((2 * BLK, chans), f32),
        ],
        cost_estimate=pl.CostEstimate(
            flops=8_000_000_000, bytes_accessed=20 << 20, transcendentals=0
        ),
        name="forward",
    )
    gated, conv, act, mspec, fspec = forward(
        projected, left, short_filter, long_filter, skip_row, fwd, inv_late
    )

    def scatter(value):
        return lax.psum_scatter(value, "tp", scatter_dimension=0, tiled=True)

    early = multiply_pieces(near_a + near_b, cols1, gated, out_grad, 6)
    out1, acc = multiply_pieces(
        mid_a + mid_b, cols2, gated, out_grad, 6, (2, *early)
    )
    out1 = scatter(out1)

    quarter = BLK // SIDE
    place = jnp.concatenate([jnp.reshape(zi, (1,)), cols3]).astype(jnp.int32)
    lasts = [w.reshape(2, chans, width) for w in far_a + far_b]
    last_spec = pl.BlockSpec((2, tile, width), lambda i, c: (0, i, 0))

    def out_grad_rows(n):
        return [pl.BlockSpec((n, width), lambda i, c, j=j: (0, c[1 + j])) for j in range(2 * SIDE)]

    def first_rows(n, *lead):
        zeros = [0] * len(lead)
        return pl.BlockSpec((*lead, n, tile), lambda i, c: (*zeros, 0, i))

    head = pl.pallas_call(
        head_kernel,
        grid_spec=pltpu.PrefetchScalarGridSpec(
            num_scalar_prefetch=1,
            grid=grid,
            in_specs=[
                first_rows(BLK + PAD),
                first_rows(BLK + PAD, 1),
                pl.BlockSpec(
                    (pl.Element(2), pl.Element(PAD), pl.Element(tile)),
                    lambda i, c: (1, 0, i * tile),
                ),
                first_rows(PAD),
                col(BLK),
                col(1),
                *out_grad_rows(BLK + PAD),
                *[last_spec] * 4,
            ],
            out_specs=col(BLK + PAD),
            scratch_shapes=[pltpu.VMEM((BLK + PAD, tile), f32)],
        ),
        out_shape=jax.ShapeDtypeStruct((BLK + PAD, chans), bf16),
        cost_estimate=pl.CostEstimate(
            flops=600_000_000, bytes_accessed=6 << 20, transcendentals=0
        ),
        name="head",
    )
    pay = head(place, acc, act, act, conv, long_filter, skip_row, *[out_grad] * (2 * SIDE), *lasts)
    got = along_x([pay] * SIDE)

    long_shape = jax.ShapeDtypeStruct((quarter, chans), bf16)
    backward = pl.pallas_call(
        backward_kernel,
        grid_spec=pltpu.PrefetchScalarGridSpec(
            num_scalar_prefetch=1,
            grid=grid,
            in_specs=[
                col(rows),
                first_rows(rows, 1),
                col(nb, 2 * BLK),
                col(2 * BLK),
                col(1),
                const,
                const_inv,
                const_inv,
                *out_grad_rows(rows),
                *[last_spec] * 4,
            ],
            out_specs=[col(rows)] + [col(quarter)] * 4 + [col(rows)],
            scratch_shapes=[
                pltpu.VMEM((BLK, tile), f32),
                pltpu.VMEM((2 * BLK, nb * tile), bf16),
                pltpu.VMEM((2 * BLK, nb * tile), f32),
                pltpu.VMEM((6 * BLK, nb * tile), bf16),
                pltpu.VMEM((6 * BLK, tile), bf16),
                pltpu.VMEM((BLK, nb * tile), f32),
            ],
        ),
        out_shape=[jax.ShapeDtypeStruct((rows, chans), f32)]
        + [long_shape] * 4
        + [jax.ShapeDtypeStruct((rows, chans), f32)],
        cost_estimate=pl.CostEstimate(
            flops=8_000_000_000, bytes_accessed=20 << 20, transcendentals=0
        ),
        name="backward",
    )
    bg, *longs, gmix = backward(
        place, acc, act, mspec, fspec, skip_row, fwd, inv_now, inv_lag,
        *[out_grad] * (2 * SIDE), *lasts,
    )

    to_z = chosen(got, readers)
    got = along_z([jnp.concatenate([v, part], 0) for v, part in zip(to_z, longs)])
    right = landed([g[: BLK + PAD] for g in got], readers)
    sums = [g[BLK + PAD :].astype(f32) for g in got]
    my_quarter = (sums[0] + sums[1]) + (sums[2] + sums[3])

    (out3,) = multiply_pieces(far_a + far_b, cols3, gated)
    out3 = scatter(out3)

    low = rows - BLK - PAD

    def rows_at(start, n, *lead):
        zeros = [0] * len(lead)
        dims = [pl.Element(d) for d in (*lead, n, tile)]
        return pl.BlockSpec(tuple(dims), lambda i: (*zeros, start, i * tile))

    def acts_at(start, n):
        return pl.BlockSpec(
            (pl.Element(2), pl.Element(n), pl.Element(tile)), lambda i: (1, start, i * tile)
        )

    gp_shape = jax.ShapeDtypeStruct((3, rows, chans), bf16)
    short_shape = jax.ShapeDtypeStruct((16, chans), f32)
    top = pl.pallas_call(
        top_kernel,
        grid=grid,
        in_specs=[
            rows_at(0, low), rows_at(0, low), rows_at(0, low), acts_at(0, low),
            rows_at(low, PAD), rows_at(low, PAD), rows_at(low, PAD), acts_at(low, PAD),
            rows_at(0, low, 3), col(3, 3),
        ],
        out_specs=[rows_at(0, low, 3), col(16)],
        out_shape=[gp_shape, short_shape],
        scratch_shapes=[pltpu.VMEM((3, low + PAD, tile), f32)],
        cost_estimate=pl.CostEstimate(
            flops=200_000_000, bytes_accessed=10 << 20, transcendentals=0
        ),
        name="top",
    )
    gp, short = top(bg, conv, gmix, act, bg, conv, gmix, act, projected, short_filter)
    rest = rows - low
    bottom = pl.pallas_call(
        bottom_kernel,
        grid=grid,
        in_specs=[
            rows_at(low, rest), rows_at(low, rest), rows_at(low, rest), acts_at(low, rest),
            col(BLK + PAD), rows_at(low, rest, 3), col(3, 3), col(2 * BLK), const, const_inv, col(16),
            pl.BlockSpec(memory_space=pl.ANY),
        ],
        out_specs=[rows_at(low, rest, 3), col(16)],
        out_shape=[gp_shape, short_shape],
        scratch_shapes=[pltpu.VMEM((3, rest + PAD, tile), f32), pltpu.VMEM((rest, tile), f32)],
        input_output_aliases={11: 0},
        cost_estimate=pl.CostEstimate(
            flops=2_000_000_000, bytes_accessed=5 << 20, transcendentals=0
        ),
        name="bottom",
    )
    gp, short = bottom(
        bg, conv, gmix, act, right, projected, short_filter, fspec, fwd, inv_now, short, gp
    )

    message = jnp.concatenate([my_quarter, short], 0)
    for along in (along_x, along_z):
        got = along([message.astype(bf16)] * SIDE)
        wide = [g.astype(f32) for g in got]
        message = (wide[0] + wide[1]) + (wide[2] + wide[3])
    long_total = jnp.concatenate([pick(got, zi ^ q)[:quarter] for q in range(SIDE)], 0)
    short_total = message[quarter : quarter + 9].reshape(3, 3, chans)

    share = rows // tp_count
    counts = tuple(o.shape[1] // width for o in (out1, out3))
    collect = pl.pallas_call(
        lambda cols, *refs: collect_kernel(counts, cols, *refs),
        grid_spec=pltpu.PrefetchScalarGridSpec(
            num_scalar_prefetch=1,
            grid=(1,),
            in_specs=[pl.BlockSpec(o.shape, lambda i, c: (0, 0)) for o in (out1, out3)],
            out_specs=pl.BlockSpec((share, 2 * width * ctx_count), lambda i, c: (0, 0)),
        ),
        out_shape=jax.ShapeDtypeStruct((share, 2 * width * ctx_count), bf16),
        cost_estimate=pl.CostEstimate(flops=10_000_000, bytes_accessed=5 << 20, transcendentals=0),
        name="collect",
    )
    mixed = collect(jnp.concatenate([cols1, cols2, cols3]), out1, out3)

    scale = 1.0 / math.sqrt(rows * ctx_count)
    return mixed, gp, long_total.astype(f32) * scale, short_total * scale


def solution(mesh):
    placed = (
        P(None, "ctx", "tp"),
        P(None, None, "tp"),
        P(None, "tp"),
        P("tp"),
        P("tp", "ctx"),
        P("ctx", None),
        P(),
    )
    return jax.shard_map(
        on_device,
        mesh=mesh,
        in_specs=placed,
        out_specs=(
            P(("ctx", "tp"), None),
            P(None, "ctx", "tp"),
            P(None, "tp"),
            P(None, None, "tp"),
        ),
        check_vma=False,
    )
```

```python
import math

import jax
import jax.numpy as jnp
import numpy as np
from jax import lax
from jax.experimental import pallas as pl
from jax.experimental.pallas import tpu as pltpu
from jax.sharding import PartitionSpec as P


f32, bf16 = jnp.float32, jnp.bfloat16
BLK = 128
SIDE = 4
PAD = 8


def split_hi_lo(matrix):
    hi = matrix.astype(np.float32).astype(bf16)
    lo = (matrix - hi.astype(np.float64)).astype(np.float32).astype(bf16)
    return hi, lo


def angles(times):
    freqs = np.concatenate([np.arange(0, BLK, 2), np.arange(1, BLK, 2)]) + 0.5
    return 2.0 * np.pi * freqs[:, None] * times[None, :] / (2 * BLK)


def forward_matrix():
    th = angles(np.arange(BLK, dtype=np.float64))
    hi, lo = split_hi_lo(np.concatenate([np.cos(th), -np.sin(th)], 0))
    return np.concatenate([hi, lo], 1)


def inverse_matrix(start):
    th = angles(np.arange(start, start + BLK, dtype=np.float64)).T
    return (np.concatenate([np.cos(th), -np.sin(th)], 1) / BLK).astype(np.float32).astype(bf16)


def spectrum(fwd, rows):
    return jnp.dot(fwd, jnp.concatenate([rows, rows], 0), preferred_element_type=f32)


def delay(v):
    h = BLK // 2
    re, im = v[:BLK], v[BLK:]
    return jnp.concatenate([im[:h], -im[h:], -re[:h], re[h:]], 0)


def product_conj(a, b):
    ar, ai, br, bi = a[:BLK], a[BLK:], b[:BLK], b[BLK:]
    return jnp.concatenate([ar * br + ai * bi, ai * br - ar * bi], 0)


def invert(inv, spec):
    return jnp.dot(inv[...], spec, preferred_element_type=f32)


def chunks(total, size):
    return [(r, min(size, total - r)) for r in range(0, total, size)]


ROWS = 32
FREQS = 16


def window_rows(spec, c, here, after):
    sr, si = slice(c, c + FREQS), slice(BLK + c, BLK + c + FREQS)
    wr, wi = spec[sr, here], spec[si, here]
    if after is None:
        return wr, wi
    ar, ai = spec[sr, after], spec[si, after]
    if c < BLK // 2:
        return wr + ai, wi - ar
    return wr - ai, wi + ar


def forward_kernel(
    proj, halo, sf, lf, skip, fwd, inv, gated, conv, act, mspec, fspec, ext, mix, spec, ybuf, out
):
    rows = proj.shape[1]
    nb, wide = rows // BLK, proj.shape[2]
    fmat = fwd[...]
    edge = halo[BLK : BLK + PAD].astype(f32)
    for m in range(3):
        ext[m, PAD - 2 : PAD] = edge[2 * m : 2 * m + 2]
        for r, n in chunks(rows, ROWS):
            ext[m, PAD + r : PAD + r + n] = proj[m, r : r + n].astype(f32)
    for h in range(2):
        mix[h * BLK : (h + 1) * BLK, :wide] = halo[:BLK]
    for r, n in chunks(rows, ROWS):
        acts = []
        for m in range(3):
            total = sf[m, 0:1] * ext[m, PAD + r : PAD + r + n]
            for s in (1, 2):
                total = total + sf[m, s : s + 1] * ext[m, PAD - s + r : PAD - s + r + n]
            act[m, r : r + n] = total
            acts.append(total)
        mixin = (acts[1] * acts[2]).astype(bf16)
        at, lane = r % BLK, (r // BLK + 1) * wide
        for h in range(2):
            mix[h * BLK + at : h * BLK + at + n, lane : lane + wide] = mixin
    filt = spectrum(fmat, lf[...])
    fspec[...] = filt
    spec[...] = jnp.dot(fmat, mix[...], preferred_element_type=f32)
    for c in range(0, BLK, FREQS):
        fr, fi = fspec[c : c + FREQS], fspec[BLK + c : BLK + c + FREQS]
        for b in range(nb):
            lanes = slice(b * wide, (b + 1) * wide)
            wr, wi = window_rows(spec, c, lanes, slice((b + 1) * wide, (b + 2) * wide))
            mspec[b, c : c + FREQS] = wr
            mspec[b, BLK + c : BLK + c + FREQS] = wi
            ybuf[c : c + FREQS, lanes] = (fr * wr - fi * wi).astype(bf16)
            ybuf[BLK + c : BLK + c + FREQS, lanes] = (fr * wi + fi * wr).astype(bf16)
    out[...] = invert(inv, ybuf[...])
    for r, n in chunks(rows, ROWS):
        at, lane = r % BLK, r // BLK * wide
        mixin = mix[at : at + n, lane + wide : lane + 2 * wide].astype(f32)
        full = out[at : at + n, lane : lane + wide] + skip[...] * mixin
        conv[r : r + n] = full
        gated[r : r + n] = (act[0, r : r + n] * full).astype(bf16)


def backward_kernel(place, acc, act0, mspec, fspec, skip, fwd, inv, invlag, *refs):
    og, refs = refs[: 2 * SIDE], refs[2 * SIDE :]
    weights, refs = refs[:4], refs[4:]
    bg, long0, long1, long2, long3, gmix, lagbuf, gbuf, spec, ybuf, lagy, out = refs
    rows, wide = bg.shape
    nb = rows // BLK
    bg[...] = acc[...] + lax.dot_general(
        jnp.concatenate([o[...] for o in og], 1),
        jnp.concatenate([w[n] for w in weights for n in range(2)], 1),
        (((1,), (1,)), ((), ())),
        preferred_element_type=f32,
    )
    for r, n in chunks(rows, ROWS):
        g = (bg[r : r + n] * act0[0, r : r + n]).astype(bf16)
        at, lane = r % BLK, r // BLK * wide
        for h in range(2):
            gbuf[h * BLK + at : h * BLK + at + n, lane : lane + wide] = g
    spec[...] = jnp.dot(fwd[...], gbuf[...], preferred_element_type=f32)
    for c in range(0, BLK, FREQS):
        sr, si = slice(c, c + FREQS), slice(BLK + c, BLK + c + FREQS)
        fr, fi = fspec[sr], fspec[si]
        lag_r = lag_i = None
        for b in range(nb):
            lanes = slice(b * wide, (b + 1) * wide)
            after = slice((b + 1) * wide, (b + 2) * wide) if b + 1 < nb else None
            gr, gi, mr, mi = spec[sr, lanes], spec[si, lanes], mspec[b, sr], mspec[b, si]
            pr, pi = gr * mr + gi * mi, gi * mr - gr * mi
            lag_r, lag_i = (pr, pi) if b == 0 else (lag_r + pr, lag_i + pi)
            wr, wi = window_rows(spec, c, lanes, after)
            ybuf[sr, lanes] = (wr * fr + wi * fi).astype(bf16)
            ybuf[si, lanes] = (wi * fr - wr * fi).astype(bf16)
        lagy[sr] = lag_r.astype(bf16)
        lagy[si] = lag_i.astype(bf16)
    lagbuf[...] = invert(invlag, lagy[...])
    quarter = BLK // SIDE
    for k, part in enumerate((long0, long1, long2, long3)):
        start = pl.multiple_of((place[0] ^ k) * quarter, quarter)
        part[...] = lagbuf[pl.ds(start, quarter)].astype(bf16)
    out[...] = invert(inv, ybuf[...])
    for r, n in chunks(rows, ROWS):
        at, lane = r % BLK, r // BLK * wide
        g = gbuf[at : at + n, lane : lane + wide].astype(f32)
        gmix[r : r + n] = out[at : at + n, lane : lane + wide] + skip[...] * g


def head_kernel(place, acc, act0, act12, convh, lf, skip, *refs):
    del place
    og, refs = refs[: 2 * SIDE], refs[2 * SIDE :]
    weights, (pay, ext) = refs[:4], refs[4:]
    bg = acc[...] + lax.dot_general(
        jnp.concatenate([o[...] for o in og], 1),
        jnp.concatenate([w[n] for w in weights for n in range(2)], 1),
        (((1,), (1,)), ((), ())),
        preferred_element_type=f32,
    )
    g = (bg * act0[0]).astype(bf16)
    ext[...] = g.astype(f32)
    taps = lf[...].astype(f32)
    gm0 = jnp.sum(taps * ext[:BLK], axis=0, keepdims=True) + skip[...] * ext[0:1]
    gm1 = jnp.sum(taps * ext[1 : BLK + 1], axis=0, keepdims=True) + skip[...] * ext[1:2]
    gm = jnp.concatenate([gm0, gm1], 0)
    edge = [bg[:2] * convh[:2], gm * act12[1, :2], gm * act12[0, :2], jnp.zeros_like(gm)]
    pay[:BLK] = g[:BLK]
    pay[BLK:] = jnp.concatenate(edge, 0).astype(bf16)


def finish_body(bg, conv, gmix, act, proj, sf, extra, gp, ext):
    rows, wide = bg.shape
    sums = []
    for m in range(3):
        for r, n in chunks(rows, ROWS):
            if m == 0:
                ext[m, r : r + n] = bg[r : r + n] * conv[r : r + n]
            else:
                ext[m, r : r + n] = gmix[r : r + n] * act[2 - m, r : r + n]
        ext[m, rows : rows + PAD] = extra[m]
        parts = [jnp.zeros((8, wide), f32)] * 3
        for r, n in chunks(rows, ROWS):
            x = proj[m, r : r + n].astype(f32)
            total = None
            for s in range(3):
                moved = ext[m, r + s : r + s + n]
                term = sf[m, s : s + 1] * moved
                total = term if s == 0 else total + term
                parts[s] = parts[s] + jnp.sum((x * moved).reshape(n // 8, 8, wide), axis=0)
            gp[m, r : r + n] = total.astype(bf16)
        sums += [jnp.sum(p, axis=0, keepdims=True) for p in parts]
    return jnp.concatenate(sums + [jnp.zeros((7, wide), f32)], 0)


def top_kernel(bg, conv, gmix, act, bgn, convn, gmixn, actn, proj, sf, gp, short, ext):
    extra = [bgn[...] * convn[...], gmixn[...] * actn[1], gmixn[...] * actn[0]]
    short[...] = finish_body(bg, conv, gmix, act, proj, sf, extra, gp, ext)


def bottom_kernel(
    bg, conv, gmix, act, halo, proj, sf, fspec, fwd, inv, short_in, gp_in, gp, short, ext, gfull
):
    del gp_in
    rows = bg.shape[0]
    late = delay(spectrum(fwd[...], halo[:BLK]))
    gfull[: rows - BLK] = gmix[: rows - BLK]
    gfull[rows - BLK :] = gmix[rows - BLK :] + invert(inv, product_conj(late, fspec[...]).astype(bf16))
    edge = halo[BLK : BLK + PAD].astype(f32)
    zeros = jnp.zeros((PAD - 2, edge.shape[1]), f32)
    extra = [jnp.concatenate([edge[2 * m : 2 * m + 2], zeros], 0) for m in range(3)]
    short[...] = short_in[...] + finish_body(bg, conv, gfull, act, proj, sf, extra, gp, ext)


def pieces_kernel(steps, per, back, more, *refs):
    count = steps * per // 2
    weights, refs = refs[:count], refs[count:]
    if back:
        gated, og, refs = refs[0], refs[1 : 1 + per], refs[1 + per :]
        if more:
            acc_in, refs = refs[0], refs[2:]
        result, acc, buf, sems = refs
    else:
        gated, result, buf, sems = refs
    step = pl.program_id(0)
    chans = gated.shape[1]
    width = buf.shape[2] // per

    def copies(i):
        return [
            pltpu.make_async_copy(
                weights[(per * i + j) // 2].at[pl.ds((per * i + j) % 2 * chans, chans)],
                buf.at[i % 2, :, pl.ds(j * width, width)],
                sems.at[i % 2, j],
            )
            for j in range(per)
        ]

    @pl.when(step == 0)
    def _():
        for c in copies(0):
            c.start()
        if back:
            acc[...] = acc_in[...] if more else jnp.zeros_like(acc)

    for i in range(steps):

        @pl.when(step == i)
        def _(i=i):
            if i + 1 < steps:
                for c in copies(i + 1):
                    c.start()
            for c in copies(i):
                c.wait()

    w = buf[step % 2]
    result[...] = jnp.dot(gated[...], w, preferred_element_type=f32).astype(bf16)
    if back:
        acc[...] += lax.dot_general(
            jnp.concatenate([o[...] for o in og], 1),
            w,
            (((1,), (1,)), ((), ())),
            preferred_element_type=f32,
        )


def multiply_pieces(weights, table, gated, out_grad=None, total=None, before=None, per=SIDE):
    rows, chans = gated.shape
    width = weights[0].shape[1]
    steps = 2 * len(weights) // per
    back, more = out_grad is not None, before is not None
    total = total or steps
    offset = before[0] if more else 0
    whole = pl.BlockSpec((rows, chans), lambda i, c: (0, 0), pipeline_mode=pl.Buffered(1))
    in_specs = [pl.BlockSpec(memory_space=pl.ANY)] * len(weights) + [whole]
    operands = [*weights, gated]
    aliases = {}
    if back:
        in_specs += [
            pl.BlockSpec((rows, width), lambda i, c, j=j: (0, c[1 + per * (i + offset) + j])) for j in range(per)
        ]
        operands += [out_grad] * per
        if more:
            in_specs += [whole, pl.BlockSpec(memory_space=pl.ANY)]
            operands += [before[2], before[1]]
            aliases = {len(operands): 0}
    result_shape = jax.ShapeDtypeStruct((rows, total * per * width), bf16)
    result_spec = pl.BlockSpec((rows, per * width), lambda i, c: (0, i + offset))

    def kernel(cols_ref, *refs):
        del cols_ref
        pieces_kernel(steps, per, back, more, *refs)

    return pl.pallas_call(
        kernel,
        grid_spec=pltpu.PrefetchScalarGridSpec(
            num_scalar_prefetch=1,
            grid=(steps,),
            in_specs=in_specs,
            out_specs=[result_spec] + [whole] * back,
            scratch_shapes=[
                pltpu.VMEM((2, chans, per * width), bf16),
                pltpu.SemaphoreType.DMA((2, per)),
            ],
        ),
        out_shape=[result_shape] + [jax.ShapeDtypeStruct((rows, chans), f32)] * back,
        input_output_aliases=aliases,
        cost_estimate=pl.CostEstimate(
            flops=(2 + 2 * back) * rows * chans * width * per * steps,
            bytes_accessed=per * steps * (2 * chans * width + 4 * rows * width) + 6 * rows * chans,
            transcendentals=0,
        ),
        name="pieces",
    )(table, *operands)


def collect_kernel(counts, cols, *refs):
    mixed = refs[-1]
    width = mixed.shape[1] // sum(counts)
    begin = 0
    for ref, count in zip(refs, counts):

        @pl.loop(0, count)
        def _(p, ref=ref, begin=begin):
            lanes = pl.ds(pl.multiple_of(p * width, width), width)
            start = pl.multiple_of(cols[1 + begin + p] * width, width)
            mixed[:, pl.ds(start, width)] = ref[:, lanes]

        begin += count


def on_device(projected, short_filter, long_filter, skip_gain, out_weight, out_grad, left_source):
    rows, chans = projected.shape[1:]
    width = out_weight.shape[1] // 2
    ctx_count, tp_count = lax.axis_size("ctx"), lax.axis_size("tp")
    me = lax.axis_index("ctx")
    zi, xi = me // SIDE, me % SIDE

    def ring(value, axis, step):
        if axis == "x":
            pairs = [(d, d // SIDE * SIDE + (d + step) % SIDE) for d in range(ctx_count)]
        else:
            pairs = [(d, (d + SIDE * step) % ctx_count) for d in range(ctx_count)]
        return lax.ppermute(value, "ctx", pairs)

    def swap(value, axis, k):
        shift = {"x": k, "z": k * SIDE}[axis]
        return lax.ppermute(value, "ctx", [(d, d ^ shift) for d in range(ctx_count)])

    def gather(piece, first, second):
        h = piece.shape[0] // 2
        p, q = ring(piece, first, 1), ring(piece, first, -1)
        t, b = ring(p[:h], first, 1), ring(q[h:], first, -1)
        one, two = jnp.concatenate([piece, p], 0), jnp.concatenate([q, t, b], 0)
        op, oq = ring(one, second, 1), ring(one, second, -1)
        tp_, tq = ring(two, second, 1), ring(two, second, -1)
        far_one = ring(op, second, 1)
        far_two = ring(tq, second, -1)
        return [one, two], [op, tp_, oq, tq], [far_one, far_two]

    def blocks(half, near, far_steps):
        steps = [(f, n) if half == 0 else (n, f) for f in far_steps for n in near]
        return [(half, z, x) for z, x in steps]

    order4 = (0, -1, 1, 2)
    halves, dz, dx = np.array(
        [b for far in ((0,), (-1, 1), (2,)) for half in (0, 1) for b in blocks(half, order4, far)]
    ).T
    table = 2 * ((zi + dz) % SIDE * SIDE + (xi + dx) % SIDE) + halves
    table = jnp.concatenate([jnp.reshape(zi, (1,)), table]).astype(jnp.int32)

    positions = jnp.arange(ctx_count, dtype=jnp.int32)
    matches = left_source[None, :] == positions[:, None]
    readers = jnp.where(
        jnp.any(matches, 1), jnp.sum(jnp.where(matches, positions[None, :], 0), 1), -1
    )

    def pick(options, index):
        low = jnp.where(index == 1, options[1], options[0])
        high = jnp.where(index == 3, options[3], options[2])
        return jnp.where(index >= 2, high, low)

    def at(table, index):
        return lax.dynamic_index_in_dim(table, index, 0, keepdims=False)

    def along_x(payloads):
        return [payloads[0]] + [swap(payloads[k], "x", k) for k in (1, 2, 3)]

    def along_z(payloads):
        return [payloads[0]] + [swap(payloads[k], "z", k) for k in (1, 2, 3)]

    def chosen(got, table):
        out = []
        for k in range(SIDE):
            source = jnp.maximum(at(table, (zi ^ k) * SIDE + xi), 0)
            out.append(pick(got, (source % SIDE) ^ xi))
        return out

    def landed(got, table):
        source = at(table, me)
        value = pick(got, (jnp.maximum(source, 0) // SIDE) ^ zi)
        return jnp.where(source >= 0, value, jnp.zeros_like(value))

    near = projected[1:, rows - BLK - PAD :].astype(f32)
    tail = jnp.zeros((2, BLK, chans), f32)
    for s in range(3):
        tail = tail + short_filter[1:, s][:, None] * near[:, PAD - s : PAD - s + BLK]
    raw = projected[:, rows - 2 :].reshape(6, chans)
    sent = jnp.concatenate(
        [(tail[0] * tail[1]).astype(bf16), raw, jnp.zeros((2, chans), bf16)], 0
    )
    got = along_x([sent] * SIDE)
    to_z = chosen(got, left_source)
    got = along_z(to_z)
    left = landed(got, left_source)

    near_a, mid_a, far_a = gather(out_weight[:, :width], "x", "z")
    near_b, mid_b, far_b = gather(out_weight[:, width:], "z", "x")

    fwd = jnp.asarray(forward_matrix())
    inv_late, inv_now, inv_lag = (jnp.asarray(inverse_matrix(s)) for s in (BLK, 0, -BLK))
    skip_row = skip_gain[None, :]
    tile = 256
    grid = (chans // tile,)
    nb = rows // BLK

    def col(*lead):
        return pl.BlockSpec((*lead, tile), lambda i, *_: (*([0] * len(lead)), i))

    const = pl.BlockSpec((2 * BLK, 2 * BLK), lambda i, *_: (0, 0))
    const_inv = pl.BlockSpec((BLK, 2 * BLK), lambda i, *_: (0, 0))
    forward = pl.pallas_call(
        forward_kernel,
        grid=grid,
        in_specs=[
            col(3, rows), col(BLK + PAD), col(3, 3), col(BLK), col(1), const, const_inv,
        ],
        out_specs=[col(rows), col(rows), col(3, rows), col(nb, 2 * BLK), col(2 * BLK)],
        scratch_shapes=[
            pltpu.VMEM((3, rows + PAD, tile), f32),
            pltpu.VMEM((2 * BLK, (nb + 1) * tile), bf16),
            pltpu.VMEM((2 * BLK, (nb + 1) * tile), f32),
            pltpu.VMEM((2 * BLK, nb * tile), bf16),
            pltpu.VMEM((BLK, nb * tile), f32),
        ],
        out_shape=[
            jax.ShapeDtypeStruct((rows, chans), bf16),
            jax.ShapeDtypeStruct((rows, chans), f32),
            jax.ShapeDtypeStruct((3, rows, chans), f32),
            jax.ShapeDtypeStruct((nb, 2 * BLK, chans), f32),
            jax.ShapeDtypeStruct((2 * BLK, chans), f32),
        ],
        cost_estimate=pl.CostEstimate(
            flops=8_000_000_000, bytes_accessed=20 << 20, transcendentals=0
        ),
        name="forward",
    )
    gated, conv, act, mspec, fspec = forward(
        projected, left, short_filter, long_filter, skip_row, fwd, inv_late
    )

    def scatter(value):
        return lax.psum_scatter(value, "tp", scatter_dimension=0, tiled=True)

    early = multiply_pieces(near_a + near_b, table, gated, out_grad, 6)
    out1, acc = multiply_pieces(
        mid_a + mid_b, table, gated, out_grad, 6, (2, *early)
    )
    out1 = scatter(out1)

    quarter = BLK // SIDE
    lasts = [w.reshape(2, chans, width) for w in far_a + far_b]
    last_spec = pl.BlockSpec((2, tile, width), lambda i, c: (0, i, 0))

    def out_grad_rows(n):
        return [pl.BlockSpec((n, width), lambda i, c, j=j: (0, c[1 + 6 * SIDE + j])) for j in range(2 * SIDE)]

    def first_rows(n, *lead):
        zeros = [0] * len(lead)
        return pl.BlockSpec((*lead, n, tile), lambda i, c: (*zeros, 0, i))

    head = pl.pallas_call(
        head_kernel,
        grid_spec=pltpu.PrefetchScalarGridSpec(
            num_scalar_prefetch=1,
            grid=grid,
            in_specs=[
                first_rows(BLK + PAD),
                first_rows(BLK + PAD, 1),
                pl.BlockSpec(
                    (pl.Element(2), pl.Element(PAD), pl.Element(tile)),
                    lambda i, c: (1, 0, i * tile),
                ),
                first_rows(PAD),
                col(BLK),
                col(1),
                *out_grad_rows(BLK + PAD),
                *[last_spec] * 4,
            ],
            out_specs=col(BLK + PAD),
            scratch_shapes=[pltpu.VMEM((BLK + PAD, tile), f32)],
        ),
        out_shape=jax.ShapeDtypeStruct((BLK + PAD, chans), bf16),
        cost_estimate=pl.CostEstimate(
            flops=600_000_000, bytes_accessed=6 << 20, transcendentals=0
        ),
        name="head",
    )
    pay = head(table, acc, act, act, conv, long_filter, skip_row, *[out_grad] * (2 * SIDE), *lasts)
    got = along_x([pay] * SIDE)

    long_shape = jax.ShapeDtypeStruct((quarter, chans), bf16)
    backward = pl.pallas_call(
        backward_kernel,
        grid_spec=pltpu.PrefetchScalarGridSpec(
            num_scalar_prefetch=1,
            grid=grid,
            in_specs=[
                col(rows),
                first_rows(rows, 1),
                col(nb, 2 * BLK),
                col(2 * BLK),
                col(1),
                const,
                const_inv,
                const_inv,
                *out_grad_rows(rows),
                *[last_spec] * 4,
            ],
            out_specs=[col(rows)] + [col(quarter)] * 4 + [col(rows)],
            scratch_shapes=[
                pltpu.VMEM((BLK, tile), f32),
                pltpu.VMEM((2 * BLK, nb * tile), bf16),
                pltpu.VMEM((2 * BLK, nb * tile), f32),
                pltpu.VMEM((2 * BLK, nb * tile), bf16),
                pltpu.VMEM((2 * BLK, tile), bf16),
                pltpu.VMEM((BLK, nb * tile), f32),
            ],
        ),
        out_shape=[jax.ShapeDtypeStruct((rows, chans), f32)]
        + [long_shape] * 4
        + [jax.ShapeDtypeStruct((rows, chans), f32)],
        cost_estimate=pl.CostEstimate(
            flops=8_000_000_000, bytes_accessed=20 << 20, transcendentals=0
        ),
        name="backward",
    )
    bg, *longs, gmix = backward(
        table, acc, act, mspec, fspec, skip_row, fwd, inv_now, inv_lag,
        *[out_grad] * (2 * SIDE), *lasts,
    )

    to_z = chosen(got, readers)
    got = along_z([jnp.concatenate([v, part], 0) for v, part in zip(to_z, longs)])
    right = landed([g[: BLK + PAD] for g in got], readers)
    sums = [g[BLK + PAD :].astype(f32) for g in got]
    my_quarter = (sums[0] + sums[1]) + (sums[2] + sums[3])

    (out3,) = multiply_pieces(far_a + far_b, table, gated, per=2)
    out3 = scatter(out3)

    low = rows - BLK - PAD

    def rows_at(start, n, *lead):
        zeros = [0] * len(lead)
        dims = [pl.Element(d) for d in (*lead, n, tile)]
        return pl.BlockSpec(tuple(dims), lambda i: (*zeros, start, i * tile))

    def acts_at(start, n):
        return pl.BlockSpec(
            (pl.Element(2), pl.Element(n), pl.Element(tile)), lambda i: (1, start, i * tile)
        )

    gp_shape = jax.ShapeDtypeStruct((3, rows, chans), bf16)
    short_shape = jax.ShapeDtypeStruct((16, chans), f32)
    top = pl.pallas_call(
        top_kernel,
        grid=grid,
        in_specs=[
            rows_at(0, low), rows_at(0, low), rows_at(0, low), acts_at(0, low),
            rows_at(low, PAD), rows_at(low, PAD), rows_at(low, PAD), acts_at(low, PAD),
            rows_at(0, low, 3), col(3, 3),
        ],
        out_specs=[rows_at(0, low, 3), col(16)],
        out_shape=[gp_shape, short_shape],
        scratch_shapes=[pltpu.VMEM((3, low + PAD, tile), f32)],
        cost_estimate=pl.CostEstimate(
            flops=200_000_000, bytes_accessed=10 << 20, transcendentals=0
        ),
        name="top",
    )
    gp, short = top(bg, conv, gmix, act, bg, conv, gmix, act, projected, short_filter)
    rest = rows - low
    bottom = pl.pallas_call(
        bottom_kernel,
        grid=grid,
        in_specs=[
            rows_at(low, rest), rows_at(low, rest), rows_at(low, rest), acts_at(low, rest),
            col(BLK + PAD), rows_at(low, rest, 3), col(3, 3), col(2 * BLK), const, const_inv, col(16),
            pl.BlockSpec(memory_space=pl.ANY),
        ],
        out_specs=[rows_at(low, rest, 3), col(16)],
        out_shape=[gp_shape, short_shape],
        scratch_shapes=[pltpu.VMEM((3, rest + PAD, tile), f32), pltpu.VMEM((rest, tile), f32)],
        input_output_aliases={11: 0},
        cost_estimate=pl.CostEstimate(
            flops=2_000_000_000, bytes_accessed=5 << 20, transcendentals=0
        ),
        name="bottom",
    )
    gp, short = bottom(
        bg, conv, gmix, act, right, projected, short_filter, fspec, fwd, inv_now, short, gp
    )

    message = jnp.concatenate([my_quarter, short], 0)
    for along in (along_x, along_z):
        got = along([message.astype(bf16)] * SIDE)
        wide = [g.astype(f32) for g in got]
        message = (wide[0] + wide[1]) + (wide[2] + wide[3])
    long_total = jnp.concatenate([pick(got, zi ^ q)[:quarter] for q in range(SIDE)], 0)
    short_total = message[quarter : quarter + 9].reshape(3, 3, chans)

    share = rows // tp_count
    counts = tuple(o.shape[1] // width for o in (out1, out3))
    collect = pl.pallas_call(
        lambda cols, *refs: collect_kernel(counts, cols, *refs),
        grid_spec=pltpu.PrefetchScalarGridSpec(
            num_scalar_prefetch=1,
            grid=(1,),
            in_specs=[pl.BlockSpec(o.shape, lambda i, c: (0, 0)) for o in (out1, out3)],
            out_specs=pl.BlockSpec((share, 2 * width * ctx_count), lambda i, c: (0, 0)),
        ),
        out_shape=jax.ShapeDtypeStruct((share, 2 * width * ctx_count), bf16),
        cost_estimate=pl.CostEstimate(flops=10_000_000, bytes_accessed=5 << 20, transcendentals=0),
        name="collect",
    )
    mixed = collect(table, out1, out3)

    scale = 1.0 / math.sqrt(rows * ctx_count)
    return mixed, gp, long_total.astype(f32) * scale, short_total * scale


def solution(mesh):
    placed = (
        P(None, "ctx", "tp"),
        P(None, None, "tp"),
        P(None, "tp"),
        P("tp"),
        P("tp", "ctx"),
        P("ctx", None),
        P(),
    )
    return jax.shard_map(
        on_device,
        mesh=mesh,
        in_specs=placed,
        out_specs=(
            P(("ctx", "tp"), None),
            P(None, "ctx", "tp"),
            P(None, "tp"),
            P(None, None, "tp"),
        ),
        check_vma=False,
    )
```

```python
import math

import jax
import jax.numpy as jnp
import numpy as np
from jax import lax
from jax.experimental import pallas as pl
from jax.experimental.pallas import tpu as pltpu
from jax.sharding import PartitionSpec as P


f32, bf16 = jnp.float32, jnp.bfloat16
BLK = 128
SIDE = 4
PAD = 8


def split_hi_lo(matrix):
    hi = matrix.astype(np.float32).astype(bf16)
    lo = (matrix - hi.astype(np.float64)).astype(np.float32).astype(bf16)
    return hi, lo


def angles(times):
    freqs = np.concatenate([np.arange(0, BLK, 2), np.arange(1, BLK, 2)]) + 0.5
    return 2.0 * np.pi * freqs[:, None] * times[None, :] / (2 * BLK)


def forward_matrix():
    th = angles(np.arange(BLK, dtype=np.float64))
    hi, lo = split_hi_lo(np.concatenate([np.cos(th), -np.sin(th)], 0))
    return np.concatenate([hi, lo], 1)


def inverse_matrix(start):
    th = angles(np.arange(start, start + BLK, dtype=np.float64)).T
    return (np.concatenate([np.cos(th), -np.sin(th)], 1) / BLK).astype(np.float32).astype(bf16)


def spectrum(fwd, rows):
    return jnp.dot(fwd, jnp.concatenate([rows, rows], 0), preferred_element_type=f32)


def delay(v):
    h = BLK // 2
    re, im = v[:BLK], v[BLK:]
    return jnp.concatenate([im[:h], -im[h:], -re[:h], re[h:]], 0)


def product_conj(a, b):
    ar, ai, br, bi = a[:BLK], a[BLK:], b[:BLK], b[BLK:]
    return jnp.concatenate([ar * br + ai * bi, ai * br - ar * bi], 0)


def invert(inv, spec):
    return jnp.dot(inv[...], spec, preferred_element_type=f32)


def chunks(total, size):
    return [(r, min(size, total - r)) for r in range(0, total, size)]


ROWS = 32
FREQS = 16


def window_rows(spec, c, here, after):
    sr, si = slice(c, c + FREQS), slice(BLK + c, BLK + c + FREQS)
    wr, wi = spec[sr, here], spec[si, here]
    if after is None:
        return wr, wi
    ar, ai = spec[sr, after], spec[si, after]
    if c < BLK // 2:
        return wr + ai, wi - ar
    return wr - ai, wi + ar


def forward_kernel(
    proj, halo, sf, lf, skip, fwd, inv, gated, conv, act, mspec, fspec, ext, mix, spec, ybuf, out
):
    rows = proj.shape[1]
    nb, wide = rows // BLK, proj.shape[2]
    fmat = fwd[...]
    edge = halo[BLK : BLK + PAD].astype(f32)
    for m in range(3):
        ext[m, PAD - 2 : PAD] = edge[2 * m : 2 * m + 2]
        for r, n in chunks(rows, ROWS):
            ext[m, PAD + r : PAD + r + n] = proj[m, r : r + n].astype(f32)
    for h in range(2):
        mix[h * BLK : (h + 1) * BLK, :wide] = halo[:BLK]
    for r, n in chunks(rows, ROWS):
        acts = []
        for m in range(3):
            total = sf[m, 0:1] * ext[m, PAD + r : PAD + r + n]
            for s in (1, 2):
                total = total + sf[m, s : s + 1] * ext[m, PAD - s + r : PAD - s + r + n]
            act[m, r : r + n] = total
            acts.append(total)
        mixin = (acts[1] * acts[2]).astype(bf16)
        at, lane = r % BLK, (r // BLK + 1) * wide
        for h in range(2):
            mix[h * BLK + at : h * BLK + at + n, lane : lane + wide] = mixin
    filt = spectrum(fmat, lf[...])
    fspec[...] = filt
    spec[...] = jnp.dot(fmat, mix[...], preferred_element_type=f32)
    for c in range(0, BLK, FREQS):
        fr, fi = fspec[c : c + FREQS], fspec[BLK + c : BLK + c + FREQS]
        for b in range(nb):
            lanes = slice(b * wide, (b + 1) * wide)
            wr, wi = window_rows(spec, c, lanes, slice((b + 1) * wide, (b + 2) * wide))
            mspec[b, c : c + FREQS] = wr
            mspec[b, BLK + c : BLK + c + FREQS] = wi
            ybuf[c : c + FREQS, lanes] = (fr * wr - fi * wi).astype(bf16)
            ybuf[BLK + c : BLK + c + FREQS, lanes] = (fr * wi + fi * wr).astype(bf16)
    out[...] = invert(inv, ybuf[...])
    for r, n in chunks(rows, ROWS):
        at, lane = r % BLK, r // BLK * wide
        mixin = mix[at : at + n, lane + wide : lane + 2 * wide].astype(f32)
        full = out[at : at + n, lane : lane + wide] + skip[...] * mixin
        conv[r : r + n] = full
        gated[r : r + n] = (act[0, r : r + n] * full).astype(bf16)


def backward_kernel(place, acc, act0, mspec, fspec, skip, fwd, inv, invlag, *refs):
    og, refs = refs[: 2 * SIDE], refs[2 * SIDE :]
    weights, refs = refs[:4], refs[4:]
    bg, long0, long1, long2, long3, gmix, lagbuf, gbuf, spec, ybuf, lagy, out = refs
    rows, wide = bg.shape
    nb = rows // BLK
    bg[...] = acc[...] + lax.dot_general(
        jnp.concatenate([o[...] for o in og], 1),
        jnp.concatenate([w[n] for w in weights for n in range(2)], 1),
        (((1,), (1,)), ((), ())),
        preferred_element_type=f32,
    )
    for r, n in chunks(rows, ROWS):
        g = (bg[r : r + n] * act0[0, r : r + n]).astype(bf16)
        at, lane = r % BLK, r // BLK * wide
        for h in range(2):
            gbuf[h * BLK + at : h * BLK + at + n, lane : lane + wide] = g
    spec[...] = jnp.dot(fwd[...], gbuf[...], preferred_element_type=f32)
    for c in range(0, BLK, FREQS):
        sr, si = slice(c, c + FREQS), slice(BLK + c, BLK + c + FREQS)
        fr, fi = fspec[sr], fspec[si]
        lag_r = lag_i = None
        for b in range(nb):
            lanes = slice(b * wide, (b + 1) * wide)
            after = slice((b + 1) * wide, (b + 2) * wide) if b + 1 < nb else None
            gr, gi, mr, mi = spec[sr, lanes], spec[si, lanes], mspec[b, sr], mspec[b, si]
            pr, pi = gr * mr + gi * mi, gi * mr - gr * mi
            lag_r, lag_i = (pr, pi) if b == 0 else (lag_r + pr, lag_i + pi)
            wr, wi = window_rows(spec, c, lanes, after)
            ybuf[sr, lanes] = (wr * fr + wi * fi).astype(bf16)
            ybuf[si, lanes] = (wi * fr - wr * fi).astype(bf16)
        lagy[sr] = lag_r.astype(bf16)
        lagy[si] = lag_i.astype(bf16)
    lagbuf[...] = invert(invlag, lagy[...])
    quarter = BLK // SIDE
    for k, part in enumerate((long0, long1, long2, long3)):
        start = pl.multiple_of((place[0] ^ k) * quarter, quarter)
        part[...] = lagbuf[pl.ds(start, quarter)].astype(bf16)
    out[...] = invert(inv, ybuf[...])
    for r, n in chunks(rows, ROWS):
        at, lane = r % BLK, r // BLK * wide
        g = gbuf[at : at + n, lane : lane + wide].astype(f32)
        gmix[r : r + n] = out[at : at + n, lane : lane + wide] + skip[...] * g


def head_kernel(place, acc, act0, act12, convh, lf, skip, *refs):
    del place
    og, refs = refs[: 2 * SIDE], refs[2 * SIDE :]
    weights, (pay, ext) = refs[:4], refs[4:]
    bg = acc[...] + lax.dot_general(
        jnp.concatenate([o[...] for o in og], 1),
        jnp.concatenate([w[n] for w in weights for n in range(2)], 1),
        (((1,), (1,)), ((), ())),
        preferred_element_type=f32,
    )
    g = (bg * act0[0]).astype(bf16)
    ext[...] = g.astype(f32)
    taps = lf[...].astype(f32)
    gm0 = jnp.sum(taps * ext[:BLK], axis=0, keepdims=True) + skip[...] * ext[0:1]
    gm1 = jnp.sum(taps * ext[1 : BLK + 1], axis=0, keepdims=True) + skip[...] * ext[1:2]
    gm = jnp.concatenate([gm0, gm1], 0)
    edge = [bg[:2] * convh[:2], gm * act12[1, :2], gm * act12[0, :2], jnp.zeros_like(gm)]
    pay[:BLK] = g[:BLK]
    pay[BLK:] = jnp.concatenate(edge, 0).astype(bf16)


def finish_body(bg, conv, gmix, act, proj, sf, extra, gp, ext):
    rows, wide = bg.shape
    sums = []
    for m in range(3):
        for r, n in chunks(rows, ROWS):
            if m == 0:
                ext[m, r : r + n] = bg[r : r + n] * conv[r : r + n]
            else:
                ext[m, r : r + n] = gmix[r : r + n] * act[2 - m, r : r + n]
        ext[m, rows : rows + PAD] = extra[m]
        parts = [jnp.zeros((8, wide), f32)] * 3
        for r, n in chunks(rows, ROWS):
            x = proj[m, r : r + n].astype(f32)
            total = None
            for s in range(3):
                moved = ext[m, r + s : r + s + n]
                term = sf[m, s : s + 1] * moved
                total = term if s == 0 else total + term
                parts[s] = parts[s] + jnp.sum((x * moved).reshape(n // 8, 8, wide), axis=0)
            gp[m, r : r + n] = total.astype(bf16)
        sums += [jnp.sum(p, axis=0, keepdims=True) for p in parts]
    return jnp.concatenate(sums + [jnp.zeros((7, wide), f32)], 0)


def top_kernel(bg, conv, gmix, act, bgn, convn, gmixn, actn, proj, sf, gp, short, ext):
    extra = [bgn[...] * convn[...], gmixn[...] * actn[1], gmixn[...] * actn[0]]
    short[...] = finish_body(bg, conv, gmix, act, proj, sf, extra, gp, ext)


def bottom_kernel(
    bg, conv, gmix, act, halo, proj, sf, fspec, fwd, inv, short_in, gp_in, gp, short, ext, gfull
):
    del gp_in
    rows = bg.shape[0]
    late = delay(spectrum(fwd[...], halo[:BLK]))
    gfull[: rows - BLK] = gmix[: rows - BLK]
    gfull[rows - BLK :] = gmix[rows - BLK :] + invert(inv, product_conj(late, fspec[...]).astype(bf16))
    edge = halo[BLK : BLK + PAD].astype(f32)
    zeros = jnp.zeros((PAD - 2, edge.shape[1]), f32)
    extra = [jnp.concatenate([edge[2 * m : 2 * m + 2], zeros], 0) for m in range(3)]
    short[...] = short_in[...] + finish_body(bg, conv, gfull, act, proj, sf, extra, gp, ext)


def pieces_kernel(steps, per, back, more, *refs):
    count = steps * per // 2
    weights, refs = refs[:count], refs[count:]
    if back:
        gated, og, refs = refs[0], refs[1 : 1 + per], refs[1 + per :]
        if more:
            acc_in, refs = refs[0], refs[2:]
        result, acc, buf, sems = refs
    else:
        gated, (result, buf, sems) = refs[0], refs[1 + more :]
    step = pl.program_id(0)
    chans = gated.shape[1]
    width = buf.shape[2] // per

    def copies(i):
        return [
            pltpu.make_async_copy(
                weights[(per * i + j) // 2].at[pl.ds((per * i + j) % 2 * chans, chans)],
                buf.at[i % 2, :, pl.ds(j * width, width)],
                sems.at[i % 2, j],
            )
            for j in range(per)
        ]

    @pl.when(step == 0)
    def _():
        for c in copies(0):
            c.start()
        if back:
            acc[...] = acc_in[...] if more else jnp.zeros_like(acc)

    for i in range(steps):

        @pl.when(step == i)
        def _(i=i):
            if i + 1 < steps:
                for c in copies(i + 1):
                    c.start()
            for c in copies(i):
                c.wait()

    w = buf[step % 2]
    result[...] = jnp.dot(gated[...], w, preferred_element_type=f32).astype(bf16)
    if back:
        acc[...] += lax.dot_general(
            jnp.concatenate([o[...] for o in og], 1),
            w,
            (((1,), (1,)), ((), ())),
            preferred_element_type=f32,
        )


def multiply_pieces(weights, table, gated, out_grad=None, total=None, before=None, per=SIDE):
    rows, chans = gated.shape
    width = weights[0].shape[1]
    steps = 2 * len(weights) // per
    back, more = out_grad is not None, before is not None
    total = total or steps
    offset = before[0] if more else 0
    whole = pl.BlockSpec((rows, chans), lambda i, c: (0, 0), pipeline_mode=pl.Buffered(1))
    in_specs = [pl.BlockSpec(memory_space=pl.ANY)] * len(weights) + [whole]
    operands = [*weights, gated]
    aliases = {}
    if back:
        in_specs += [
            pl.BlockSpec((rows, width), lambda i, c, j=j: (0, c[1 + per * (i + offset) + j])) for j in range(per)
        ]
        operands += [out_grad] * per
        if more:
            in_specs.append(whole)
            operands.append(before[2])
    if more:
        in_specs.append(pl.BlockSpec(memory_space=pl.ANY))
        operands.append(before[1])
        aliases = {len(operands): 0}
    result_shape = jax.ShapeDtypeStruct((rows, total * per * width), bf16)
    result_spec = pl.BlockSpec((rows, per * width), lambda i, c: (0, i + offset))

    def kernel(cols_ref, *refs):
        del cols_ref
        pieces_kernel(steps, per, back, more, *refs)

    return pl.pallas_call(
        kernel,
        grid_spec=pltpu.PrefetchScalarGridSpec(
            num_scalar_prefetch=1,
            grid=(steps,),
            in_specs=in_specs,
            out_specs=[result_spec] + [whole] * back,
            scratch_shapes=[
                pltpu.VMEM((2, chans, per * width), bf16),
                pltpu.SemaphoreType.DMA((2, per)),
            ],
        ),
        out_shape=[result_shape] + [jax.ShapeDtypeStruct((rows, chans), f32)] * back,
        input_output_aliases=aliases,
        cost_estimate=pl.CostEstimate(
            flops=(2 + 2 * back) * rows * chans * width * per * steps,
            bytes_accessed=per * steps * (2 * chans * width + 4 * rows * width) + 6 * rows * chans,
            transcendentals=0,
        ),
        name="pieces",
    )(table, *operands)


def collect_kernel(counts, cols, *refs):
    mixed = refs[-1]
    width = mixed.shape[1] // sum(counts)
    begin = 0
    for ref, count in zip(refs, counts):

        @pl.loop(0, count)
        def _(p, ref=ref, begin=begin):
            lanes = pl.ds(pl.multiple_of(p * width, width), width)
            start = pl.multiple_of(cols[1 + begin + p] * width, width)
            mixed[:, pl.ds(start, width)] = ref[:, lanes]

        begin += count


def on_device(projected, short_filter, long_filter, skip_gain, out_weight, out_grad, left_source):
    rows, chans = projected.shape[1:]
    width = out_weight.shape[1] // 2
    ctx_count, tp_count = lax.axis_size("ctx"), lax.axis_size("tp")
    me = lax.axis_index("ctx").astype(jnp.uint32)
    zu, xu = me >> 2, me & 3
    zi, xi = zu.astype(jnp.int32), xu.astype(jnp.int32)

    def ring(value, axis, step):
        if axis == "x":
            pairs = [(d, d // SIDE * SIDE + (d + step) % SIDE) for d in range(ctx_count)]
        else:
            pairs = [(d, (d + SIDE * step) % ctx_count) for d in range(ctx_count)]
        return lax.ppermute(value, "ctx", pairs)

    def swap(value, axis, k):
        shift = {"x": k, "z": k * SIDE}[axis]
        return lax.ppermute(value, "ctx", [(d, d ^ shift) for d in range(ctx_count)])

    def gather(piece, first, second):
        h = piece.shape[0] // 2
        p, q = ring(piece, first, 1), ring(piece, first, -1)
        t, b = ring(p[:h], first, 1), ring(q[h:], first, -1)
        one, two = jnp.concatenate([piece, p], 0), jnp.concatenate([q, t, b], 0)
        op, oq = ring(one, second, 1), ring(one, second, -1)
        tp_, tq = ring(two, second, 1), ring(two, second, -1)
        far_one = ring(op, second, 1)
        far_two = ring(tq, second, -1)
        return [one, two], [op, tp_, oq, tq], [far_one, far_two]

    def blocks(half, near, far_steps):
        steps = [(f, n) if half == 0 else (n, f) for f in far_steps for n in near]
        return [(half, z, x) for z, x in steps]

    order4 = (0, -1, 1, 2)
    halves, dz, dx = np.array(
        [b for far in ((0,), (-1, 1), (2,)) for half in (0, 1) for b in blocks(half, order4, far)]
    ).T
    table = 2 * (((zi + dz) & 3) * SIDE + ((xi + dx) & 3)) + halves
    table = jnp.concatenate([jnp.reshape(zi, (1,)), table]).astype(jnp.int32)

    positions = jnp.arange(ctx_count, dtype=jnp.int32)
    matches = left_source[None, :] == positions[:, None]
    readers = jnp.where(
        jnp.any(matches, 1), jnp.sum(jnp.where(matches, positions[None, :], 0), 1), -1
    )

    def pick(options, index):
        low = jnp.where(index == 1, options[1], options[0])
        high = jnp.where(index == 3, options[3], options[2])
        return jnp.where(index >= 2, high, low)

    def at(table, index):
        return lax.dynamic_index_in_dim(table, index, 0, keepdims=False)

    def along_x(payloads):
        return [payloads[0]] + [swap(payloads[k], "x", k) for k in (1, 2, 3)]

    def along_z(payloads):
        return [payloads[0]] + [swap(payloads[k], "z", k) for k in (1, 2, 3)]

    def chosen(got, sources):
        return [pick(got, (at(sources, me ^ (4 * k)) & 3) ^ xi) for k in range(SIDE)]

    def landed(got, sources):
        source = at(sources, me)
        value = pick(got, ((source >> 2) & 3) ^ zi)
        return jnp.where(source >= 0, value, jnp.zeros_like(value))

    near = projected[1:, rows - BLK - PAD :].astype(f32)
    tail = jnp.zeros((2, BLK, chans), f32)
    for s in range(3):
        tail = tail + short_filter[1:, s][:, None] * near[:, PAD - s : PAD - s + BLK]
    raw = projected[:, rows - 2 :].reshape(6, chans)
    sent = jnp.concatenate(
        [(tail[0] * tail[1]).astype(bf16), raw, jnp.zeros((2, chans), bf16)], 0
    )
    got = along_x([sent] * SIDE)
    to_z = chosen(got, left_source)
    got = along_z(to_z)
    left = landed(got, left_source)

    near_a, mid_a, far_a = gather(out_weight[:, :width], "x", "z")
    near_b, mid_b, far_b = gather(out_weight[:, width:], "z", "x")

    fwd = jnp.asarray(forward_matrix())
    inv_late, inv_now, inv_lag = (jnp.asarray(inverse_matrix(s)) for s in (BLK, 0, -BLK))
    skip_row = skip_gain[None, :]
    tile = 256
    grid = (chans // tile,)
    nb = rows // BLK

    def col(*lead):
        return pl.BlockSpec((*lead, tile), lambda i, *_: (*([0] * len(lead)), i))

    const = pl.BlockSpec((2 * BLK, 2 * BLK), lambda i, *_: (0, 0))
    const_inv = pl.BlockSpec((BLK, 2 * BLK), lambda i, *_: (0, 0))
    forward = pl.pallas_call(
        forward_kernel,
        grid=grid,
        in_specs=[
            col(3, rows), col(BLK + PAD), col(3, 3), col(BLK), col(1), const, const_inv,
        ],
        out_specs=[col(rows), col(rows), col(3, rows), col(nb, 2 * BLK), col(2 * BLK)],
        scratch_shapes=[
            pltpu.VMEM((3, rows + PAD, tile), f32),
            pltpu.VMEM((2 * BLK, (nb + 1) * tile), bf16),
            pltpu.VMEM((2 * BLK, (nb + 1) * tile), f32),
            pltpu.VMEM((2 * BLK, nb * tile), bf16),
            pltpu.VMEM((BLK, nb * tile), f32),
        ],
        out_shape=[
            jax.ShapeDtypeStruct((rows, chans), bf16),
            jax.ShapeDtypeStruct((rows, chans), f32),
            jax.ShapeDtypeStruct((3, rows, chans), f32),
            jax.ShapeDtypeStruct((nb, 2 * BLK, chans), f32),
            jax.ShapeDtypeStruct((2 * BLK, chans), f32),
        ],
        cost_estimate=pl.CostEstimate(
            flops=8_000_000_000, bytes_accessed=20 << 20, transcendentals=0
        ),
        name="forward",
    )
    gated, conv, act, mspec, fspec = forward(
        projected, left, short_filter, long_filter, skip_row, fwd, inv_late
    )

    def scatter(value):
        return lax.psum_scatter(value, "tp", scatter_dimension=0, tiled=True)

    early = multiply_pieces(near_a + near_b, table, gated, out_grad, 8)
    out1, acc = multiply_pieces(
        mid_a + mid_b, table, gated, out_grad, 8, (2, *early)
    )
    quarter = BLK // SIDE
    lasts = [w.reshape(2, chans, width) for w in far_a + far_b]
    last_spec = pl.BlockSpec((2, tile, width), lambda i, c: (0, i, 0))

    def out_grad_rows(n):
        return [pl.BlockSpec((n, width), lambda i, c, j=j: (0, c[1 + 6 * SIDE + j])) for j in range(2 * SIDE)]

    def first_rows(n, *lead):
        zeros = [0] * len(lead)
        return pl.BlockSpec((*lead, n, tile), lambda i, c: (*zeros, 0, i))

    head = pl.pallas_call(
        head_kernel,
        grid_spec=pltpu.PrefetchScalarGridSpec(
            num_scalar_prefetch=1,
            grid=grid,
            in_specs=[
                first_rows(BLK + PAD),
                first_rows(BLK + PAD, 1),
                pl.BlockSpec(
                    (pl.Element(2), pl.Element(PAD), pl.Element(tile)),
                    lambda i, c: (1, 0, i * tile),
                ),
                first_rows(PAD),
                col(BLK),
                col(1),
                *out_grad_rows(BLK + PAD),
                *[last_spec] * 4,
            ],
            out_specs=col(BLK + PAD),
            scratch_shapes=[pltpu.VMEM((BLK + PAD, tile), f32)],
        ),
        out_shape=jax.ShapeDtypeStruct((BLK + PAD, chans), bf16),
        cost_estimate=pl.CostEstimate(
            flops=600_000_000, bytes_accessed=6 << 20, transcendentals=0
        ),
        name="head",
    )
    pay = head(table, acc, act, act, conv, long_filter, skip_row, *[out_grad] * (2 * SIDE), *lasts)
    got = along_x([pay] * SIDE)

    long_shape = jax.ShapeDtypeStruct((quarter, chans), bf16)
    backward = pl.pallas_call(
        backward_kernel,
        grid_spec=pltpu.PrefetchScalarGridSpec(
            num_scalar_prefetch=1,
            grid=grid,
            in_specs=[
                col(rows),
                first_rows(rows, 1),
                col(nb, 2 * BLK),
                col(2 * BLK),
                col(1),
                const,
                const_inv,
                const_inv,
                *out_grad_rows(rows),
                *[last_spec] * 4,
            ],
            out_specs=[col(rows)] + [col(quarter)] * 4 + [col(rows)],
            scratch_shapes=[
                pltpu.VMEM((BLK, tile), f32),
                pltpu.VMEM((2 * BLK, nb * tile), bf16),
                pltpu.VMEM((2 * BLK, nb * tile), f32),
                pltpu.VMEM((2 * BLK, nb * tile), bf16),
                pltpu.VMEM((2 * BLK, tile), bf16),
                pltpu.VMEM((BLK, nb * tile), f32),
            ],
        ),
        out_shape=[jax.ShapeDtypeStruct((rows, chans), f32)]
        + [long_shape] * 4
        + [jax.ShapeDtypeStruct((rows, chans), f32)],
        cost_estimate=pl.CostEstimate(
            flops=8_000_000_000, bytes_accessed=20 << 20, transcendentals=0
        ),
        name="backward",
    )
    bg, *longs, gmix = backward(
        table, acc, act, mspec, fspec, skip_row, fwd, inv_now, inv_lag,
        *[out_grad] * (2 * SIDE), *lasts,
    )

    to_z = chosen(got, readers)
    got = along_z([jnp.concatenate([v, part], 0) for v, part in zip(to_z, longs)])
    right = landed([g[: BLK + PAD] for g in got], readers)
    sums = [g[BLK + PAD :].astype(f32) for g in got]
    my_quarter = (sums[0] + sums[1]) + (sums[2] + sums[3])

    (out1,) = multiply_pieces(
        far_a + far_b, table, gated, None, 16, (12, out1), per=2
    )
    out1 = scatter(out1)

    low = rows - BLK - PAD

    def rows_at(start, n, *lead):
        zeros = [0] * len(lead)
        dims = [pl.Element(d) for d in (*lead, n, tile)]
        return pl.BlockSpec(tuple(dims), lambda i: (*zeros, start, i * tile))

    def acts_at(start, n):
        return pl.BlockSpec(
            (pl.Element(2), pl.Element(n), pl.Element(tile)), lambda i: (1, start, i * tile)
        )

    gp_shape = jax.ShapeDtypeStruct((3, rows, chans), bf16)
    short_shape = jax.ShapeDtypeStruct((16, chans), f32)
    top = pl.pallas_call(
        top_kernel,
        grid=grid,
        in_specs=[
            rows_at(0, low), rows_at(0, low), rows_at(0, low), acts_at(0, low),
            rows_at(low, PAD), rows_at(low, PAD), rows_at(low, PAD), acts_at(low, PAD),
            rows_at(0, low, 3), col(3, 3),
        ],
        out_specs=[rows_at(0, low, 3), col(16)],
        out_shape=[gp_shape, short_shape],
        scratch_shapes=[pltpu.VMEM((3, low + PAD, tile), f32)],
        cost_estimate=pl.CostEstimate(
            flops=200_000_000, bytes_accessed=10 << 20, transcendentals=0
        ),
        name="top",
    )
    gp, short = top(bg, conv, gmix, act, bg, conv, gmix, act, projected, short_filter)
    rest = rows - low
    bottom = pl.pallas_call(
        bottom_kernel,
        grid=grid,
        in_specs=[
            rows_at(low, rest), rows_at(low, rest), rows_at(low, rest), acts_at(low, rest),
            col(BLK + PAD), rows_at(low, rest, 3), col(3, 3), col(2 * BLK), const, const_inv, col(16),
            pl.BlockSpec(memory_space=pl.ANY),
        ],
        out_specs=[rows_at(low, rest, 3), col(16)],
        out_shape=[gp_shape, short_shape],
        scratch_shapes=[pltpu.VMEM((3, rest + PAD, tile), f32), pltpu.VMEM((rest, tile), f32)],
        input_output_aliases={11: 0},
        cost_estimate=pl.CostEstimate(
            flops=2_000_000_000, bytes_accessed=5 << 20, transcendentals=0
        ),
        name="bottom",
    )
    gp, short = bottom(
        bg, conv, gmix, act, right, projected, short_filter, fspec, fwd, inv_now, short, gp
    )

    message = jnp.concatenate([my_quarter, short], 0)
    for along in (along_x, along_z):
        got = along([message.astype(bf16)] * SIDE)
        wide = [g.astype(f32) for g in got]
        message = (wide[0] + wide[1]) + (wide[2] + wide[3])
    long_total = jnp.concatenate([pick(got, zi ^ q)[:quarter] for q in range(SIDE)], 0)
    short_total = message[quarter : quarter + 9].reshape(3, 3, chans)

    share = rows // tp_count
    counts = tuple(o.shape[1] // width for o in (out1,))
    collect = pl.pallas_call(
        lambda cols, *refs: collect_kernel(counts, cols, *refs),
        grid_spec=pltpu.PrefetchScalarGridSpec(
            num_scalar_prefetch=1,
            grid=(1,),
            in_specs=[pl.BlockSpec(o.shape, lambda i, c: (0, 0)) for o in (out1,)],
            out_specs=pl.BlockSpec((share, 2 * width * ctx_count), lambda i, c: (0, 0)),
        ),
        out_shape=jax.ShapeDtypeStruct((share, 2 * width * ctx_count), bf16),
        cost_estimate=pl.CostEstimate(flops=10_000_000, bytes_accessed=5 << 20, transcendentals=0),
        name="collect",
    )
    mixed = collect(table, out1)

    scale = 1.0 / math.sqrt(rows * ctx_count)
    return mixed, gp, long_total.astype(f32) * scale, short_total * scale


def solution(mesh):
    placed = (
        P(None, "ctx", "tp"),
        P(None, None, "tp"),
        P(None, "tp"),
        P("tp"),
        P("tp", "ctx"),
        P("ctx", None),
        P(),
    )
    return jax.shard_map(
        on_device,
        mesh=mesh,
        in_specs=placed,
        out_specs=(
            P(("ctx", "tp"), None),
            P(None, "ctx", "tp"),
            P(None, "tp"),
            P(None, None, "tp"),
        ),
        check_vma=False,
    )
```

```python
import math

import jax
import jax.numpy as jnp
import numpy as np
from jax import lax
from jax.experimental import pallas as pl
from jax.experimental.pallas import tpu as pltpu
from jax.sharding import PartitionSpec as P


f32, bf16 = jnp.float32, jnp.bfloat16
BLK = 128
SIDE = 4
PAD = 8


def split_hi_lo(matrix):
    hi = matrix.astype(np.float32).astype(bf16)
    lo = (matrix - hi.astype(np.float64)).astype(np.float32).astype(bf16)
    return hi, lo


def angles(times):
    freqs = np.concatenate([np.arange(0, BLK, 2), np.arange(1, BLK, 2)]) + 0.5
    return 2.0 * np.pi * freqs[:, None] * times[None, :] / (2 * BLK)


def forward_matrix():
    th = angles(np.arange(BLK, dtype=np.float64))
    hi, lo = split_hi_lo(np.concatenate([np.cos(th), -np.sin(th)], 0))
    return np.concatenate([hi, lo], 1)


def inverse_matrix(start):
    th = angles(np.arange(start, start + BLK, dtype=np.float64)).T
    return (np.concatenate([np.cos(th), -np.sin(th)], 1) / BLK).astype(np.float32).astype(bf16)


def spectrum(fwd, rows):
    return jnp.dot(fwd, jnp.concatenate([rows, rows], 0), preferred_element_type=f32)


def delay(v):
    h = BLK // 2
    re, im = v[:BLK], v[BLK:]
    return jnp.concatenate([im[:h], -im[h:], -re[:h], re[h:]], 0)


def product_conj(a, b):
    ar, ai, br, bi = a[:BLK], a[BLK:], b[:BLK], b[BLK:]
    return jnp.concatenate([ar * br + ai * bi, ai * br - ar * bi], 0)


def invert(inv, spec):
    return jnp.dot(inv[...], spec, preferred_element_type=f32)


def chunks(total, size):
    return [(r, min(size, total - r)) for r in range(0, total, size)]


ROWS = 32
FREQS = 16


def window_rows(spec, c, here, after):
    sr, si = slice(c, c + FREQS), slice(BLK + c, BLK + c + FREQS)
    wr, wi = spec[sr, here], spec[si, here]
    if after is None:
        return wr, wi
    ar, ai = spec[sr, after], spec[si, after]
    if c < BLK // 2:
        return wr + ai, wi - ar
    return wr - ai, wi + ar


def forward_kernel(
    proj, halo, sf, lf, skip, fwd, inv, gated, conv, act, mspec, fspec, ext, mix, spec, ybuf, out
):
    rows = proj.shape[1]
    nb, wide = rows // BLK, proj.shape[2]
    fmat = fwd[...]
    edge = halo[BLK : BLK + PAD].astype(f32)
    for m in range(3):
        ext[m, PAD - 2 : PAD] = edge[2 * m : 2 * m + 2]
        for r, n in chunks(rows, ROWS):
            ext[m, PAD + r : PAD + r + n] = proj[m, r : r + n].astype(f32)
    for h in range(2):
        mix[h * BLK : (h + 1) * BLK, :wide] = halo[:BLK]
    for r, n in chunks(rows, ROWS):
        acts = []
        for m in range(3):
            total = sf[m, 0:1] * ext[m, PAD + r : PAD + r + n]
            for s in (1, 2):
                total = total + sf[m, s : s + 1] * ext[m, PAD - s + r : PAD - s + r + n]
            act[m, r : r + n] = total
            acts.append(total)
        mixin = (acts[1] * acts[2]).astype(bf16)
        at, lane = r % BLK, (r // BLK + 1) * wide
        for h in range(2):
            mix[h * BLK + at : h * BLK + at + n, lane : lane + wide] = mixin
    filt = spectrum(fmat, lf[...])
    fspec[...] = filt
    spec[...] = jnp.dot(fmat, mix[...], preferred_element_type=f32)
    for c in range(0, BLK, FREQS):
        fr, fi = fspec[c : c + FREQS], fspec[BLK + c : BLK + c + FREQS]
        for b in range(nb):
            lanes = slice(b * wide, (b + 1) * wide)
            wr, wi = window_rows(spec, c, lanes, slice((b + 1) * wide, (b + 2) * wide))
            mspec[b, c : c + FREQS] = wr
            mspec[b, BLK + c : BLK + c + FREQS] = wi
            ybuf[c : c + FREQS, lanes] = (fr * wr - fi * wi).astype(bf16)
            ybuf[BLK + c : BLK + c + FREQS, lanes] = (fr * wi + fi * wr).astype(bf16)
    out[...] = invert(inv, ybuf[...])
    for r, n in chunks(rows, ROWS):
        at, lane = r % BLK, r // BLK * wide
        mixin = mix[at : at + n, lane + wide : lane + 2 * wide].astype(f32)
        full = out[at : at + n, lane : lane + wide] + skip[...] * mixin
        conv[r : r + n] = full
        gated[r : r + n] = (act[0, r : r + n] * full).astype(bf16)


def backward_kernel(place, acc, act0, mspec, fspec, skip, fwd, inv, invlag, *refs):
    og, refs = refs[: 2 * SIDE], refs[2 * SIDE :]
    weights, refs = refs[:4], refs[4:]
    bg, long0, long1, long2, long3, gmix, lagbuf, gbuf, spec, ybuf, lagy, out = refs
    rows, wide = bg.shape
    nb = rows // BLK
    bg[...] = acc[...] + lax.dot_general(
        jnp.concatenate([o[...] for o in og], 1),
        jnp.concatenate([w[n] for w in weights for n in range(2)], 1),
        (((1,), (1,)), ((), ())),
        preferred_element_type=f32,
    )
    for r, n in chunks(rows, ROWS):
        g = (bg[r : r + n] * act0[0, r : r + n]).astype(bf16)
        at, lane = r % BLK, r // BLK * wide
        for h in range(2):
            gbuf[h * BLK + at : h * BLK + at + n, lane : lane + wide] = g
    spec[...] = jnp.dot(fwd[...], gbuf[...], preferred_element_type=f32)
    for c in range(0, BLK, FREQS):
        sr, si = slice(c, c + FREQS), slice(BLK + c, BLK + c + FREQS)
        fr, fi = fspec[sr], fspec[si]
        lag_r = lag_i = None
        for b in range(nb):
            lanes = slice(b * wide, (b + 1) * wide)
            after = slice((b + 1) * wide, (b + 2) * wide) if b + 1 < nb else None
            gr, gi, mr, mi = spec[sr, lanes], spec[si, lanes], mspec[b, sr], mspec[b, si]
            pr, pi = gr * mr + gi * mi, gi * mr - gr * mi
            lag_r, lag_i = (pr, pi) if b == 0 else (lag_r + pr, lag_i + pi)
            wr, wi = window_rows(spec, c, lanes, after)
            ybuf[sr, lanes] = (wr * fr + wi * fi).astype(bf16)
            ybuf[si, lanes] = (wi * fr - wr * fi).astype(bf16)
        lagy[sr] = lag_r.astype(bf16)
        lagy[si] = lag_i.astype(bf16)
    lagbuf[...] = invert(invlag, lagy[...])
    quarter = BLK // SIDE
    for k, part in enumerate((long0, long1, long2, long3)):
        start = pl.multiple_of((place[0] ^ k) * quarter, quarter)
        part[...] = lagbuf[pl.ds(start, quarter)].astype(bf16)
    out[...] = invert(inv, ybuf[...])
    for r, n in chunks(rows, ROWS):
        at, lane = r % BLK, r // BLK * wide
        g = gbuf[at : at + n, lane : lane + wide].astype(f32)
        gmix[r : r + n] = out[at : at + n, lane : lane + wide] + skip[...] * g


def head_kernel(place, acc, act0, act12, convh, lf, skip, *refs):
    del place
    og, refs = refs[: 2 * SIDE], refs[2 * SIDE :]
    weights, (pay, ext) = refs[:4], refs[4:]
    bg = acc[...] + lax.dot_general(
        jnp.concatenate([o[...] for o in og], 1),
        jnp.concatenate([w[n] for w in weights for n in range(2)], 1),
        (((1,), (1,)), ((), ())),
        preferred_element_type=f32,
    )
    g = (bg * act0[0]).astype(bf16)
    ext[...] = g.astype(f32)
    taps = lf[...].astype(f32)
    gm0 = jnp.sum(taps * ext[:BLK], axis=0, keepdims=True) + skip[...] * ext[0:1]
    gm1 = jnp.sum(taps * ext[1 : BLK + 1], axis=0, keepdims=True) + skip[...] * ext[1:2]
    gm = jnp.concatenate([gm0, gm1], 0)
    edge = [bg[:2] * convh[:2], gm * act12[1, :2], gm * act12[0, :2], jnp.zeros_like(gm)]
    pay[:BLK] = g[:BLK]
    pay[BLK:] = jnp.concatenate(edge, 0).astype(bf16)


def finish_body(bg, conv, gmix, act, proj, sf, extra, gp, ext):
    rows, wide = bg.shape
    sums = []
    for m in range(3):
        for r, n in chunks(rows, ROWS):
            if m == 0:
                ext[m, r : r + n] = bg[r : r + n] * conv[r : r + n]
            else:
                ext[m, r : r + n] = gmix[r : r + n] * act[2 - m, r : r + n]
        ext[m, rows : rows + PAD] = extra[m]
        parts = [jnp.zeros((8, wide), f32)] * 3
        for r, n in chunks(rows, ROWS):
            x = proj[m, r : r + n].astype(f32)
            total = None
            for s in range(3):
                moved = ext[m, r + s : r + s + n]
                term = sf[m, s : s + 1] * moved
                total = term if s == 0 else total + term
                parts[s] = parts[s] + jnp.sum((x * moved).reshape(n // 8, 8, wide), axis=0)
            gp[m, r : r + n] = total.astype(bf16)
        sums += [jnp.sum(p, axis=0, keepdims=True) for p in parts]
    return jnp.concatenate(sums + [jnp.zeros((7, wide), f32)], 0)


def top_kernel(bg, conv, gmix, act, bgn, convn, gmixn, actn, proj, sf, gp, short, ext):
    extra = [bgn[...] * convn[...], gmixn[...] * actn[1], gmixn[...] * actn[0]]
    short[...] = finish_body(bg, conv, gmix, act, proj, sf, extra, gp, ext)


def bottom_kernel(
    bg, conv, gmix, act, halo, proj, sf, fspec, fwd, inv, short_in, gp_in, gp, short, ext, gfull
):
    del gp_in
    rows = bg.shape[0]
    late = delay(spectrum(fwd[...], halo[:BLK]))
    gfull[: rows - BLK] = gmix[: rows - BLK]
    gfull[rows - BLK :] = gmix[rows - BLK :] + invert(inv, product_conj(late, fspec[...]).astype(bf16))
    edge = halo[BLK : BLK + PAD].astype(f32)
    zeros = jnp.zeros((PAD - 2, edge.shape[1]), f32)
    extra = [jnp.concatenate([edge[2 * m : 2 * m + 2], zeros], 0) for m in range(3)]
    short[...] = short_in[...] + finish_body(bg, conv, gfull, act, proj, sf, extra, gp, ext)


def pieces_kernel(steps, per, back, more, *refs):
    count = steps * per // 2
    weights, refs = refs[:count], refs[count:]
    if back:
        gated, og, refs = refs[0], refs[1 : 1 + per], refs[1 + per :]
        if more:
            acc_in, refs = refs[0], refs[2:]
        result, acc, buf, sems = refs
    else:
        gated, (result, buf, sems) = refs[0], refs[1 + more :]
    step = pl.program_id(0)
    chans = gated.shape[1]
    width = buf.shape[2] // per

    def copies(i):
        return [
            pltpu.make_async_copy(
                weights[(per * i + j) // 2].at[pl.ds((per * i + j) % 2 * chans, chans)],
                buf.at[i % 2, :, pl.ds(j * width, width)],
                sems.at[i % 2, j],
            )
            for j in range(per)
        ]

    @pl.when(step == 0)
    def _():
        for c in copies(0):
            c.start()
        if back:
            acc[...] = acc_in[...] if more else jnp.zeros_like(acc)

    for i in range(steps):

        @pl.when(step == i)
        def _(i=i):
            if i + 1 < steps:
                for c in copies(i + 1):
                    c.start()
            for c in copies(i):
                c.wait()

    w = buf[step % 2]
    result[...] = jnp.dot(gated[...], w, preferred_element_type=f32).astype(bf16)
    if back:
        acc[...] += lax.dot_general(
            jnp.concatenate([o[...] for o in og], 1),
            w,
            (((1,), (1,)), ((), ())),
            preferred_element_type=f32,
        )


def multiply_pieces(weights, table, gated, out_grad=None, total=None, before=None, per=SIDE):
    rows, chans = gated.shape
    width = weights[0].shape[1]
    steps = 2 * len(weights) // per
    back, more = out_grad is not None, before is not None
    total = total or steps
    offset = before[0] if more else 0
    whole = pl.BlockSpec((rows, chans), lambda i, c: (0, 0), pipeline_mode=pl.Buffered(1))
    in_specs = [pl.BlockSpec(memory_space=pl.ANY)] * len(weights) + [whole]
    operands = [*weights, gated]
    aliases = {}
    if back:
        in_specs += [
            pl.BlockSpec((rows, width), lambda i, c, j=j: (0, c[1 + per * (i + offset) + j])) for j in range(per)
        ]
        operands += [out_grad] * per
        if more:
            in_specs.append(whole)
            operands.append(before[2])
    if more:
        in_specs.append(pl.BlockSpec(memory_space=pl.ANY))
        operands.append(before[1])
        aliases = {len(operands): 0}
    result_shape = jax.ShapeDtypeStruct((rows, total * per * width), bf16)
    result_spec = pl.BlockSpec((rows, per * width), lambda i, c: (0, i + offset))

    def kernel(cols_ref, *refs):
        del cols_ref
        pieces_kernel(steps, per, back, more, *refs)

    return pl.pallas_call(
        kernel,
        grid_spec=pltpu.PrefetchScalarGridSpec(
            num_scalar_prefetch=1,
            grid=(steps,),
            in_specs=in_specs,
            out_specs=[result_spec] + [whole] * back,
            scratch_shapes=[
                pltpu.VMEM((2, chans, per * width), bf16),
                pltpu.SemaphoreType.DMA((2, per)),
            ],
        ),
        out_shape=[result_shape] + [jax.ShapeDtypeStruct((rows, chans), f32)] * back,
        input_output_aliases=aliases,
        cost_estimate=pl.CostEstimate(
            flops=(2 + 2 * back) * rows * chans * width * per * steps,
            bytes_accessed=per * steps * (2 * chans * width + 4 * rows * width) + 6 * rows * chans,
            transcendentals=0,
        ),
        name="pieces",
    )(table, *operands)


def collect_kernel(counts, cols, *refs):
    mixed = refs[-1]
    width = mixed.shape[1] // sum(counts)
    begin = 0
    for ref, count in zip(refs, counts):

        @pl.loop(0, count)
        def _(p, ref=ref, begin=begin):
            lanes = pl.ds(pl.multiple_of(p * width, width), width)
            start = pl.multiple_of(cols[1 + begin + p] * width, width)
            mixed[:, pl.ds(start, width)] = ref[:, lanes]

        begin += count


def on_device(projected, short_filter, long_filter, skip_gain, out_weight, out_grad, left_source):
    rows, chans = projected.shape[1:]
    width = out_weight.shape[1] // 2
    ctx_count, tp_count = lax.axis_size("ctx"), lax.axis_size("tp")
    me = lax.axis_index("ctx").astype(jnp.uint32)
    zu, xu = me >> 2, me & 3
    zi, xi = zu.astype(jnp.int32), xu.astype(jnp.int32)

    def ring(value, axis, step):
        if axis == "x":
            pairs = [(d, d // SIDE * SIDE + (d + step) % SIDE) for d in range(ctx_count)]
        else:
            pairs = [(d, (d + SIDE * step) % ctx_count) for d in range(ctx_count)]
        return lax.ppermute(value, "ctx", pairs)

    def swap(value, axis, k):
        shift = {"x": k, "z": k * SIDE}[axis]
        return lax.ppermute(value, "ctx", [(d, d ^ shift) for d in range(ctx_count)])

    def gather(piece, first, second):
        h = piece.shape[0] // 2
        p, q = ring(piece, first, 1), ring(piece, first, -1)
        t, b = ring(p[:h], first, 1), ring(q[h:], first, -1)
        one, two = jnp.concatenate([piece, p], 0), jnp.concatenate([q, t, b], 0)
        op, oq = ring(one, second, 1), ring(one, second, -1)
        tp_, tq = ring(two, second, 1), ring(two, second, -1)
        far_one = ring(op, second, 1)
        far_two = ring(tq, second, -1)
        return [one, two], [op, tp_, oq, tq], [far_one, far_two]

    def blocks(half, near, far_steps):
        steps = [(f, n) if half == 0 else (n, f) for f in far_steps for n in near]
        return [(half, z, x) for z, x in steps]

    order4 = (0, -1, 1, 2)
    halves, dz, dx = np.array(
        [b for far in ((0,), (-1, 1), (2,)) for half in (0, 1) for b in blocks(half, order4, far)]
    ).T
    table = 2 * (((zi + dz) & 3) * SIDE + ((xi + dx) & 3)) + halves
    table = jnp.concatenate([jnp.reshape(zi, (1,)), table]).astype(jnp.int32)

    positions = jnp.arange(ctx_count, dtype=jnp.int32)
    matches = left_source[None, :] == positions[:, None]
    readers = jnp.where(
        jnp.any(matches, 1), jnp.sum(jnp.where(matches, positions[None, :], 0), 1), -1
    )

    def pick(options, index):
        low = jnp.where(index == 1, options[1], options[0])
        high = jnp.where(index == 3, options[3], options[2])
        return jnp.where(index >= 2, high, low)

    def at(table, index):
        return lax.dynamic_index_in_dim(table, index, 0, keepdims=False)

    def along_x(payloads):
        return [payloads[0]] + [swap(payloads[k], "x", k) for k in (1, 2, 3)]

    def along_z(payloads):
        return [payloads[0]] + [swap(payloads[k], "z", k) for k in (1, 2, 3)]

    def chosen(got, sources):
        columns = (sources & 3) ^ xi
        return [pick(got, at(columns, me ^ (4 * k))) for k in range(SIDE)]

    def landed(got, sources):
        value = pick(got, at(((sources >> 2) & 3) ^ zi, me))
        return jnp.where(at(sources, me) >= 0, value, jnp.zeros_like(value))

    near = projected[1:, rows - BLK - PAD :].astype(f32)
    tail = jnp.zeros((2, BLK, chans), f32)
    for s in range(3):
        tail = tail + short_filter[1:, s][:, None] * near[:, PAD - s : PAD - s + BLK]
    raw = projected[:, rows - 2 :].reshape(6, chans)
    sent = jnp.concatenate(
        [(tail[0] * tail[1]).astype(bf16), raw, jnp.zeros((2, chans), bf16)], 0
    )
    got = along_x([sent] * SIDE)
    to_z = chosen(got, left_source)
    got = along_z(to_z)
    left = landed(got, left_source)

    near_a, mid_a, far_a = gather(out_weight[:, :width], "x", "z")
    near_b, mid_b, far_b = gather(out_weight[:, width:], "z", "x")

    fwd = jnp.asarray(forward_matrix())
    inv_late, inv_now, inv_lag = (jnp.asarray(inverse_matrix(s)) for s in (BLK, 0, -BLK))
    skip_row = skip_gain[None, :]
    tile = 256
    grid = (chans // tile,)
    nb = rows // BLK

    def col(*lead, t=tile):
        return pl.BlockSpec((*lead, t), lambda i, *_: (*([0] * len(lead)), i))

    const = pl.BlockSpec((2 * BLK, 2 * BLK), lambda i, *_: (0, 0))
    const_inv = pl.BlockSpec((BLK, 2 * BLK), lambda i, *_: (0, 0))
    forward = pl.pallas_call(
        forward_kernel,
        grid=grid,
        in_specs=[
            col(3, rows), col(BLK + PAD), col(3, 3), col(BLK), col(1), const, const_inv,
        ],
        out_specs=[col(rows), col(rows), col(3, rows), col(nb, 2 * BLK), col(2 * BLK)],
        scratch_shapes=[
            pltpu.VMEM((3, rows + PAD, tile), f32),
            pltpu.VMEM((2 * BLK, (nb + 1) * tile), bf16),
            pltpu.VMEM((2 * BLK, (nb + 1) * tile), f32),
            pltpu.VMEM((2 * BLK, nb * tile), bf16),
            pltpu.VMEM((BLK, nb * tile), f32),
        ],
        out_shape=[
            jax.ShapeDtypeStruct((rows, chans), bf16),
            jax.ShapeDtypeStruct((rows, chans), f32),
            jax.ShapeDtypeStruct((3, rows, chans), f32),
            jax.ShapeDtypeStruct((nb, 2 * BLK, chans), f32),
            jax.ShapeDtypeStruct((2 * BLK, chans), f32),
        ],
        cost_estimate=pl.CostEstimate(
            flops=8_000_000_000, bytes_accessed=20 << 20, transcendentals=0
        ),
        name="forward",
    )
    gated, conv, act, mspec, fspec = forward(
        projected, left, short_filter, long_filter, skip_row, fwd, inv_late
    )

    def scatter(value):
        return lax.psum_scatter(value, "tp", scatter_dimension=0, tiled=True)

    early = multiply_pieces(near_a + near_b, table, gated, out_grad, 8)
    out1, acc = multiply_pieces(
        mid_a + mid_b, table, gated, out_grad, 8, (2, *early)
    )
    quarter = BLK // SIDE
    lasts = [w.reshape(2, chans, width) for w in far_a + far_b]
    last_spec = pl.BlockSpec((2, tile, width), lambda i, c: (0, i, 0))

    def out_grad_rows(n):
        return [pl.BlockSpec((n, width), lambda i, c, j=j: (0, c[1 + 6 * SIDE + j])) for j in range(2 * SIDE)]

    def first_rows(n, *lead, t=tile):
        zeros = [0] * len(lead)
        return pl.BlockSpec((*lead, n, t), lambda i, c: (*zeros, 0, i))

    big = 2 * tile
    head = pl.pallas_call(
        head_kernel,
        grid_spec=pltpu.PrefetchScalarGridSpec(
            num_scalar_prefetch=1,
            grid=(chans // big,),
            in_specs=[
                first_rows(BLK + PAD, t=big),
                first_rows(BLK + PAD, 1, t=big),
                pl.BlockSpec(
                    (pl.Element(2), pl.Element(PAD), pl.Element(big)),
                    lambda i, c: (1, 0, i * big),
                ),
                first_rows(PAD, t=big),
                col(BLK, t=big),
                col(1, t=big),
                *out_grad_rows(BLK + PAD),
                *[pl.BlockSpec((2, big, width), lambda i, c: (0, i, 0))] * 4,
            ],
            out_specs=col(BLK + PAD, t=big),
            scratch_shapes=[pltpu.VMEM((BLK + PAD, big), f32)],
        ),
        out_shape=jax.ShapeDtypeStruct((BLK + PAD, chans), bf16),
        cost_estimate=pl.CostEstimate(
            flops=600_000_000, bytes_accessed=6 << 20, transcendentals=0
        ),
        name="head",
    )
    pay = head(table, acc, act, act, conv, long_filter, skip_row, *[out_grad] * (2 * SIDE), *lasts)
    got = along_x([pay] * SIDE)

    long_shape = jax.ShapeDtypeStruct((quarter, chans), bf16)
    backward = pl.pallas_call(
        backward_kernel,
        grid_spec=pltpu.PrefetchScalarGridSpec(
            num_scalar_prefetch=1,
            grid=grid,
            in_specs=[
                col(rows),
                first_rows(rows, 1),
                col(nb, 2 * BLK),
                col(2 * BLK),
                col(1),
                const,
                const_inv,
                const_inv,
                *out_grad_rows(rows),
                *[last_spec] * 4,
            ],
            out_specs=[col(rows)] + [col(quarter)] * 4 + [col(rows)],
            scratch_shapes=[
                pltpu.VMEM((BLK, tile), f32),
                pltpu.VMEM((2 * BLK, nb * tile), bf16),
                pltpu.VMEM((2 * BLK, nb * tile), f32),
                pltpu.VMEM((2 * BLK, nb * tile), bf16),
                pltpu.VMEM((2 * BLK, tile), bf16),
                pltpu.VMEM((BLK, nb * tile), f32),
            ],
        ),
        out_shape=[jax.ShapeDtypeStruct((rows, chans), f32)]
        + [long_shape] * 4
        + [jax.ShapeDtypeStruct((rows, chans), f32)],
        cost_estimate=pl.CostEstimate(
            flops=8_000_000_000, bytes_accessed=20 << 20, transcendentals=0
        ),
        name="backward",
    )
    bg, *longs, gmix = backward(
        table, acc, act, mspec, fspec, skip_row, fwd, inv_now, inv_lag,
        *[out_grad] * (2 * SIDE), *lasts,
    )

    to_z = chosen(got, readers)
    got = along_z([jnp.concatenate([v, part], 0) for v, part in zip(to_z, longs)])
    right = landed([g[: BLK + PAD] for g in got], readers)
    sums = [g[BLK + PAD :].astype(f32) for g in got]
    my_quarter = (sums[0] + sums[1]) + (sums[2] + sums[3])

    (out1,) = multiply_pieces(
        far_a + far_b, table, gated, None, 8, (6, out1)
    )
    out1 = scatter(out1)

    low = rows - BLK - PAD

    def rows_at(start, n, *lead, t=tile):
        zeros = [0] * len(lead)
        dims = [pl.Element(d) for d in (*lead, n, t)]
        return pl.BlockSpec(tuple(dims), lambda i: (*zeros, start, i * t))

    def acts_at(start, n, t=tile):
        return pl.BlockSpec(
            (pl.Element(2), pl.Element(n), pl.Element(t)), lambda i: (1, start, i * t)
        )

    gp_shape = jax.ShapeDtypeStruct((3, rows, chans), bf16)
    short_shape = jax.ShapeDtypeStruct((16, chans), f32)
    top = pl.pallas_call(
        top_kernel,
        grid=grid,
        in_specs=[
            rows_at(0, low), rows_at(0, low), rows_at(0, low), acts_at(0, low),
            rows_at(low, PAD), rows_at(low, PAD), rows_at(low, PAD), acts_at(low, PAD),
            rows_at(0, low, 3), col(3, 3),
        ],
        out_specs=[rows_at(0, low, 3), col(16)],
        out_shape=[gp_shape, short_shape],
        scratch_shapes=[pltpu.VMEM((3, low + PAD, tile), f32)],
        cost_estimate=pl.CostEstimate(
            flops=200_000_000, bytes_accessed=10 << 20, transcendentals=0
        ),
        name="top",
    )
    gp, short = top(bg, conv, gmix, act, bg, conv, gmix, act, projected, short_filter)
    rest = rows - low
    bottom = pl.pallas_call(
        bottom_kernel,
        grid=(chans // big,),
        in_specs=[
            rows_at(low, rest, t=big), rows_at(low, rest, t=big), rows_at(low, rest, t=big), acts_at(low, rest, t=big),
            col(BLK + PAD, t=big), rows_at(low, rest, 3, t=big), col(3, 3, t=big), col(2 * BLK, t=big), const, const_inv, col(16, t=big),
            pl.BlockSpec(memory_space=pl.ANY),
        ],
        out_specs=[rows_at(low, rest, 3, t=big), col(16, t=big)],
        out_shape=[gp_shape, short_shape],
        scratch_shapes=[pltpu.VMEM((3, rest + PAD, big), f32), pltpu.VMEM((rest, big), f32)],
        input_output_aliases={11: 0},
        cost_estimate=pl.CostEstimate(
            flops=2_000_000_000, bytes_accessed=5 << 20, transcendentals=0
        ),
        name="bottom",
    )
    gp, short = bottom(
        bg, conv, gmix, act, right, projected, short_filter, fspec, fwd, inv_now, short, gp
    )

    message = jnp.concatenate([my_quarter, short], 0)
    for along in (along_x, along_z):
        got = along([message.astype(bf16)] * SIDE)
        wide = [g.astype(f32) for g in got]
        message = (wide[0] + wide[1]) + (wide[2] + wide[3])
    long_total = jnp.concatenate([pick(got, zi ^ q)[:quarter] for q in range(SIDE)], 0)
    short_total = message[quarter : quarter + 9].reshape(3, 3, chans)

    share = rows // tp_count
    counts = tuple(o.shape[1] // width for o in (out1,))
    collect = pl.pallas_call(
        lambda cols, *refs: collect_kernel(counts, cols, *refs),
        grid_spec=pltpu.PrefetchScalarGridSpec(
            num_scalar_prefetch=1,
            grid=(1,),
            in_specs=[pl.BlockSpec(o.shape, lambda i, c: (0, 0)) for o in (out1,)],
            out_specs=pl.BlockSpec((share, 2 * width * ctx_count), lambda i, c: (0, 0)),
        ),
        out_shape=jax.ShapeDtypeStruct((share, 2 * width * ctx_count), bf16),
        cost_estimate=pl.CostEstimate(flops=10_000_000, bytes_accessed=5 << 20, transcendentals=0),
        name="collect",
    )
    mixed = collect(table, out1)

    scale = 1.0 / math.sqrt(rows * ctx_count)
    return mixed, gp, long_total.astype(f32) * scale, short_total * scale


def solution(mesh):
    placed = (
        P(None, "ctx", "tp"),
        P(None, None, "tp"),
        P(None, "tp"),
        P("tp"),
        P("tp", "ctx"),
        P("ctx", None),
        P(),
    )
    return jax.shard_map(
        on_device,
        mesh=mesh,
        in_specs=placed,
        out_specs=(
            P(("ctx", "tp"), None),
            P(None, "ctx", "tp"),
            P(None, "tp"),
            P(None, None, "tp"),
        ),
        check_vma=False,
    )
```

```python
import math

import jax
import jax.numpy as jnp
import numpy as np
from jax import lax
from jax.experimental import pallas as pl
from jax.experimental.pallas import tpu as pltpu
from jax.sharding import PartitionSpec as P


f32, bf16 = jnp.float32, jnp.bfloat16
BLK = 128
SIDE = 4
PAD = 8


def split_hi_lo(matrix):
    hi = matrix.astype(np.float32).astype(bf16)
    lo = (matrix - hi.astype(np.float64)).astype(np.float32).astype(bf16)
    return hi, lo


def angles(times):
    freqs = np.concatenate([np.arange(0, BLK, 2), np.arange(1, BLK, 2)]) + 0.5
    return 2.0 * np.pi * freqs[:, None] * times[None, :] / (2 * BLK)


def forward_matrix():
    th = angles(np.arange(BLK, dtype=np.float64))
    hi, lo = split_hi_lo(np.concatenate([np.cos(th), -np.sin(th)], 0))
    return np.concatenate([hi, lo], 1)


def inverse_matrix(start):
    th = angles(np.arange(start, start + BLK, dtype=np.float64)).T
    return (np.concatenate([np.cos(th), -np.sin(th)], 1) / BLK).astype(np.float32).astype(bf16)


def spectrum(fwd, rows):
    return jnp.dot(fwd, jnp.concatenate([rows, rows], 0), preferred_element_type=f32)


def delay(v):
    h = BLK // 2
    re, im = v[:BLK], v[BLK:]
    return jnp.concatenate([im[:h], -im[h:], -re[:h], re[h:]], 0)


def product_conj(a, b):
    ar, ai, br, bi = a[:BLK], a[BLK:], b[:BLK], b[BLK:]
    return jnp.concatenate([ar * br + ai * bi, ai * br - ar * bi], 0)


def invert(inv, spec):
    return jnp.dot(inv[...], spec, preferred_element_type=f32)


def chunks(total, size):
    return [(r, min(size, total - r)) for r in range(0, total, size)]


ROWS = 32
FREQS = 16


def window_rows(spec, c, here, after):
    sr, si = slice(c, c + FREQS), slice(BLK + c, BLK + c + FREQS)
    wr, wi = spec[sr, here], spec[si, here]
    if after is None:
        return wr, wi
    ar, ai = spec[sr, after], spec[si, after]
    if c < BLK // 2:
        return wr + ai, wi - ar
    return wr - ai, wi + ar


def forward_kernel(
    proj, halo, sf, lf, skip, fwd, inv, gated, conv, act, mspec, fspec, ext, mix, spec, ybuf, out
):
    rows = proj.shape[1]
    nb, wide = rows // BLK, proj.shape[2]
    fmat = fwd[...]
    edge = halo[BLK : BLK + PAD].astype(f32)
    for m in range(3):
        ext[m, PAD - 2 : PAD] = edge[2 * m : 2 * m + 2]
        for r, n in chunks(rows, ROWS):
            ext[m, PAD + r : PAD + r + n] = proj[m, r : r + n].astype(f32)
    for h in range(2):
        mix[h * BLK : (h + 1) * BLK, :wide] = halo[:BLK]
    for r, n in chunks(rows, ROWS):
        acts = []
        for m in range(3):
            total = sf[m, 0:1] * ext[m, PAD + r : PAD + r + n]
            for s in (1, 2):
                total = total + sf[m, s : s + 1] * ext[m, PAD - s + r : PAD - s + r + n]
            act[m, r : r + n] = total
            acts.append(total)
        mixin = (acts[1] * acts[2]).astype(bf16)
        at, lane = r % BLK, (r // BLK + 1) * wide
        for h in range(2):
            mix[h * BLK + at : h * BLK + at + n, lane : lane + wide] = mixin
    filt = spectrum(fmat, lf[...])
    fspec[...] = filt
    spec[...] = jnp.dot(fmat, mix[...], preferred_element_type=f32)
    for c in range(0, BLK, FREQS):
        fr, fi = fspec[c : c + FREQS], fspec[BLK + c : BLK + c + FREQS]
        for b in range(nb):
            lanes = slice(b * wide, (b + 1) * wide)
            wr, wi = window_rows(spec, c, lanes, slice((b + 1) * wide, (b + 2) * wide))
            mspec[b, c : c + FREQS] = wr
            mspec[b, BLK + c : BLK + c + FREQS] = wi
            ybuf[c : c + FREQS, lanes] = (fr * wr - fi * wi).astype(bf16)
            ybuf[BLK + c : BLK + c + FREQS, lanes] = (fr * wi + fi * wr).astype(bf16)
    out[...] = invert(inv, ybuf[...])
    for r, n in chunks(rows, ROWS):
        at, lane = r % BLK, r // BLK * wide
        mixin = mix[at : at + n, lane + wide : lane + 2 * wide].astype(f32)
        full = out[at : at + n, lane : lane + wide] + skip[...] * mixin
        conv[r : r + n] = full
        gated[r : r + n] = (act[0, r : r + n] * full).astype(bf16)


def backward_kernel(place, acc, act0, mspec, fspec, skip, fwd, inv, invlag, *refs):
    og, refs = refs[: 2 * SIDE], refs[2 * SIDE :]
    weights, refs = refs[:4], refs[4:]
    bg, long0, long1, long2, long3, gmix, lagbuf, gbuf, spec, ybuf, lagy, out = refs
    rows, wide = bg.shape
    nb = rows // BLK
    bg[...] = acc[...] + lax.dot_general(
        jnp.concatenate([o[...] for o in og], 1),
        jnp.concatenate([w[n] for w in weights for n in range(2)], 1),
        (((1,), (1,)), ((), ())),
        preferred_element_type=f32,
    )
    for r, n in chunks(rows, ROWS):
        g = (bg[r : r + n] * act0[0, r : r + n]).astype(bf16)
        at, lane = r % BLK, r // BLK * wide
        for h in range(2):
            gbuf[h * BLK + at : h * BLK + at + n, lane : lane + wide] = g
    spec[...] = jnp.dot(fwd[...], gbuf[...], preferred_element_type=f32)
    for c in range(0, BLK, FREQS):
        sr, si = slice(c, c + FREQS), slice(BLK + c, BLK + c + FREQS)
        fr, fi = fspec[sr], fspec[si]
        lag_r = lag_i = None
        for b in range(nb):
            lanes = slice(b * wide, (b + 1) * wide)
            after = slice((b + 1) * wide, (b + 2) * wide) if b + 1 < nb else None
            gr, gi, mr, mi = spec[sr, lanes], spec[si, lanes], mspec[b, sr], mspec[b, si]
            pr, pi = gr * mr + gi * mi, gi * mr - gr * mi
            lag_r, lag_i = (pr, pi) if b == 0 else (lag_r + pr, lag_i + pi)
            wr, wi = window_rows(spec, c, lanes, after)
            ybuf[sr, lanes] = (wr * fr + wi * fi).astype(bf16)
            ybuf[si, lanes] = (wi * fr - wr * fi).astype(bf16)
        lagy[sr] = lag_r.astype(bf16)
        lagy[si] = lag_i.astype(bf16)
    lagbuf[...] = invert(invlag, lagy[...])
    quarter = BLK // SIDE
    for k, part in enumerate((long0, long1, long2, long3)):
        start = pl.multiple_of((place[0] ^ k) * quarter, quarter)
        part[...] = lagbuf[pl.ds(start, quarter)].astype(bf16)
    out[...] = invert(inv, ybuf[...])
    for r, n in chunks(rows, ROWS):
        at, lane = r % BLK, r // BLK * wide
        g = gbuf[at : at + n, lane : lane + wide].astype(f32)
        gmix[r : r + n] = out[at : at + n, lane : lane + wide] + skip[...] * g


def head_kernel(place, acc, act0, act12, convh, lf, skip, *refs):
    del place
    og, refs = refs[: 2 * SIDE], refs[2 * SIDE :]
    weights, (pay, ext) = refs[:4], refs[4:]
    bg = acc[...] + lax.dot_general(
        jnp.concatenate([o[...] for o in og], 1),
        jnp.concatenate([w[n] for w in weights for n in range(2)], 1),
        (((1,), (1,)), ((), ())),
        preferred_element_type=f32,
    )
    g = (bg * act0[0]).astype(bf16)
    ext[...] = g.astype(f32)
    taps = lf[...].astype(f32)
    gm0 = jnp.sum(taps * ext[:BLK], axis=0, keepdims=True) + skip[...] * ext[0:1]
    gm1 = jnp.sum(taps * ext[1 : BLK + 1], axis=0, keepdims=True) + skip[...] * ext[1:2]
    gm = jnp.concatenate([gm0, gm1], 0)
    edge = [bg[:2] * convh[:2], gm * act12[1, :2], gm * act12[0, :2], jnp.zeros_like(gm)]
    pay[:BLK] = g[:BLK]
    pay[BLK:] = jnp.concatenate(edge, 0).astype(bf16)


def finish_body(bg, conv, gmix, act, proj, sf, extra, gp, ext):
    rows, wide = bg.shape
    sums = []
    for m in range(3):
        for r, n in chunks(rows, ROWS):
            if m == 0:
                ext[m, r : r + n] = bg[r : r + n] * conv[r : r + n]
            else:
                ext[m, r : r + n] = gmix[r : r + n] * act[2 - m, r : r + n]
        ext[m, rows : rows + PAD] = extra[m]
        parts = [jnp.zeros((8, wide), f32)] * 3
        for r, n in chunks(rows, ROWS):
            x = proj[m, r : r + n].astype(f32)
            total = None
            for s in range(3):
                moved = ext[m, r + s : r + s + n]
                term = sf[m, s : s + 1] * moved
                total = term if s == 0 else total + term
                parts[s] = parts[s] + jnp.sum((x * moved).reshape(n // 8, 8, wide), axis=0)
            gp[m, r : r + n] = total.astype(bf16)
        sums += [jnp.sum(p, axis=0, keepdims=True) for p in parts]
    return jnp.concatenate(sums + [jnp.zeros((7, wide), f32)], 0)


def top_kernel(bg, conv, gmix, act, bgn, convn, gmixn, actn, proj, sf, gp, short, ext):
    extra = [bgn[...] * convn[...], gmixn[...] * actn[1], gmixn[...] * actn[0]]
    short[...] = finish_body(bg, conv, gmix, act, proj, sf, extra, gp, ext)


def bottom_kernel(
    bg, conv, gmix, act, halo, proj, sf, fspec, fwd, inv, short_in, gp_in, gp, short, ext, gfull
):
    del gp_in
    rows = bg.shape[0]
    late = delay(spectrum(fwd[...], halo[:BLK]))
    gfull[: rows - BLK] = gmix[: rows - BLK]
    gfull[rows - BLK :] = gmix[rows - BLK :] + invert(inv, product_conj(late, fspec[...]).astype(bf16))
    edge = halo[BLK : BLK + PAD].astype(f32)
    zeros = jnp.zeros((PAD - 2, edge.shape[1]), f32)
    extra = [jnp.concatenate([edge[2 * m : 2 * m + 2], zeros], 0) for m in range(3)]
    short[...] = short_in[...] + finish_body(bg, conv, gfull, act, proj, sf, extra, gp, ext)


def pieces_kernel(steps, per, back, more, *refs):
    count = steps * per // 2
    weights, refs = refs[:count], refs[count:]
    if back:
        gated, og, refs = refs[0], refs[1 : 1 + per], refs[1 + per :]
        if more:
            acc_in, refs = refs[0], refs[2:]
        result, acc, buf, sems = refs
    else:
        gated, (result, buf, sems) = refs[0], refs[1 + more :]
    step = pl.program_id(0)
    chans = gated.shape[1]
    width = buf.shape[2] // per

    def copies(i):
        return [
            pltpu.make_async_copy(
                weights[(per * i + j) // 2].at[pl.ds((per * i + j) % 2 * chans, chans)],
                buf.at[i % 2, :, pl.ds(j * width, width)],
                sems.at[i % 2, j],
            )
            for j in range(per)
        ]

    @pl.when(step == 0)
    def _():
        for c in copies(0):
            c.start()
        if back:
            acc[...] = acc_in[...] if more else jnp.zeros_like(acc)

    for i in range(steps):

        @pl.when(step == i)
        def _(i=i):
            if i + 1 < steps:
                for c in copies(i + 1):
                    c.start()
            for c in copies(i):
                c.wait()

    w = buf[step % 2]
    result[...] = jnp.dot(gated[...], w, preferred_element_type=f32).astype(bf16)
    if back:
        acc[...] += lax.dot_general(
            jnp.concatenate([o[...] for o in og], 1),
            w,
            (((1,), (1,)), ((), ())),
            preferred_element_type=f32,
        )


def multiply_pieces(weights, table, gated, out_grad=None, total=None, before=None, per=SIDE):
    rows, chans = gated.shape
    width = weights[0].shape[1]
    steps = 2 * len(weights) // per
    back, more = out_grad is not None, before is not None
    total = total or steps
    offset = before[0] if more else 0
    whole = pl.BlockSpec((rows, chans), lambda i, c: (0, 0), pipeline_mode=pl.Buffered(1))
    in_specs = [pl.BlockSpec(memory_space=pl.ANY)] * len(weights) + [whole]
    operands = [*weights, gated]
    aliases = {}
    if back:
        in_specs += [
            pl.BlockSpec((rows, width), lambda i, c, j=j: (0, c[1 + per * (i + offset) + j])) for j in range(per)
        ]
        operands += [out_grad] * per
        if more:
            in_specs.append(whole)
            operands.append(before[2])
    if more:
        in_specs.append(pl.BlockSpec(memory_space=pl.ANY))
        operands.append(before[1])
        aliases = {len(operands): 0}
    result_shape = jax.ShapeDtypeStruct((rows, total * per * width), bf16)
    result_spec = pl.BlockSpec((rows, per * width), lambda i, c: (0, i + offset))

    def kernel(cols_ref, *refs):
        del cols_ref
        pieces_kernel(steps, per, back, more, *refs)

    return pl.pallas_call(
        kernel,
        grid_spec=pltpu.PrefetchScalarGridSpec(
            num_scalar_prefetch=1,
            grid=(steps,),
            in_specs=in_specs,
            out_specs=[result_spec] + [whole] * back,
            scratch_shapes=[
                pltpu.VMEM((2, chans, per * width), bf16),
                pltpu.SemaphoreType.DMA((2, per)),
            ],
        ),
        out_shape=[result_shape] + [jax.ShapeDtypeStruct((rows, chans), f32)] * back,
        input_output_aliases=aliases,
        cost_estimate=pl.CostEstimate(
            flops=(2 + 2 * back) * rows * chans * width * per * steps,
            bytes_accessed=per * steps * (2 * chans * width + 4 * rows * width) + 6 * rows * chans,
            transcendentals=0,
        ),
        name="pieces",
    )(table, *operands)


def collect_kernel(counts, cols, *refs):
    mixed = refs[-1]
    width = mixed.shape[1] // sum(counts)
    begin = 0
    for ref, count in zip(refs, counts):

        @pl.loop(0, count)
        def _(p, ref=ref, begin=begin):
            lanes = pl.ds(pl.multiple_of(p * width, width), width)
            start = pl.multiple_of(cols[1 + begin + p] * width, width)
            mixed[:, pl.ds(start, width)] = ref[:, lanes]

        begin += count


def on_device(projected, short_filter, long_filter, skip_gain, out_weight, out_grad, left_source):
    rows, chans = projected.shape[1:]
    width = out_weight.shape[1] // 2
    ctx_count, tp_count = lax.axis_size("ctx"), lax.axis_size("tp")
    me = lax.axis_index("ctx").astype(jnp.uint32)
    zu, xu = me >> 2, me & 3
    zi, xi = zu.astype(jnp.int32), xu.astype(jnp.int32)

    def ring(value, axis, step):
        if axis == "x":
            pairs = [(d, d // SIDE * SIDE + (d + step) % SIDE) for d in range(ctx_count)]
        else:
            pairs = [(d, (d + SIDE * step) % ctx_count) for d in range(ctx_count)]
        return lax.ppermute(value, "ctx", pairs)

    def swap(value, axis, k):
        shift = {"x": k, "z": k * SIDE}[axis]
        return lax.ppermute(value, "ctx", [(d, d ^ shift) for d in range(ctx_count)])

    def gather(piece, first, second):
        h = piece.shape[0] // 2
        p, q = ring(piece, first, 1), ring(piece, first, -1)
        t, b = ring(p[:h], first, 1), ring(q[h:], first, -1)
        one, two = jnp.concatenate([piece, p], 0), jnp.concatenate([q, t, b], 0)
        op, oq = ring(one, second, 1), ring(one, second, -1)
        tp_, tq = ring(two, second, 1), ring(two, second, -1)
        far_one = ring(op, second, 1)
        far_two = ring(tq, second, -1)
        return [one, two], [op, tp_, oq, tq], [far_one, far_two]

    def blocks(half, near, far_steps):
        steps = [(f, n) if half == 0 else (n, f) for f in far_steps for n in near]
        return [(half, z, x) for z, x in steps]

    order4 = (0, -1, 1, 2)
    halves, dz, dx = np.array(
        [b for far in ((0,), (-1, 1), (2,)) for half in (0, 1) for b in blocks(half, order4, far)]
    ).T
    table = 2 * (((zi + dz) & 3) * SIDE + ((xi + dx) & 3)) + halves
    table = jnp.concatenate([jnp.reshape(zi, (1,)), table]).astype(jnp.int32)

    positions = jnp.arange(ctx_count, dtype=jnp.int32)
    matches = left_source[None, :] == positions[:, None]
    readers = jnp.where(
        jnp.any(matches, 1), jnp.sum(jnp.where(matches, positions[None, :], 0), 1), -1
    )

    def pick(options, index):
        low = jnp.where(index == 1, options[1], options[0])
        high = jnp.where(index == 3, options[3], options[2])
        return jnp.where(index >= 2, high, low)

    def at(table, index):
        return lax.dynamic_index_in_dim(table, index, 0, keepdims=False)

    def along_x(payloads):
        return [payloads[0]] + [swap(payloads[k], "x", k) for k in (1, 2, 3)]

    def along_z(payloads):
        return [payloads[0]] + [swap(payloads[k], "z", k) for k in (1, 2, 3)]

    def chosen(got, sources):
        return [pick(got, (at(sources, me ^ (4 * k)) & 3) ^ xi) for k in range(SIDE)]

    def landed(got, sources):
        source = at(sources, me)
        value = pick(got, ((source >> 2) & 3) ^ zi)
        return jnp.where(source >= 0, value, jnp.zeros_like(value))

    near = projected[1:, rows - BLK - PAD :].astype(f32)
    tail = jnp.zeros((2, BLK, chans), f32)
    for s in range(3):
        tail = tail + short_filter[1:, s][:, None] * near[:, PAD - s : PAD - s + BLK]
    raw = projected[:, rows - 2 :].reshape(6, chans)
    sent = jnp.concatenate(
        [(tail[0] * tail[1]).astype(bf16), raw, jnp.zeros((2, chans), bf16)], 0
    )
    got = along_x([sent] * SIDE)
    to_z = chosen(got, left_source)
    got = along_z(to_z)
    left = landed(got, left_source)

    near_a, mid_a, far_a = gather(out_weight[:, :width], "x", "z")
    near_b, mid_b, far_b = gather(out_weight[:, width:], "z", "x")

    fwd = jnp.asarray(forward_matrix())
    inv_late, inv_now, inv_lag = (jnp.asarray(inverse_matrix(s)) for s in (BLK, 0, -BLK))
    skip_row = skip_gain[None, :]
    tile = 256
    grid = (chans // tile,)
    nb = rows // BLK

    def col(*lead, t=tile):
        return pl.BlockSpec((*lead, t), lambda i, *_: (*([0] * len(lead)), i))

    const = pl.BlockSpec((2 * BLK, 2 * BLK), lambda i, *_: (0, 0))
    const_inv = pl.BlockSpec((BLK, 2 * BLK), lambda i, *_: (0, 0))
    forward = pl.pallas_call(
        forward_kernel,
        grid=grid,
        in_specs=[
            col(3, rows), col(BLK + PAD), col(3, 3), col(BLK), col(1), const, const_inv,
        ],
        out_specs=[col(rows), col(rows), col(3, rows), col(nb, 2 * BLK), col(2 * BLK)],
        scratch_shapes=[
            pltpu.VMEM((3, rows + PAD, tile), f32),
            pltpu.VMEM((2 * BLK, (nb + 1) * tile), bf16),
            pltpu.VMEM((2 * BLK, (nb + 1) * tile), f32),
            pltpu.VMEM((2 * BLK, nb * tile), bf16),
            pltpu.VMEM((BLK, nb * tile), f32),
        ],
        out_shape=[
            jax.ShapeDtypeStruct((rows, chans), bf16),
            jax.ShapeDtypeStruct((rows, chans), f32),
            jax.ShapeDtypeStruct((3, rows, chans), f32),
            jax.ShapeDtypeStruct((nb, 2 * BLK, chans), f32),
            jax.ShapeDtypeStruct((2 * BLK, chans), f32),
        ],
        cost_estimate=pl.CostEstimate(
            flops=8_000_000_000, bytes_accessed=20 << 20, transcendentals=0
        ),
        name="forward",
    )
    gated, conv, act, mspec, fspec = forward(
        projected, left, short_filter, long_filter, skip_row, fwd, inv_late
    )

    def scatter(value):
        return lax.psum_scatter(value, "tp", scatter_dimension=0, tiled=True)

    early = multiply_pieces(near_a + near_b, table, gated, out_grad, 8)
    out1, acc = multiply_pieces(
        mid_a + mid_b, table, gated, out_grad, 8, (2, *early)
    )
    quarter = BLK // SIDE
    lasts = [w.reshape(2, chans, width) for w in far_a + far_b]
    last_spec = pl.BlockSpec((2, tile, width), lambda i, c: (0, i, 0))

    def out_grad_rows(n):
        return [pl.BlockSpec((n, width), lambda i, c, j=j: (0, c[1 + 6 * SIDE + j])) for j in range(2 * SIDE)]

    def first_rows(n, *lead, t=tile):
        zeros = [0] * len(lead)
        return pl.BlockSpec((*lead, n, t), lambda i, c: (*zeros, 0, i))

    big = 2 * tile
    head = pl.pallas_call(
        head_kernel,
        grid_spec=pltpu.PrefetchScalarGridSpec(
            num_scalar_prefetch=1,
            grid=(chans // big,),
            in_specs=[
                first_rows(BLK + PAD, t=big),
                first_rows(BLK + PAD, 1, t=big),
                pl.BlockSpec(
                    (pl.Element(2), pl.Element(PAD), pl.Element(big)),
                    lambda i, c: (1, 0, i * big),
                ),
                first_rows(PAD, t=big),
                col(BLK, t=big),
                col(1, t=big),
                *out_grad_rows(BLK + PAD),
                *[pl.BlockSpec((2, big, width), lambda i, c: (0, i, 0))] * 4,
            ],
            out_specs=col(BLK + PAD, t=big),
            scratch_shapes=[pltpu.VMEM((BLK + PAD, big), f32)],
        ),
        out_shape=jax.ShapeDtypeStruct((BLK + PAD, chans), bf16),
        cost_estimate=pl.CostEstimate(
            flops=600_000_000, bytes_accessed=6 << 20, transcendentals=0
        ),
        name="head",
    )
    pay = head(table, acc, act, act, conv, long_filter, skip_row, *[out_grad] * (2 * SIDE), *lasts)
    got = along_x([pay] * SIDE)

    long_shape = jax.ShapeDtypeStruct((quarter, chans), bf16)
    backward = pl.pallas_call(
        backward_kernel,
        grid_spec=pltpu.PrefetchScalarGridSpec(
            num_scalar_prefetch=1,
            grid=grid,
            in_specs=[
                col(rows),
                first_rows(rows, 1),
                col(nb, 2 * BLK),
                col(2 * BLK),
                col(1),
                const,
                const_inv,
                const_inv,
                *out_grad_rows(rows),
                *[last_spec] * 4,
            ],
            out_specs=[col(rows)] + [col(quarter)] * 4 + [col(rows)],
            scratch_shapes=[
                pltpu.VMEM((BLK, tile), f32),
                pltpu.VMEM((2 * BLK, nb * tile), bf16),
                pltpu.VMEM((2 * BLK, nb * tile), f32),
                pltpu.VMEM((2 * BLK, nb * tile), bf16),
                pltpu.VMEM((2 * BLK, tile), bf16),
                pltpu.VMEM((BLK, nb * tile), f32),
            ],
        ),
        out_shape=[jax.ShapeDtypeStruct((rows, chans), f32)]
        + [long_shape] * 4
        + [jax.ShapeDtypeStruct((rows, chans), f32)],
        cost_estimate=pl.CostEstimate(
            flops=8_000_000_000, bytes_accessed=20 << 20, transcendentals=0
        ),
        name="backward",
    )
    bg, *longs, gmix = backward(
        table, acc, act, mspec, fspec, skip_row, fwd, inv_now, inv_lag,
        *[out_grad] * (2 * SIDE), *lasts,
    )

    to_z = chosen(got, readers)
    got = along_z([jnp.concatenate([v, part], 0) for v, part in zip(to_z, longs)])
    right = landed([g[: BLK + PAD] for g in got], readers)
    sums = [g[BLK + PAD :].astype(f32) for g in got]
    my_quarter = (sums[0] + sums[1]) + (sums[2] + sums[3])

    (out1,) = multiply_pieces(
        far_a + far_b, table, gated, None, 8, (6, out1)
    )
    out1 = scatter(out1)

    low = rows - BLK - PAD

    def rows_at(start, n, *lead, t=tile):
        zeros = [0] * len(lead)
        dims = [pl.Element(d) for d in (*lead, n, t)]
        return pl.BlockSpec(tuple(dims), lambda i: (*zeros, start, i * t))

    def acts_at(start, n, t=tile):
        return pl.BlockSpec(
            (pl.Element(2), pl.Element(n), pl.Element(t)), lambda i: (1, start, i * t)
        )

    gp_shape = jax.ShapeDtypeStruct((3, rows, chans), bf16)
    short_shape = jax.ShapeDtypeStruct((16, chans), f32)
    top = pl.pallas_call(
        top_kernel,
        grid=grid,
        in_specs=[
            rows_at(0, low), rows_at(0, low), rows_at(0, low), acts_at(0, low),
            rows_at(low, PAD), rows_at(low, PAD), rows_at(low, PAD), acts_at(low, PAD),
            rows_at(0, low, 3), col(3, 3),
        ],
        out_specs=[rows_at(0, low, 3), col(16)],
        out_shape=[gp_shape, short_shape],
        scratch_shapes=[pltpu.VMEM((3, low + PAD, tile), f32)],
        cost_estimate=pl.CostEstimate(
            flops=200_000_000, bytes_accessed=10 << 20, transcendentals=0
        ),
        name="top",
    )
    gp, short = top(bg, conv, gmix, act, bg, conv, gmix, act, projected, short_filter)
    rest = rows - low
    bottom = pl.pallas_call(
        bottom_kernel,
        grid=(chans // big,),
        in_specs=[
            rows_at(low, rest, t=big), rows_at(low, rest, t=big), rows_at(low, rest, t=big), acts_at(low, rest, t=big),
            col(BLK + PAD, t=big), rows_at(low, rest, 3, t=big), col(3, 3, t=big), col(2 * BLK, t=big), const, const_inv, col(16, t=big),
            pl.BlockSpec(memory_space=pl.ANY),
        ],
        out_specs=[rows_at(low, rest, 3, t=big), col(16, t=big)],
        out_shape=[gp_shape, short_shape],
        scratch_shapes=[pltpu.VMEM((3, rest + PAD, big), f32), pltpu.VMEM((rest, big), f32)],
        input_output_aliases={11: 0},
        cost_estimate=pl.CostEstimate(
            flops=2_000_000_000, bytes_accessed=5 << 20, transcendentals=0
        ),
        name="bottom",
    )
    gp, short = bottom(
        bg, conv, gmix, act, right, projected, short_filter, fspec, fwd, inv_now, short, gp
    )

    message = jnp.concatenate([my_quarter, short], 0)
    for along in (along_x, along_z):
        got = along([message.astype(bf16)] * SIDE)
        wide = [g.astype(f32) for g in got]
        message = (wide[0] + wide[1]) + (wide[2] + wide[3])
    long_total = jnp.concatenate([pick(got, zi ^ q)[:quarter] for q in range(SIDE)], 0)
    short_total = message[quarter : quarter + 9].reshape(3, 3, chans)

    share = rows // tp_count
    counts = tuple(o.shape[1] // width for o in (out1,))
    collect = pl.pallas_call(
        lambda cols, *refs: collect_kernel(counts, cols, *refs),
        grid_spec=pltpu.PrefetchScalarGridSpec(
            num_scalar_prefetch=1,
            grid=(1,),
            in_specs=[pl.BlockSpec(o.shape, lambda i, c: (0, 0)) for o in (out1,)],
            out_specs=pl.BlockSpec((share, 2 * width * ctx_count), lambda i, c: (0, 0)),
        ),
        out_shape=jax.ShapeDtypeStruct((share, 2 * width * ctx_count), bf16),
        cost_estimate=pl.CostEstimate(flops=10_000_000, bytes_accessed=5 << 20, transcendentals=0),
        name="collect",
    )
    mixed = collect(table, out1)

    scale = 1.0 / math.sqrt(rows * ctx_count)
    return mixed, gp, long_total.astype(f32) * scale, short_total * scale


def solution(mesh):
    placed = (
        P(None, "ctx", "tp"),
        P(None, None, "tp"),
        P(None, "tp"),
        P("tp"),
        P("tp", "ctx"),
        P("ctx", None),
        P(),
    )
    return jax.shard_map(
        on_device,
        mesh=mesh,
        in_specs=placed,
        out_specs=(
            P(("ctx", "tp"), None),
            P(None, "ctx", "tp"),
            P(None, "tp"),
            P(None, None, "tp"),
        ),
        check_vma=False,
    )
```
